512 devices in a mesh: blk: 16 (over y, x_hi, core), group: 32 (over x_lo, z).
Axes of the slice: x: 4 (x_hi: 2, x_lo: 2; x = x_hi * 2 + x_lo), y: 4, z: 16, core: 2. Of those that a mesh axis runs over, the one named last changes fastest.
Arguments:
- student_features: bfloat16 [65536, 768], P(('blk', 'group')), may hold values from -8 to 8
- teacher_image: bfloat16 [65536, 1152], P(('blk', 'group')), may hold values from -8 to 8
- text_embeds: bfloat16 [65536, 1152], P(('blk', 'group')), may hold values from -8 to 8
- pair_ids: int32 [65536], replicated, may hold values from 0 to 8191
- head_weights: bfloat16 [1152, 768], replicated, may hold values from -1 to 1
- moment_first: float32 [1152, 768], P('group'), may hold values from -4 to 4
- moment_second: float32 [1152, 768], P('group'), may hold values from 0.01 to 0.3
Outputs:
- row_loss: float32 [65536], P(('blk', 'group'))
- new_first: float32 [1152, 768], P('group')
- new_second: float32 [1152, 768], P('group')
- new_weights: bfloat16 [1152, 768], replicated
The draws below stay inside these ranges and needn't reach their ends.
All inputs are finite; a program needn't handle non-finite values.
Results may differ from the reference program's by a relative error of at most 0.0025.
The reference program's roundings to bfloat16 on the way (of `student_b`, `teacher_b`, `texts_b`, `coeff` and `grad_projected`) count: a program that leaves them out, or rounds other values in their place, can miss the bound.
Values may be sent and summed in bfloat16 or wider, within the bound.
No kernel may reach another device: no remote copies, remote signals or barrier semaphores. Data moves between devices by JAX's collectives and lax.ppermute only.
A program may use at most 64 MiB of HBM per device.

```python
import math
import jax
import jax.numpy as jnp
import numpy as np
from jax import lax

D = 1152
DS = 768
ROWS_DEV = 128
ROWS = 65536
N_BLK = 16
N_GROUP = 32


def head_matrix(key):
    head_key = jax.random.fold_in(jax.random.fold_in(key, 4099), 3)
    values = jax.random.normal(head_key, (D, DS), jnp.float32) / math.sqrt(DS)
    return jnp.clip(values, -1.0, 1.0)


def latent_parts(key):
    base_key = jax.random.fold_in(key, 4099)
    latent_count = 32
    coeffs = jax.random.normal(jax.random.fold_in(base_key, 1), (ROWS, latent_count), jnp.float32)
    factors = jax.random.normal(jax.random.fold_in(base_key, 2), (latent_count, DS), jnp.float32)
    return (coeffs, factors, latent_count)


def noise_field(key, salt, dims):
    noise_key = jax.random.fold_in(jax.random.fold_in(key, 5003), salt)
    return jax.random.normal(noise_key, dims, jnp.float32)


def shared_embedding(key):
    coeffs, factors, latent_count = latent_parts(key)
    mapped = jnp.dot(factors, jnp.transpose(head_matrix(key)), precision=lax.Precision.HIGHEST)
    return jnp.dot(coeffs, mapped, precision=lax.Precision.HIGHEST) / math.sqrt(latent_count)


def draw_head_weights(key, part):
    return head_matrix(key).astype(jnp.bfloat16)


def draw_student_features(key, part):
    coeffs, factors, latent_count = latent_parts(key)
    common = jnp.dot(coeffs, factors, precision=lax.Precision.HIGHEST) / math.sqrt(latent_count)
    values = 0.775 * common + 0.632 * noise_field(key, 11, (ROWS, DS))
    return jnp.clip(values, -8.0, 8.0).astype(jnp.bfloat16)


def draw_teacher_image(key, part):
    common = shared_embedding(key)
    values = 0.8 * common + 0.6 * noise_field(key, 21, (ROWS, D))
    return jnp.clip(values, -8.0, 8.0).astype(jnp.bfloat16)


def draw_text_embeds(key, part):
    common = shared_embedding(key)
    values = 0.75 * common + 0.66 * noise_field(key, 31, (ROWS, D))
    return jnp.clip(values, -8.0, 8.0).astype(jnp.bfloat16)


def plant(entries, key, smallest, top_value):
    index_at = [jax.random.randint(jax.random.fold_in(key, axis), (), 0, length) for axis, length in enumerate(entries.shape)]
    main_axis = entries.shape.index(max(entries.shape))
    neighbour = index_at[:main_axis] + [(index_at[main_axis] + 1) % entries.shape[main_axis]] + index_at[main_axis + 1:]
    return entries.at[tuple(index_at)].set(smallest).at[tuple(neighbour)].set(top_value)


def levels(key, shape, pieces, smallest, top_value):
    gain = 1.0
    for position, parts in pieces:
        heights = jax.random.uniform(jax.random.fold_in(jax.random.fold_in(key, 6), position), (parts,), jnp.float32, smallest / len(pieces), top_value / len(pieces))
        gain = gain * jnp.repeat(jnp.exp(heights), shape[position] // parts).reshape((-1,) + (1,) * (len(shape) - 1 - position))
    return gain


def cumulative_ranks(number_of, lean):
    portions = [(1 << 20) // math.isqrt(grade ** lean) + 1 for grade in range(1, number_of + 1)]
    deviation = 1 + sum(portions) // (1 << 30)
    return np.cumsum(np.array([max(1, weight // deviation) for weight in portions]))


def skewed_ids(rng, shape, number_of, lean):
    table = cumulative_ranks(number_of, lean)
    ticket = jax.random.randint(jax.random.fold_in(rng, 1), shape, 0, int(table[number_of - 1]))
    rank = jnp.searchsorted(jnp.asarray(table, jnp.int32), ticket, side="right")
    return jax.random.permutation(jax.random.fold_in(rng, 2), number_of)[rank].astype(jnp.int32)


def gaussian(key, shape, width, reach, split=(), kind=jnp.bfloat16):
    result = jax.random.normal(key, shape, jnp.float32) * width
    if len(split) > 0:
        result = levels(key, shape, split, -0.22, 0.18) * result
    return jnp.clip(result, min=-reach, max=reach).astype(kind)


def setup_inputs(seed: int = 0) -> dict:
    arg_keys = jax.random.split(jax.random.key(seed), 8)
    return {
        "student_features": draw_student_features(jax.random.fold_in(arg_keys[7], 71), 0),
        "teacher_image": draw_teacher_image(jax.random.fold_in(arg_keys[7], 71), 0),
        "text_embeds": draw_text_embeds(jax.random.fold_in(arg_keys[7], 71), 0),
        "pair_ids": plant(skewed_ids(arg_keys[3], (ROWS,), ROWS // 8, 2), jax.random.fold_in(arg_keys[3], 3), 0, (ROWS // 8) - 1).astype(jnp.int32),
        "head_weights": draw_head_weights(jax.random.fold_in(arg_keys[7], 71), 0),
        "moment_first": gaussian(arg_keys[5], (D, DS), 0.3, 4.0, ((0, 32),), jnp.float32),
        "moment_second": jnp.clip(jnp.exp(math.log(0.3) - 3.4011974 * jax.random.uniform(arg_keys[6], (D, DS), jnp.float32) ** levels(arg_keys[6], (D, DS), ((0, 32),), -0.2, 0.2)), 0.01, 0.3),
    }


student_scale = 20.0
student_bias = -1.0
teacher_scale = 25.0
teacher_bias = -1.5
label_mix = 0.5
norm_eps = 1e-06
beta_one = 0.9
beta_two = 0.95
learn_rate = 0.01
weight_decay = 0.0001
adam_eps = 1e-08
adam_step = 100.0

def unit_rows(values):
    values = values.astype(jnp.float32)
    return values * lax.rsqrt(lax.optimization_barrier(jnp.sum(values * values, axis=-1, keepdims=True)) + norm_eps)

def pair_terms(student_rows, teacher_rows, left_ids, text_rows, right_ids):
    dims = (((1,), (1,)), ((), ()))
    student_logit = student_scale * lax.dot_general(student_rows, text_rows, dims, preferred_element_type=jnp.float32) + student_bias
    teacher_logit = teacher_scale * lax.dot_general(teacher_rows, text_rows, dims, preferred_element_type=jnp.float32) + teacher_bias
    labels = (left_ids[:, None] == right_ids[None, :]).astype(jnp.float32)
    target = (1.0 - label_mix) * labels + label_mix * jax.nn.sigmoid(teacher_logit)
    losses = lax.optimization_barrier(jnp.sum(jax.nn.softplus(student_logit) - target * student_logit, axis=1))
    coeff = (jax.nn.sigmoid(student_logit) - target).astype(jnp.bfloat16)
    pulled = jnp.dot(coeff, text_rows, preferred_element_type=jnp.float32)
    return (losses, pulled)

def reference(student_features, teacher_image, text_embeds, pair_ids, head_weights, moment_first, moment_second):
    projected = lax.dot_general(student_features, head_weights, (((1,), (1,)), ((), ())), preferred_element_type=jnp.float32)
    inverse = lax.rsqrt(lax.optimization_barrier(jnp.sum(projected * projected, axis=-1, keepdims=True)) + norm_eps)
    student = projected * inverse
    student_b = student.astype(jnp.bfloat16)
    teacher_b = unit_rows(teacher_image).astype(jnp.bfloat16)
    texts_b = unit_rows(text_embeds).astype(jnp.bfloat16)
    student_grid = student_b.reshape(N_BLK, N_GROUP, ROWS_DEV, D)
    teacher_grid = teacher_b.reshape(N_BLK, N_GROUP, ROWS_DEV, D)
    text_grid = texts_b.reshape(N_BLK, N_GROUP, ROWS_DEV, D)
    ids_grid = pair_ids.reshape(N_BLK, N_GROUP, ROWS_DEV)

    def one_group(group_index):
        partner_index = (group_index + N_GROUP // 2) % N_GROUP
        images = student_grid[:, group_index].reshape(N_BLK * ROWS_DEV, D)
        teachers = teacher_grid[:, group_index].reshape(N_BLK * ROWS_DEV, D)
        left_ids = ids_grid[:, group_index].reshape(N_BLK * ROWS_DEV)
        window = jnp.concatenate([text_grid[:, group_index].reshape(N_BLK * ROWS_DEV, D), text_grid[:, partner_index].reshape(N_BLK * ROWS_DEV, D)], axis=0)
        window_ids = jnp.concatenate([ids_grid[:, group_index].reshape(N_BLK * ROWS_DEV), ids_grid[:, partner_index].reshape(N_BLK * ROWS_DEV)], axis=0)
        return pair_terms(images, teachers, left_ids, window, window_ids)
    losses, pulled = lax.map(one_group, jnp.arange(N_GROUP, dtype=jnp.int32))
    losses = jnp.transpose(losses.reshape(N_GROUP, N_BLK, ROWS_DEV), (1, 0, 2)).reshape(ROWS)
    pulled = jnp.transpose(pulled.reshape(N_GROUP, N_BLK, ROWS_DEV, D), (1, 0, 2, 3)).reshape(ROWS, D)
    row_loss = losses / ROWS_DEV
    grad_student = student_scale / ROWS_DEV * pulled
    grad_projected = (inverse * (grad_student - student * lax.optimization_barrier(jnp.sum(student * grad_student, axis=-1, keepdims=True)))).astype(jnp.bfloat16)
    head_grad = lax.dot_general(grad_projected, student_features, (((0,), (0,)), ((), ())), preferred_element_type=jnp.float32)
    new_first = beta_one * moment_first + (1.0 - beta_one) * head_grad
    new_second = beta_two * moment_second + (1.0 - beta_two) * head_grad * head_grad
    first_hat = new_first / (1.0 - beta_one ** adam_step)
    second_hat = new_second / (1.0 - beta_two ** adam_step)
    weights = head_weights.astype(jnp.float32)
    updated = weights - learn_rate * (first_hat / (jnp.sqrt(second_hat) + adam_eps) + weight_decay * weights)
    return (row_loss, new_first, new_second, updated.astype(jnp.bfloat16))
```

```python
import jax
import jax.numpy as jnp
from jax import lax
from jax.sharding import PartitionSpec as P

student_scale = 20.0
student_bias = -1.0
teacher_scale = 25.0
teacher_bias = -1.5
label_mix = 0.5
norm_eps = 1e-06
beta_one = 0.9
beta_two = 0.95
learn_rate = 0.01
weight_decay = 0.0001
adam_eps = 1e-08
adam_step = 100.0

AXES = ("blk", "group")


def device(X, y, core, z):
    return (y * 4 + X % 2 * 2 + core) * 32 + X // 2 * 16 + z


def x_line(y, core, z):
    return [device(X, y, core, z) for X in range(4)]


def y_line(X, core, z):
    return [device(X, y, core, z) for y in range(4)]


def lines(along_x):
    groups = []
    for core in range(2):
        line = x_line if (core == 0) == along_x else y_line
        groups += [line(i, core, z) for z in range(16) for i in range(4)]
    return groups


FIRST = lines(True)
SECOND = lines(False)
PLANE = [
    [device(X, y, core, z) for X in range(4) for y in range(4)]
    for core in range(2)
    for z in range(16)
]
COLUMN = [
    [device(X, y, core, z) for z in range(16)]
    for X in range(4)
    for y in range(4)
    for core in range(2)
]
TWIN = [(i, i ^ 32) for i in range(512)]


def exchange(pieces, groups):
    return lax.all_to_all(pieces, AXES, 0, 0, axis_index_groups=groups, tiled=True)


def share(block, groups):
    return exchange(jnp.broadcast_to(block[None], (len(groups[0]), *block.shape)), groups)


def from_twin(shard):
    return lax.ppermute(shard, AXES, TWIN)


def unit_rows(values):
    values = values.astype(jnp.float32)
    return values * lax.rsqrt(jnp.sum(values * values, axis=-1, keepdims=True) + norm_eps)


def pair_terms(student_rows, teacher_rows, left_ids, text_rows, right_ids):
    dims = (((1,), (1,)), ((), ()))
    student_logit = (
        student_scale
        * lax.dot_general(student_rows, text_rows, dims, preferred_element_type=jnp.float32)
        + student_bias
    )
    teacher_logit = (
        teacher_scale
        * lax.dot_general(teacher_rows, text_rows, dims, preferred_element_type=jnp.float32)
        + teacher_bias
    )
    labels = (left_ids[:, None] == right_ids[None, :]).astype(jnp.float32)
    target = (1.0 - label_mix) * labels + label_mix * jax.nn.sigmoid(teacher_logit)
    losses = jnp.sum(jax.nn.softplus(student_logit) - target * student_logit, axis=1)
    coeff = (jax.nn.sigmoid(student_logit) - target).astype(jnp.bfloat16)
    pulled = jnp.dot(coeff, text_rows, preferred_element_type=jnp.float32)
    return (losses, pulled)


def row_order(core):
    place = lax.iota(jnp.int32, 1152)
    first, second = place // 288, place // 72 % 4
    X = jnp.where(core == 0, first, second)
    y = jnp.where(core == 0, second, first)
    return X * 288 + place // 9 % 8 * 36 + y * 9 + place % 9


def one_hot(index):
    return (index[:, None] == lax.iota(jnp.int32, 1152)[None, :]).astype(jnp.bfloat16)


def rounded(values):
    return lax.reduce_precision(values, 8, 7)


def per_device(
    student_features,
    teacher_image,
    text_embeds,
    pair_ids,
    head_weights,
    moment_first,
    moment_second,
):
    rows = student_features.shape[0]
    blk_index = lax.axis_index("blk")
    group_index = lax.axis_index("group")
    y, xh, core = blk_index // 4, blk_index // 2 % 2, blk_index % 2
    xl, z = group_index // 16, group_index % 16

    texts_b = unit_rows(text_embeds).astype(jnp.bfloat16)
    near = share(jnp.concatenate([texts_b, student_features], axis=1), FIRST)
    features = near[:, :, 1152:]
    texts = share(near[:, :, :1152].reshape(512, 1152), SECOND).reshape(2048, 1152)

    both_features = jnp.concatenate([student_features, from_twin(student_features)], axis=0)
    both_teacher = jnp.concatenate([teacher_image, from_twin(teacher_image)], axis=0)
    projected = lax.dot_general(
        both_features, head_weights, (((1,), (1,)), ((), ())), preferred_element_type=jnp.float32
    )
    inverse = lax.rsqrt(jnp.sum(projected * projected, axis=-1, keepdims=True) + norm_eps)
    student = projected * inverse
    student_b = student.astype(jnp.bfloat16)
    teacher_b = unit_rows(both_teacher).astype(jnp.bfloat16)

    ids_grid = pair_ids.reshape(4, 2, 2, 2, 16, rows)
    ids_plane = lax.dynamic_index_in_dim(ids_grid, z, 4, keepdims=False)
    ids_core = lax.dynamic_index_in_dim(ids_plane, core, 2, keepdims=False)
    ids_yx = ids_core.transpose(0, 2, 1, 3).reshape(4, 4, rows)
    text_ids = jnp.where(core == 0, ids_yx, ids_yx.transpose(1, 0, 2)).reshape(-1)
    ids_rows = pair_ids.reshape(512, rows)
    left_ids = jnp.concatenate(
        [
            lax.dynamic_index_in_dim(ids_rows, blk_index * 32 + group_index, 0, keepdims=False),
            lax.dynamic_index_in_dim(ids_rows, (blk_index ^ 1) * 32 + group_index, 0, keepdims=False),
        ]
    )
    losses, pulled = pair_terms(student_b, teacher_b, left_ids, texts, text_ids)

    pulled = pulled[:rows] + from_twin(pulled[rows:])
    student, inverse = student[:rows], inverse[:rows]
    grad_student = student_scale / rows * pulled
    grad_projected = (
        inverse * (grad_student - student * jnp.sum(student * grad_student, axis=-1, keepdims=True))
    ).astype(jnp.bfloat16)

    grad_rows = lax.dot_general(
        one_hot(row_order(core)),
        grad_projected,
        (((1,), (1,)), ((), ())),
        preferred_element_type=jnp.float32,
    ).astype(jnp.bfloat16)
    grad_rows = exchange(grad_rows.reshape(4, 288, rows), FIRST)
    line_grad = lax.dot_general(
        grad_rows, features, (((0, 2), (0, 1)), ((), ())), preferred_element_type=jnp.float32
    )
    core_grad = jnp.sum(exchange(line_grad.reshape(4, 72, 768), SECOND), axis=0)
    left, right = core_grad[:, :384], core_grad[:, 384:]
    other_losses = jnp.pad(losses[rows:].reshape(1, rows), ((0, 7), (0, 256)))
    arrived = from_twin(jnp.concatenate([jnp.where(core == 0, right, left), other_losses], axis=0))
    chip_grad = jnp.where(core == 0, left, right) + arrived[:72]
    row_loss = (losses[:rows] + arrived[72, :rows]) / rows

    plane_grad = chip_grad.reshape(8, 9, 384)
    own_grad = jnp.sum(exchange(jnp.concatenate([plane_grad, plane_grad], axis=0), COLUMN), axis=0)

    def adam(head_grad, first, second, weights):
        new_first = beta_one * first + (1.0 - beta_one) * head_grad
        new_second = beta_two * second + (1.0 - beta_two) * head_grad * head_grad
        first_hat = new_first / (1.0 - beta_one**adam_step)
        second_hat = new_second / (1.0 - beta_two**adam_step)
        weights = weights.astype(jnp.float32)
        updated = weights - learn_rate * (
            first_hat / (jnp.sqrt(second_hat) + adam_eps) + weight_decay * weights
        )
        return new_first, new_second, updated.astype(jnp.bfloat16)

    def piece(values, start):
        return lax.dynamic_slice(values, (start + y * 9, core * 384), (9, 384))

    _, _, own_weights = adam(
        own_grad,
        piece(moment_first, 0),
        piece(moment_second, 0),
        piece(head_weights, group_index * 36),
    )
    column = share(own_weights, COLUMN)
    chip_weights = lax.dynamic_slice_in_dim(column, xh * 8, 8, 0).reshape(72, 384)
    high = rounded(own_grad)
    middle = rounded(own_grad - high)
    low = own_grad - high - middle
    grad_parts = jnp.concatenate([high, middle, low], axis=0).astype(jnp.bfloat16)
    half = share(jnp.concatenate([chip_weights, grad_parts], axis=0), PLANE)
    twin_half = from_twin(half)
    whole = jnp.concatenate(
        [jnp.where(core == 0, half, twin_half), jnp.where(core == 0, twin_half, half)], axis=2
    )
    new_weights = lax.dot_general(
        one_hot(row_order(0)),
        whole[:, :72].reshape(1152, 768),
        (((0,), (0,)), ((), ())),
        preferred_element_type=jnp.float32,
    ).astype(jnp.bfloat16)
    parts = lax.dynamic_slice_in_dim(whole, (xl * 2 + z // 8) * 4, 4, 0)[:, 72:]
    parts = parts.reshape(4, 3, 9, 768).astype(jnp.float32)
    head_grad = ((parts[:, 0] + parts[:, 1]) + parts[:, 2]).reshape(36, 768)
    new_first = beta_one * moment_first + (1.0 - beta_one) * head_grad
    new_second = beta_two * moment_second + (1.0 - beta_two) * head_grad * head_grad
    return (row_loss, new_first, new_second, new_weights)


def solution(mesh):
    placed = (
        P(("blk", "group"), None),
        P(("blk", "group"), None),
        P(("blk", "group"), None),
        P(),
        P(),
        P("group", None),
        P("group", None),
    )
    return jax.shard_map(
        per_device,
        mesh=mesh,
        in_specs=placed,
        out_specs=(P(("blk", "group")), P("group", None), P("group", None), P()),
        check_vma=False,
    )
```

```python
import jax
import jax.numpy as jnp
from jax import lax
from jax.sharding import PartitionSpec as P

student_scale = 20.0
student_bias = -1.0
teacher_scale = 25.0
teacher_bias = -1.5
label_mix = 0.5
norm_eps = 1e-06
beta_one = 0.9
beta_two = 0.95
learn_rate = 0.01
weight_decay = 0.0001
adam_eps = 1e-08
adam_step = 100.0

AXES = ("blk", "group")


def device(X, y, core, z):
    return (y * 4 + X % 2 * 2 + core) * 32 + X // 2 * 16 + z


def x_line(y, core, z):
    return [device(X, y, core, z) for X in range(4)]


def y_line(X, core, z):
    return [device(X, y, core, z) for y in range(4)]


def lines(along_x):
    groups = []
    for core in range(2):
        line = x_line if (core == 0) == along_x else y_line
        groups += [line(i, core, z) for z in range(16) for i in range(4)]
    return groups


FIRST = lines(True)
SECOND = lines(False)
PLANE = [
    [device(X, y, core, z) for X in range(4) for y in range(4)]
    for core in range(2)
    for z in range(16)
]
COLUMN = [
    [device(X, y, core, z) for z in range(16)]
    for X in range(4)
    for y in range(4)
    for core in range(2)
]
SPLIT = ((0, 3), (3, 4))
TWIN = [(i, i ^ 32) for i in range(512)]


def exchange(pieces, groups):
    return lax.all_to_all(pieces, AXES, 0, 0, axis_index_groups=groups, tiled=True)


def share(block, groups):
    return exchange(jnp.broadcast_to(block[None], (len(groups[0]), *block.shape)), groups)


def from_twin(shard):
    return lax.ppermute(shard, AXES, TWIN)


def unit_rows(values):
    values = values.astype(jnp.float32)
    return values * lax.rsqrt(jnp.sum(values * values, axis=-1, keepdims=True) + norm_eps)


def pair_terms(student_rows, teacher_rows, left_ids, text_rows, right_ids):
    dims = (((1,), (1,)), ((), ()))
    student_logit = (
        student_scale
        * lax.dot_general(student_rows, text_rows, dims, preferred_element_type=jnp.float32)
        + student_bias
    )
    teacher_logit = (
        teacher_scale
        * lax.dot_general(teacher_rows, text_rows, dims, preferred_element_type=jnp.float32)
        + teacher_bias
    )
    labels = (left_ids[:, None] == right_ids[None, :]).astype(jnp.float32)
    target = (1.0 - label_mix) * labels + label_mix * jax.nn.sigmoid(teacher_logit)
    losses = jnp.sum(jax.nn.softplus(student_logit) - target * student_logit, axis=1)
    coeff = (jax.nn.sigmoid(student_logit) - target).astype(jnp.bfloat16)
    pulled = jnp.dot(coeff, text_rows, preferred_element_type=jnp.float32)
    return (losses, pulled)


def row_order(core):
    place = lax.iota(jnp.int32, 1280)
    first, second = place // 320, place // 80 % 4
    X = jnp.where(core == 0, first, second)
    y = jnp.where(core == 0, second, first)
    row = (X % 2 * 4 + y) * 5 + place % 5
    return jnp.where(row < 36, X // 2 * 576 + place // 5 % 16 * 36 + row, -1)


def place_order(xl):
    row = lax.iota(jnp.int32, 1152)
    q = row % 36
    weights = (row // 576 * 8 + q // 5) * 95 + row // 36 % 16 * 5 + q % 5
    part = lax.iota(jnp.int32, 120)
    q = part % 40
    grads = (xl * 8 + q // 5) * 95 + 80 + part // 40 * 5 + q % 5
    return jnp.concatenate([weights, grads])


def one_hot(index, width):
    return (index[:, None] == lax.iota(jnp.int32, width)[None, :]).astype(jnp.bfloat16)


def rounded(values):
    return lax.reduce_precision(values, 8, 7)


def per_device(
    student_features,
    teacher_image,
    text_embeds,
    pair_ids,
    head_weights,
    moment_first,
    moment_second,
):
    rows = student_features.shape[0]
    blk_index = lax.axis_index("blk")
    group_index = lax.axis_index("group")
    y, xh, core = blk_index // 4, blk_index // 2 % 2, blk_index % 2
    xl, z = group_index // 16, group_index % 16

    texts_b = unit_rows(text_embeds).astype(jnp.bfloat16)
    near = share(jnp.concatenate([texts_b, student_features], axis=1), FIRST)
    features = near[:, :, 1152:]
    texts = []
    for lo, hi in SPLIT:
        part = near[lo:hi, :, :1152].reshape((hi - lo) * rows, 1152)
        if texts:
            part, texts[-1] = lax.optimization_barrier((part, texts[-1]))
        texts.append(share(part, SECOND).reshape(-1, 1152))

    both_features = jnp.concatenate([student_features, from_twin(student_features)], axis=0)
    both_teacher = jnp.concatenate([teacher_image, from_twin(teacher_image)], axis=0)
    projected = lax.dot_general(
        both_features, head_weights, (((1,), (1,)), ((), ())), preferred_element_type=jnp.float32
    )
    inverse = lax.rsqrt(jnp.sum(projected * projected, axis=-1, keepdims=True) + norm_eps)
    student = projected * inverse
    student_b = student.astype(jnp.bfloat16)
    teacher_b = unit_rows(both_teacher).astype(jnp.bfloat16)

    ids_grid = pair_ids.reshape(4, 2, 2, 2, 16, rows)
    ids_plane = lax.dynamic_index_in_dim(ids_grid, z, 4, keepdims=False)
    ids_core = lax.dynamic_index_in_dim(ids_plane, core, 2, keepdims=False)
    ids_yx = ids_core.transpose(0, 2, 1, 3).reshape(4, 4, rows)
    text_ids = jnp.where(core == 0, ids_yx, ids_yx.transpose(1, 0, 2))
    ids_rows = pair_ids.reshape(512, rows)
    left_ids = jnp.concatenate(
        [
            lax.dynamic_index_in_dim(ids_rows, blk_index * 32 + group_index, 0, keepdims=False),
            lax.dynamic_index_in_dim(ids_rows, (blk_index ^ 1) * 32 + group_index, 0, keepdims=False),
        ]
    )
    terms = [
        pair_terms(student_b, teacher_b, left_ids, part, text_ids[:, lo:hi].reshape(-1))
        for part, (lo, hi) in zip(texts, SPLIT)
    ]
    losses, pulled = (sum(term) for term in zip(*terms))

    pulled = pulled[:rows] + from_twin(pulled[rows:])
    student, inverse = student[:rows], inverse[:rows]
    grad_student = student_scale / rows * pulled
    grad_projected = (
        inverse * (grad_student - student * jnp.sum(student * grad_student, axis=-1, keepdims=True))
    ).astype(jnp.bfloat16)

    grad_rows = lax.dot_general(
        one_hot(row_order(core), 1152),
        grad_projected,
        (((1,), (1,)), ((), ())),
        preferred_element_type=jnp.float32,
    ).astype(jnp.bfloat16)
    grad_rows = exchange(grad_rows.reshape(4, 320, rows), FIRST)
    line_grad = lax.dot_general(
        grad_rows, features, (((0, 2), (0, 1)), ((), ())), preferred_element_type=jnp.float32
    )
    core_grad = jnp.sum(exchange(line_grad.reshape(4, 80, 768), SECOND), axis=0)
    left, right = core_grad[:, :384], core_grad[:, 384:]
    other_losses = jnp.pad(losses[rows:].reshape(1, rows), ((0, 7), (0, 256)))
    arrived = from_twin(jnp.concatenate([jnp.where(core == 0, right, left), other_losses], axis=0))
    chip_grad = jnp.where(core == 0, left, right) + arrived[:80]
    row_loss = (losses[:rows] + arrived[80, :rows]) / rows

    column_grad = jnp.pad(chip_grad.reshape(16, 15, 128), ((0, 0), (0, 1), (0, 0)))
    own_grad = jnp.sum(exchange(column_grad, COLUMN), axis=0)[:15].reshape(5, 384)

    def adam(head_grad, first, second, weights):
        new_first = beta_one * first + (1.0 - beta_one) * head_grad
        new_second = beta_two * second + (1.0 - beta_two) * head_grad * head_grad
        first_hat = new_first / (1.0 - beta_one**adam_step)
        second_hat = new_second / (1.0 - beta_two**adam_step)
        weights = weights.astype(jnp.float32)
        updated = weights - learn_rate * (
            first_hat / (jnp.sqrt(second_hat) + adam_eps) + weight_decay * weights
        )
        return updated.astype(jnp.bfloat16)

    def piece(values, start):
        group_rows = lax.dynamic_slice_in_dim(values, start, 36, 0)
        padded = jnp.pad(group_rows, ((0, 4), (0, 0)))
        return lax.dynamic_slice(padded, ((xh * 4 + y) * 5, core * 384), (5, 384))

    own_weights = adam(
        own_grad,
        piece(moment_first, 0),
        piece(moment_second, 0),
        piece(head_weights, group_index * 36),
    )
    chip_weights = share(own_weights, COLUMN).reshape(80, 384)
    high = rounded(own_grad)
    middle = rounded(own_grad - high)
    low = own_grad - high - middle
    grad_parts = jnp.concatenate([high, middle, low], axis=0).astype(jnp.bfloat16)
    plane = share(jnp.concatenate([chip_weights, grad_parts], axis=0), PLANE)
    half = lax.dot_general(
        one_hot(place_order(xl), 1520),
        plane.reshape(1520, 384),
        (((1,), (0,)), ((), ())),
        preferred_element_type=jnp.float32,
    ).astype(jnp.bfloat16)
    twin_half = from_twin(half)
    whole = jnp.concatenate(
        [jnp.where(core == 0, half, twin_half), jnp.where(core == 0, twin_half, half)], axis=1
    )
    new_weights = whole[:1152]
    parts = whole[1152:].reshape(3, 40, 768).astype(jnp.float32)
    head_grad = ((parts[0] + parts[1]) + parts[2])[:36]
    new_first = beta_one * moment_first + (1.0 - beta_one) * head_grad
    new_second = beta_two * moment_second + (1.0 - beta_two) * head_grad * head_grad
    return (row_loss, new_first, new_second, new_weights)


def solution(mesh):
    placed = (
        P(("blk", "group"), None),
        P(("blk", "group"), None),
        P(("blk", "group"), None),
        P(),
        P(),
        P("group", None),
        P("group", None),
    )
    return jax.shard_map(
        per_device,
        mesh=mesh,
        in_specs=placed,
        out_specs=(P(("blk", "group")), P("group", None), P("group", None), P()),
        check_vma=False,
    )
```

```python
import jax
import jax.numpy as jnp
from jax import lax
from jax.sharding import PartitionSpec as P

student_scale = 20.0
student_bias = -1.0
teacher_scale = 25.0
teacher_bias = -1.5
label_mix = 0.5
norm_eps = 1e-06
beta_one = 0.9
beta_two = 0.95
learn_rate = 0.01
weight_decay = 0.0001
adam_eps = 1e-08
adam_step = 100.0

AXES = ("blk", "group")


def device(X, y, core, z):
    return (y * 4 + X % 2 * 2 + core) * 32 + X // 2 * 16 + z


def x_line(y, core, z):
    return [device(X, y, core, z) for X in range(4)]


def y_line(X, core, z):
    return [device(X, y, core, z) for y in range(4)]


def lines(along_x):
    groups = []
    for core in range(2):
        line = x_line if (core == 0) == along_x else y_line
        groups += [line(i, core, z) for z in range(16) for i in range(4)]
    return groups


FIRST = lines(True)
SECOND = lines(False)
PLANE = [
    [device(X, y, core, z) for X in range(4) for y in range(4)]
    for core in range(2)
    for z in range(16)
]
COLUMN = [
    [device(X, y, core, z) for z in range(16)]
    for X in range(4)
    for y in range(4)
    for core in range(2)
]
TWIN = [(i, i ^ 32) for i in range(512)]


def hop(step):
    pairs = []
    for i in range(512):
        blk, group = divmod(i, 32)
        y, xh, core = blk // 4, blk // 2 % 2, blk % 2
        xl, z = divmod(group, 16)
        x = xh * 2 + xl
        if core == 0:
            y = (y + step) % 4
        else:
            x = (x + step) % 4
        pairs.append((i, device(x % 2 * 2 + x // 2, y, core, z)))
    return pairs


FORTH = hop(1)
BACK = hop(-1)


def exchange(pieces, groups):
    return lax.all_to_all(pieces, AXES, 0, 0, axis_index_groups=groups, tiled=True)


def share(block, groups):
    return exchange(jnp.broadcast_to(block[None], (len(groups[0]), *block.shape)), groups)


def from_twin(shard):
    return lax.ppermute(shard, AXES, TWIN)


def unit_rows(values):
    values = values.astype(jnp.float32)
    return values * lax.rsqrt(jnp.sum(values * values, axis=-1, keepdims=True) + norm_eps)


def pair_terms(student_rows, teacher_rows, left_ids, text_rows, right_ids):
    dims = (((1,), (1,)), ((), ()))
    student_logit = (
        student_scale
        * lax.dot_general(student_rows, text_rows, dims, preferred_element_type=jnp.float32)
        + student_bias
    )
    teacher_logit = (
        teacher_scale
        * lax.dot_general(teacher_rows, text_rows, dims, preferred_element_type=jnp.float32)
        + teacher_bias
    )
    labels = (left_ids[:, None] == right_ids[None, :]).astype(jnp.float32)
    target = (1.0 - label_mix) * labels + label_mix * jax.nn.sigmoid(teacher_logit)
    losses = jnp.sum(jax.nn.softplus(student_logit) - target * student_logit, axis=1)
    coeff = (jax.nn.sigmoid(student_logit) - target).astype(jnp.bfloat16)
    pulled = jnp.dot(coeff, text_rows, preferred_element_type=jnp.float32)
    return (losses, pulled)


def row_order(core):
    place = lax.iota(jnp.int32, 1280)
    first, second = place // 320, place // 80 % 4
    X = jnp.where(core == 0, first, second)
    y = jnp.where(core == 0, second, first)
    row = (X % 2 * 4 + y) * 5 + place % 5
    return jnp.where(row < 36, X // 2 * 576 + place // 5 % 16 * 36 + row, -1)


def weight_order():
    row = lax.iota(jnp.int32, 576)
    q = row % 36
    return q // 5 * 96 + row // 36 * 5 + q % 5


def grad_order():
    part = lax.iota(jnp.int32, 120)
    q = part % 40
    return q // 5 * 96 + 80 + part // 40 * 5 + q % 5


def one_hot(index, width):
    return (index[:, None] == lax.iota(jnp.int32, width)[None, :]).astype(jnp.bfloat16)


def rounded(values):
    return lax.reduce_precision(values, 8, 7)


def per_device(
    student_features,
    teacher_image,
    text_embeds,
    pair_ids,
    head_weights,
    moment_first,
    moment_second,
):
    rows = student_features.shape[0]
    blk_index = lax.axis_index("blk")
    group_index = lax.axis_index("group")
    y, xh, core = blk_index // 4, blk_index // 2 % 2, blk_index % 2
    xl, z = group_index // 16, group_index % 16

    texts_b = unit_rows(text_embeds).astype(jnp.bfloat16)
    near = share(jnp.concatenate([texts_b, student_features], axis=1), FIRST)
    features = near[:, :, 1152:]
    bundle = near[:, :, :1152].reshape(4 * rows, 1152)
    before = lax.ppermute(bundle, AXES, FORTH)
    after = lax.ppermute(bundle, AXES, BACK)
    far_first = lax.ppermute(before[: 2 * rows], AXES, FORTH)
    far_last = lax.ppermute(after[2 * rows :], AXES, BACK)

    both_features = jnp.concatenate([student_features, from_twin(student_features)], axis=0)
    both_teacher = jnp.concatenate([teacher_image, from_twin(teacher_image)], axis=0)
    projected = lax.dot_general(
        both_features, head_weights, (((1,), (1,)), ((), ())), preferred_element_type=jnp.float32
    )
    inverse = lax.rsqrt(jnp.sum(projected * projected, axis=-1, keepdims=True) + norm_eps)
    student = projected * inverse
    student_b = student.astype(jnp.bfloat16)
    teacher_b = unit_rows(both_teacher).astype(jnp.bfloat16)

    ids_grid = pair_ids.reshape(4, 2, 2, 2, 16, rows)
    ids_plane = lax.dynamic_index_in_dim(ids_grid, z, 4, keepdims=False)
    ids_core = lax.dynamic_index_in_dim(ids_plane, core, 2, keepdims=False)
    ids_yx = ids_core.transpose(0, 2, 1, 3).reshape(4, 4, rows)
    ids_xy = ids_core.transpose(1, 2, 0, 3).reshape(4, 4, rows)
    text_ids = jnp.where(core == 0, ids_yx, ids_xy)
    place = jnp.where(core == 0, y, xh * 2 + xl)

    def ids_at(step):
        return lax.dynamic_index_in_dim(text_ids, (place + step) % 4, 0, keepdims=False)

    ids_rows = pair_ids.reshape(512, rows)
    left_ids = jnp.concatenate(
        [
            lax.dynamic_index_in_dim(ids_rows, blk_index * 32 + group_index, 0, keepdims=False),
            lax.dynamic_index_in_dim(ids_rows, (blk_index ^ 1) * 32 + group_index, 0, keepdims=False),
        ]
    )
    chunks = (
        (bundle, ids_at(0)),
        (before, ids_at(3)),
        (after, ids_at(1)),
        (far_first, ids_at(2)[:2]),
        (far_last, ids_at(2)[2:]),
    )
    terms = [
        pair_terms(student_b, teacher_b, left_ids, chunk, ids.reshape(-1)) for chunk, ids in chunks
    ]
    losses, pulled = (sum(term) for term in zip(*terms))

    pulled = pulled[:rows] + from_twin(pulled[rows:])
    student, inverse = student[:rows], inverse[:rows]
    grad_student = student_scale / rows * pulled
    grad_projected = (
        inverse * (grad_student - student * jnp.sum(student * grad_student, axis=-1, keepdims=True))
    ).astype(jnp.bfloat16)

    grad_rows = lax.dot_general(
        one_hot(row_order(core), 1152),
        grad_projected,
        (((1,), (1,)), ((), ())),
        preferred_element_type=jnp.float32,
    ).astype(jnp.bfloat16)
    grad_rows = exchange(grad_rows.reshape(4, 320, rows), FIRST)
    line_grad = lax.dot_general(
        grad_rows, features, (((0, 2), (0, 1)), ((), ())), preferred_element_type=jnp.float32
    )
    core_grad = jnp.sum(exchange(line_grad.reshape(4, 80, 768), SECOND), axis=0)
    left, right = core_grad[:, :384], core_grad[:, 384:]
    other_losses = jnp.pad(losses[rows:].reshape(1, rows), ((0, 7), (0, 256)))
    arrived = from_twin(jnp.concatenate([jnp.where(core == 0, right, left), other_losses], axis=0))
    chip_grad = jnp.where(core == 0, left, right) + arrived[:80]
    row_loss = (losses[:rows] + arrived[80, :rows]) / rows

    column_grad = jnp.pad(chip_grad.reshape(16, 15, 128), ((0, 0), (0, 1), (0, 0)))
    own_grad = jnp.sum(exchange(column_grad, COLUMN), axis=0)[:15].reshape(5, 384)

    def adam(head_grad, first, second, weights):
        new_first = beta_one * first + (1.0 - beta_one) * head_grad
        new_second = beta_two * second + (1.0 - beta_two) * head_grad * head_grad
        first_hat = new_first / (1.0 - beta_one**adam_step)
        second_hat = new_second / (1.0 - beta_two**adam_step)
        weights = weights.astype(jnp.float32)
        updated = weights - learn_rate * (
            first_hat / (jnp.sqrt(second_hat) + adam_eps) + weight_decay * weights
        )
        return updated.astype(jnp.bfloat16)

    def piece(values, start):
        group_rows = lax.dynamic_slice_in_dim(values, start, 36, 0)
        padded = jnp.pad(group_rows, ((0, 4), (0, 0)))
        return lax.dynamic_slice(padded, ((xh * 4 + y) * 5, core * 384), (5, 384))

    own_weights = adam(
        own_grad,
        piece(moment_first, 0),
        piece(moment_second, 0),
        piece(head_weights, group_index * 36),
    )
    chip_weights = share(own_weights, COLUMN).reshape(80, 384)
    high = rounded(own_grad)
    middle = rounded(own_grad - high)
    low = own_grad - high - middle
    spare = jnp.zeros((1, 384), jnp.float32)
    grad_parts = jnp.concatenate([high, middle, low, spare], axis=0).astype(jnp.bfloat16)
    plane = share(jnp.concatenate([chip_weights, grad_parts], axis=0), PLANE).reshape(2, 768, 384)
    select_weights = one_hot(weight_order(), 768)
    halves = [
        jnp.dot(select_weights, plane[i], preferred_element_type=jnp.float32) for i in range(2)
    ]
    group_parts = jnp.dot(
        one_hot(grad_order(), 768),
        lax.dynamic_index_in_dim(plane, xl, 0, keepdims=False),
        preferred_element_type=jnp.float32,
    )
    half = jnp.concatenate([*halves, group_parts], axis=0).astype(jnp.bfloat16)
    twin_half = from_twin(half)
    whole = jnp.concatenate(
        [jnp.where(core == 0, half, twin_half), jnp.where(core == 0, twin_half, half)], axis=1
    )
    new_weights = whole[:1152]
    parts = whole[1152:].reshape(3, 40, 768).astype(jnp.float32)
    head_grad = ((parts[0] + parts[1]) + parts[2])[:36]
    new_first = beta_one * moment_first + (1.0 - beta_one) * head_grad
    new_second = beta_two * moment_second + (1.0 - beta_two) * head_grad * head_grad
    return (row_loss, new_first, new_second, new_weights)


def solution(mesh):
    placed = (
        P(("blk", "group"), None),
        P(("blk", "group"), None),
        P(("blk", "group"), None),
        P(),
        P(),
        P("group", None),
        P("group", None),
    )
    return jax.shard_map(
        per_device,
        mesh=mesh,
        in_specs=placed,
        out_specs=(P(("blk", "group")), P("group", None), P("group", None), P()),
        check_vma=False,
    )
```

```python
import jax
import jax.numpy as jnp
from jax import lax
from jax.experimental import pallas as pl
from jax.experimental.pallas import tpu as pltpu
from jax.sharding import PartitionSpec as P


student_scale = 20.0
student_bias = -1.0
teacher_scale = 25.0
teacher_bias = -1.5
label_mix = 0.5
norm_eps = 1e-06
beta_one = 0.9
beta_two = 0.95
learn_rate = 0.01
weight_decay = 0.0001
adam_eps = 1e-08
adam_step = 100.0

AXES = ("blk", "group")


def device(X, y, core, z):
    return (y * 4 + X % 2 * 2 + core) * 32 + X // 2 * 16 + z


def x_line(y, core, z):
    return [device(X, y, core, z) for X in range(4)]


def y_line(X, core, z):
    return [device(X, y, core, z) for y in range(4)]


def lines(along_x):
    groups = []
    for core in range(2):
        line = x_line if (core == 0) == along_x else y_line
        groups += [line(i, core, z) for z in range(16) for i in range(4)]
    return groups


FIRST = lines(True)
SECOND = lines(False)
PLANE = [
    [device(X, y, core, z) for X in range(4) for y in range(4)]
    for core in range(2)
    for z in range(16)
]
COLUMN = [
    [device(X, y, core, z) for z in range(16)]
    for X in range(4)
    for y in range(4)
    for core in range(2)
]
TWIN = [(i, i ^ 32) for i in range(512)]


def hop(step):
    pairs = []
    for i in range(512):
        blk, group = divmod(i, 32)
        y, xh, core = blk // 4, blk // 2 % 2, blk % 2
        xl, z = divmod(group, 16)
        x = xh * 2 + xl
        if core == 0:
            y = (y + step) % 4
        else:
            x = (x + step) % 4
        pairs.append((i, device(x % 2 * 2 + x // 2, y, core, z)))
    return pairs


FORTH = hop(1)
BACK = hop(-1)


def exchange(pieces, groups):
    return lax.all_to_all(pieces, AXES, 0, 0, axis_index_groups=groups, tiled=True)


def share(block, groups):
    return exchange(jnp.broadcast_to(block[None], (len(groups[0]), *block.shape)), groups)


def from_twin(shard):
    return lax.ppermute(shard, AXES, TWIN)


def unit_rows(values):
    values = values.astype(jnp.float32)
    return values * lax.rsqrt(jnp.sum(values * values, axis=-1, keepdims=True) + norm_eps)


def copies_kernel(values_ref, out_ref):
    rows = unit_rows(values_ref[...]).astype(jnp.bfloat16)
    for i in range(out_ref.shape[0]):
        out_ref[i] = rows


def unit_copies(values, count):
    return pl.pallas_call(
        copies_kernel,
        out_shape=jax.ShapeDtypeStruct((count, *values.shape), jnp.bfloat16),
        in_specs=[pl.BlockSpec(memory_space=pltpu.VMEM)],
        out_specs=pl.BlockSpec(memory_space=pltpu.VMEM),
    )(values)


def pair_terms(student_rows, teacher_rows, left_ids, text_rows, right_ids):
    dims = (((1,), (1,)), ((), ()))
    student_logit = (
        student_scale
        * lax.dot_general(student_rows, text_rows, dims, preferred_element_type=jnp.float32)
        + student_bias
    )
    teacher_logit = (
        teacher_scale
        * lax.dot_general(teacher_rows, text_rows, dims, preferred_element_type=jnp.float32)
        + teacher_bias
    )
    labels = (left_ids[:, None] == right_ids[None, :]).astype(jnp.float32)
    target = (1.0 - label_mix) * labels + label_mix * jax.nn.sigmoid(teacher_logit)
    losses = jnp.sum(jax.nn.softplus(student_logit) - target * student_logit, axis=1)
    coeff = (jax.nn.sigmoid(student_logit) - target).astype(jnp.bfloat16)
    pulled = jnp.dot(coeff, text_rows, preferred_element_type=jnp.float32)
    return (losses, pulled)


def row_order(core):
    place = lax.iota(jnp.int32, 1280)
    first, second = place // 320, place // 80 % 4
    X = jnp.where(core == 0, first, second)
    y = jnp.where(core == 0, second, first)
    row = (X % 2 * 4 + y) * 5 + place % 5
    return jnp.where(row < 36, X // 2 * 576 + place // 5 % 16 * 36 + row, -1)


def weight_order():
    row = lax.iota(jnp.int32, 576)
    q = row % 36
    return q // 5 * 96 + row // 36 * 5 + q % 5


def grad_order():
    part = lax.iota(jnp.int32, 120)
    q = part % 40
    return q // 5 * 96 + 80 + part // 40 * 5 + q % 5


def one_hot(index, width):
    return (index[:, None] == lax.iota(jnp.int32, width)[None, :]).astype(jnp.bfloat16)


def rounded(values):
    return lax.reduce_precision(values, 8, 7)


def per_device(
    student_features,
    teacher_image,
    text_embeds,
    pair_ids,
    head_weights,
    moment_first,
    moment_second,
):
    rows = student_features.shape[0]
    blk_index = lax.axis_index("blk")
    group_index = lax.axis_index("group")
    y, xh, core = blk_index // 4, blk_index // 2 % 2, blk_index % 2
    xl, z = group_index // 16, group_index % 16

    copies, teacher_image, twin_features = lax.optimization_barrier(
        (unit_copies(text_embeds, 4), teacher_image, student_features)
    )
    bundle = exchange(copies, FIRST).reshape(4 * rows, 1152)
    top, bottom = bundle[: 2 * rows], bundle[2 * rows :]
    before_top = lax.ppermute(top, AXES, FORTH)
    after_bottom = lax.ppermute(bottom, AXES, BACK)
    before_bottom = lax.ppermute(bottom, AXES, FORTH)
    after_top = lax.ppermute(top, AXES, BACK)
    far_top = lax.ppermute(before_top, AXES, FORTH)
    far_bottom = lax.ppermute(after_bottom, AXES, BACK)
    own_features, before_top, after_bottom = lax.optimization_barrier(
        (student_features, before_top, after_bottom)
    )
    features = share(own_features, FIRST)

    both_features = jnp.concatenate([student_features, from_twin(twin_features)], axis=0)
    both_teacher = jnp.concatenate([teacher_image, from_twin(teacher_image)], axis=0)
    projected = lax.dot_general(
        both_features, head_weights, (((1,), (1,)), ((), ())), preferred_element_type=jnp.float32
    )
    inverse = lax.rsqrt(jnp.sum(projected * projected, axis=-1, keepdims=True) + norm_eps)
    student = projected * inverse
    student_b = student.astype(jnp.bfloat16)
    teacher_b = unit_rows(both_teacher).astype(jnp.bfloat16)

    ids_grid = pair_ids.reshape(4, 2, 2, 2, 16, rows)
    ids_plane = lax.dynamic_index_in_dim(ids_grid, z, 4, keepdims=False)
    ids_core = lax.dynamic_index_in_dim(ids_plane, core, 2, keepdims=False)
    ids_yx = ids_core.transpose(0, 2, 1, 3).reshape(4, 4, rows)
    ids_xy = ids_core.transpose(1, 2, 0, 3).reshape(4, 4, rows)
    text_ids = jnp.where(core == 0, ids_yx, ids_xy)
    place = jnp.where(core == 0, y, xh * 2 + xl)

    def ids_at(step):
        return lax.dynamic_index_in_dim(text_ids, (place + step) % 4, 0, keepdims=False)

    ids_rows = pair_ids.reshape(512, rows)
    left_ids = jnp.concatenate(
        [
            lax.dynamic_index_in_dim(ids_rows, blk_index * 32 + group_index, 0, keepdims=False),
            lax.dynamic_index_in_dim(ids_rows, (blk_index ^ 1) * 32 + group_index, 0, keepdims=False),
        ]
    )
    chunks = (
        (bundle, ids_at(0)),
        (before_top, ids_at(3)[:2]),
        (after_bottom, ids_at(1)[2:]),
        (before_bottom, ids_at(3)[2:]),
        (after_top, ids_at(1)[:2]),
        (far_top, ids_at(2)[:2]),
        (far_bottom, ids_at(2)[2:]),
    )
    terms = [
        pair_terms(student_b, teacher_b, left_ids, chunk, ids.reshape(-1)) for chunk, ids in chunks
    ]
    losses, pulled = (sum(term) for term in zip(*terms))
    features, pulled = lax.optimization_barrier((features, pulled))

    pulled = pulled[:rows] + from_twin(pulled[rows:])
    student, inverse = student[:rows], inverse[:rows]
    grad_student = student_scale / rows * pulled
    grad_projected = (
        inverse * (grad_student - student * jnp.sum(student * grad_student, axis=-1, keepdims=True))
    ).astype(jnp.bfloat16)

    grad_rows = lax.dot_general(
        one_hot(row_order(core), 1152),
        grad_projected,
        (((1,), (1,)), ((), ())),
        preferred_element_type=jnp.float32,
    ).astype(jnp.bfloat16)
    grad_rows = exchange(grad_rows.reshape(4, 320, rows), FIRST)
    line_grad = lax.dot_general(
        grad_rows, features, (((0, 2), (0, 1)), ((), ())), preferred_element_type=jnp.float32
    )
    core_grad = jnp.sum(exchange(line_grad.reshape(4, 80, 768), SECOND), axis=0)
    left, right = core_grad[:, :384], core_grad[:, 384:]
    other_losses = jnp.pad(losses[rows:].reshape(1, rows), ((0, 7), (0, 256)))
    arrived = from_twin(jnp.concatenate([jnp.where(core == 0, right, left), other_losses], axis=0))
    chip_grad = jnp.where(core == 0, left, right) + arrived[:80]
    row_loss = (losses[:rows] + arrived[80, :rows]) / rows

    column_grad = jnp.pad(chip_grad.reshape(16, 15, 128), ((0, 0), (0, 1), (0, 0)))
    own_grad = jnp.sum(exchange(column_grad, COLUMN), axis=0)[:15].reshape(5, 384)

    def adam(head_grad, first, second, weights):
        new_first = beta_one * first + (1.0 - beta_one) * head_grad
        new_second = beta_two * second + (1.0 - beta_two) * head_grad * head_grad
        first_hat = new_first / (1.0 - beta_one**adam_step)
        second_hat = new_second / (1.0 - beta_two**adam_step)
        weights = weights.astype(jnp.float32)
        updated = weights - learn_rate * (
            first_hat / (jnp.sqrt(second_hat) + adam_eps) + weight_decay * weights
        )
        return updated.astype(jnp.bfloat16)

    def piece(values, start):
        group_rows = lax.dynamic_slice_in_dim(values, start, 36, 0)
        padded = jnp.pad(group_rows, ((0, 4), (0, 0)))
        return lax.dynamic_slice(padded, ((xh * 4 + y) * 5, core * 384), (5, 384))

    own_weights = adam(
        own_grad,
        piece(moment_first, 0),
        piece(moment_second, 0),
        piece(head_weights, group_index * 36),
    )
    chip_weights = share(own_weights, COLUMN).reshape(80, 384)
    high = rounded(own_grad)
    middle = rounded(own_grad - high)
    low = own_grad - high - middle
    spare = jnp.zeros((1, 384), jnp.float32)
    grad_parts = jnp.concatenate([high, middle, low, spare], axis=0).astype(jnp.bfloat16)
    plane = share(jnp.concatenate([chip_weights, grad_parts], axis=0), PLANE).reshape(2, 768, 384)
    select_weights = one_hot(weight_order(), 768)
    halves = [
        jnp.dot(select_weights, plane[i], preferred_element_type=jnp.float32) for i in range(2)
    ]
    group_parts = jnp.dot(
        one_hot(grad_order(), 768),
        lax.dynamic_index_in_dim(plane, xl, 0, keepdims=False),
        preferred_element_type=jnp.float32,
    )
    half = jnp.concatenate([*halves, group_parts], axis=0).astype(jnp.bfloat16)
    twin_half = from_twin(half)
    whole = jnp.concatenate(
        [jnp.where(core == 0, half, twin_half), jnp.where(core == 0, twin_half, half)], axis=1
    )
    new_weights = whole[:1152]
    parts = whole[1152:].reshape(3, 40, 768).astype(jnp.float32)
    head_grad = ((parts[0] + parts[1]) + parts[2])[:36]
    new_first = beta_one * moment_first + (1.0 - beta_one) * head_grad
    new_second = beta_two * moment_second + (1.0 - beta_two) * head_grad * head_grad
    return (row_loss, new_first, new_second, new_weights)


def solution(mesh):
    placed = (
        P(("blk", "group"), None),
        P(("blk", "group"), None),
        P(("blk", "group"), None),
        P(),
        P(),
        P("group", None),
        P("group", None),
    )
    return jax.shard_map(
        per_device,
        mesh=mesh,
        in_specs=placed,
        out_specs=(P(("blk", "group")), P("group", None), P("group", None), P()),
        check_vma=False,
    )
```

```python
import functools

import jax
import jax.numpy as jnp
from jax import lax
from jax.experimental import pallas as pl
from jax.experimental.pallas import tpu as pltpu
from jax.sharding import PartitionSpec as P


student_scale = 20.0
student_bias = -1.0
teacher_scale = 25.0
teacher_bias = -1.5
label_mix = 0.5
norm_eps = 1e-06
beta_one = 0.9
beta_two = 0.95
learn_rate = 0.01
weight_decay = 0.0001
adam_eps = 1e-08
adam_step = 100.0

AXES = ("blk", "group")


def device(X, y, core, z):
    return (y * 4 + X % 2 * 2 + core) * 32 + X // 2 * 16 + z


def x_line(y, core, z):
    return [device(X, y, core, z) for X in range(4)]


def y_line(X, core, z):
    return [device(X, y, core, z) for y in range(4)]


def lines(along_x):
    groups = []
    for core in range(2):
        line = x_line if (core == 0) == along_x else y_line
        groups += [line(i, core, z) for z in range(16) for i in range(4)]
    return groups


FIRST = lines(True)
SECOND = lines(False)
PLANE = [
    [device(X, y, core, z) for X in range(4) for y in range(4)]
    for core in range(2)
    for z in range(16)
]
COLUMN = [
    [device(X, y, core, z) for z in range(16)]
    for X in range(4)
    for y in range(4)
    for core in range(2)
]
TWIN = [(i, i ^ 32) for i in range(512)]


def hop(step):
    pairs = []
    for i in range(512):
        blk, group = divmod(i, 32)
        y, xh, core = blk // 4, blk // 2 % 2, blk % 2
        xl, z = divmod(group, 16)
        x = xh * 2 + xl
        if core == 0:
            y = (y + step) % 4
        else:
            x = (x + step) % 4
        pairs.append((i, device(x % 2 * 2 + x // 2, y, core, z)))
    return pairs


FORTH = hop(1)
BACK = hop(-1)


def exchange(pieces, groups):
    return lax.all_to_all(pieces, AXES, 0, 0, axis_index_groups=groups, tiled=True)


def share(block, groups):
    return exchange(jnp.broadcast_to(block[None], (len(groups[0]), *block.shape)), groups)


def from_twin(shard):
    return lax.ppermute(shard, AXES, TWIN)


def unit_rows(values):
    values = values.astype(jnp.float32)
    return values * lax.rsqrt(jnp.sum(values * values, axis=-1, keepdims=True) + norm_eps)


def copies_kernel(values_ref, others_ref, out_ref):
    width = values_ref.shape[1]
    rows = unit_rows(values_ref[...]).astype(jnp.bfloat16)
    for i in range(out_ref.shape[0]):
        out_ref[i, :, :width] = rows
        out_ref[i, :, width:] = others_ref[...]


def unit_copies(values, others, count):
    width = values.shape[1] + others.shape[1]
    return pl.pallas_call(
        copies_kernel,
        out_shape=jax.ShapeDtypeStruct((count, values.shape[0], width), jnp.bfloat16),
        in_specs=[pl.BlockSpec(memory_space=pltpu.VMEM)] * 2,
        out_specs=pl.BlockSpec(memory_space=pltpu.VMEM),
        compiler_params=pltpu.CompilerParams(vmem_limit_bytes=8 << 20),
        cost_estimate=pl.CostEstimate(
            flops=4 * values.size,
            bytes_accessed=2 * values.size + 2 * count * values.shape[0] * width,
            transcendentals=0,
        ),
    )(values, others)


def pair_terms(student_rows, teacher_rows, left_ids, text_rows, right_ids):
    dims = (((1,), (1,)), ((), ()))
    student_logit = (
        student_scale
        * lax.dot_general(student_rows, text_rows, dims, preferred_element_type=jnp.float32)
        + student_bias
    )
    teacher_logit = (
        teacher_scale
        * lax.dot_general(teacher_rows, text_rows, dims, preferred_element_type=jnp.float32)
        + teacher_bias
    )
    labels = (left_ids == right_ids).astype(jnp.float32)
    target = (1.0 - label_mix) * labels + label_mix * jax.nn.sigmoid(teacher_logit)
    tail = jnp.exp(-jnp.abs(student_logit))
    softplus = jnp.maximum(student_logit, 0.0) + jnp.log1p(tail)
    chance = jnp.where(student_logit >= 0.0, 1.0, tail) / (1.0 + tail)
    losses = jnp.sum(softplus - target * student_logit, axis=1, keepdims=True)
    return losses, (chance - target).astype(jnp.bfloat16)


def pair_kernel(parts, carried, *refs):
    student_ref, teacher_ref, left_ref = refs[:3]
    chunks, ids = refs[3 : 3 + parts], refs[3 + parts : 3 + 2 * parts]
    rest = refs[3 + 2 * parts :]
    pulled_ref, losses_ref = rest[-2:]
    if carried:
        pulled_ref[...] = rest[0][...]
        losses_ref[...] = rest[1][...]
    else:
        pulled_ref[...] = jnp.zeros_like(pulled_ref)
        losses_ref[...] = jnp.zeros_like(losses_ref)
    for chunk_ref, ids_ref in zip(chunks, ids):
        texts = chunk_ref[...]
        losses, coeff = pair_terms(
            student_ref[...], teacher_ref[...], left_ref[...], texts, ids_ref[...]
        )
        losses_ref[...] += losses
        pulled_ref[...] += jnp.dot(coeff, texts, preferred_element_type=jnp.float32)


def pair_sums(student_rows, teacher_rows, left_ids, chunks, carried=()):
    rows, width = student_rows.shape
    texts = [chunk for chunk, _ in chunks]
    ids = [ids.reshape(1, -1) for _, ids in chunks]
    count = sum(chunk.shape[0] for chunk in texts)
    operands = (student_rows, teacher_rows, left_ids, *texts, *ids, *carried)
    whole = pl.BlockSpec(memory_space=pltpu.VMEM)
    return pl.pallas_call(
        functools.partial(pair_kernel, len(texts), bool(carried)),
        out_shape=(
            jax.ShapeDtypeStruct((rows, width), jnp.float32),
            jax.ShapeDtypeStruct((rows, 1), jnp.float32),
        ),
        in_specs=[whole] * len(operands),
        out_specs=(whole, whole),
        compiler_params=pltpu.CompilerParams(vmem_limit_bytes=20 << 20),
        cost_estimate=pl.CostEstimate(
            flops=6 * rows * count * width,
            bytes_accessed=2 * count * width,
            transcendentals=4 * rows * count,
        ),
    )(*operands)


def row_order(core):
    place = lax.iota(jnp.int32, 1280)
    first, second = place // 320, place // 80 % 4
    X = jnp.where(core == 0, first, second)
    y = jnp.where(core == 0, second, first)
    row = (X % 2 * 4 + y) * 5 + place % 5
    return jnp.where(row < 36, X // 2 * 576 + place // 5 % 16 * 36 + row, -1)


def weight_order():
    row = lax.iota(jnp.int32, 576)
    q = row % 36
    return q // 5 * 96 + row // 36 * 5 + q % 5


def grad_order():
    part = lax.iota(jnp.int32, 120)
    q = part % 40
    return q // 5 * 96 + 80 + part // 40 * 5 + q % 5


def one_hot(index, width):
    return (index[:, None] == lax.iota(jnp.int32, width)[None, :]).astype(jnp.bfloat16)


def rounded(values):
    return lax.reduce_precision(values, 8, 7)


def per_device(
    student_features,
    teacher_image,
    text_embeds,
    pair_ids,
    head_weights,
    moment_first,
    moment_second,
):
    rows = student_features.shape[0]
    blk_index = lax.axis_index("blk")
    group_index = lax.axis_index("group")
    y, xh, core = blk_index // 4, blk_index // 2 % 2, blk_index % 2
    xl, z = group_index // 16, group_index % 16

    copies, teacher_image, twin_features = lax.optimization_barrier(
        (unit_copies(text_embeds, student_features, 4), teacher_image, student_features)
    )
    near = exchange(copies, FIRST)
    top = near[:2, :, :1152].reshape(2 * rows, 1152)
    bottom = near[2:, :, :1152].reshape(2 * rows, 1152)
    features = near[:, :, 1152:]
    before_top = lax.ppermute(top, AXES, FORTH)
    after_bottom = lax.ppermute(bottom, AXES, BACK)
    before_bottom = lax.ppermute(bottom, AXES, FORTH)
    after_top = lax.ppermute(top, AXES, BACK)
    far_top = lax.ppermute(before_top, AXES, FORTH)
    far_bottom = lax.ppermute(after_bottom, AXES, BACK)

    far_features, far_teacher = from_twin(twin_features), from_twin(teacher_image)
    both_features = jnp.concatenate([student_features, far_features], axis=0)
    both_teacher = jnp.concatenate([teacher_image, far_teacher], axis=0)
    projected = lax.dot_general(
        both_features, head_weights, (((1,), (1,)), ((), ())), preferred_element_type=jnp.float32
    )
    inverse = lax.rsqrt(jnp.sum(projected * projected, axis=-1, keepdims=True) + norm_eps)
    student = projected * inverse
    student_b = student.astype(jnp.bfloat16)
    teacher_b = unit_rows(both_teacher).astype(jnp.bfloat16)

    ids_grid = pair_ids.reshape(4, 2, 2, 2, 16, rows)
    ids_plane = lax.dynamic_index_in_dim(ids_grid, z, 4, keepdims=False)
    ids_core = lax.dynamic_index_in_dim(ids_plane, core, 2, keepdims=False)
    ids_yx = ids_core.transpose(0, 2, 1, 3).reshape(4, 4, rows)
    ids_xy = ids_core.transpose(1, 2, 0, 3).reshape(4, 4, rows)
    text_ids = jnp.where(core == 0, ids_yx, ids_xy)
    place = jnp.where(core == 0, y, xh * 2 + xl)

    def ids_at(step):
        return lax.dynamic_index_in_dim(text_ids, (place + step) % 4, 0, keepdims=False)

    ids_rows = pair_ids.reshape(512, rows)
    left_ids = jnp.concatenate(
        [
            lax.dynamic_index_in_dim(ids_rows, blk_index * 32 + group_index, 0, keepdims=False),
            lax.dynamic_index_in_dim(ids_rows, (blk_index ^ 1) * 32 + group_index, 0, keepdims=False),
        ]
    )
    images = (student_b, teacher_b, left_ids.reshape(-1, 1))
    own_chunks = [(top, ids_at(0)[:2]), (bottom, ids_at(0)[2:])]
    sums = pair_sums(*images, own_chunks)
    near_chunks = [
        (before_top, ids_at(3)[:2]),
        (after_bottom, ids_at(1)[2:]),
        (before_bottom, ids_at(3)[2:]),
        (after_top, ids_at(1)[:2]),
    ]
    sums = pair_sums(*images, near_chunks, sums)
    pulled, losses = pair_sums(
        *images, [(far_top, ids_at(2)[:2]), (far_bottom, ids_at(2)[2:])], sums
    )
    losses = losses.reshape(-1)

    pulled = pulled[:rows] + from_twin(pulled[rows:])
    student, inverse = student[:rows], inverse[:rows]
    grad_student = student_scale / rows * pulled
    grad_projected = (
        inverse * (grad_student - student * jnp.sum(student * grad_student, axis=-1, keepdims=True))
    ).astype(jnp.bfloat16)

    grad_rows = lax.dot_general(
        one_hot(row_order(core), 1152),
        grad_projected,
        (((1,), (1,)), ((), ())),
        preferred_element_type=jnp.float32,
    ).astype(jnp.bfloat16)
    grad_rows = exchange(grad_rows.reshape(4, 320, rows), FIRST)
    line_grad = lax.dot_general(
        grad_rows, features, (((0, 2), (0, 1)), ((), ())), preferred_element_type=jnp.float32
    )
    core_grad = jnp.sum(exchange(line_grad.reshape(4, 80, 768), SECOND), axis=0)
    left, right = core_grad[:, :384], core_grad[:, 384:]
    other_losses = jnp.pad(losses[rows:].reshape(1, rows), ((0, 7), (0, 256)))
    arrived = from_twin(jnp.concatenate([jnp.where(core == 0, right, left), other_losses], axis=0))
    chip_grad = jnp.where(core == 0, left, right) + arrived[:80]
    row_loss = (losses[:rows] + arrived[80, :rows]) / rows

    column_grad = jnp.pad(chip_grad.reshape(16, 15, 128), ((0, 0), (0, 1), (0, 0)))
    own_grad = jnp.sum(exchange(column_grad, COLUMN), axis=0)[:15].reshape(5, 384)

    def adam(head_grad, first, second, weights):
        new_first = beta_one * first + (1.0 - beta_one) * head_grad
        new_second = beta_two * second + (1.0 - beta_two) * head_grad * head_grad
        first_hat = new_first / (1.0 - beta_one**adam_step)
        second_hat = new_second / (1.0 - beta_two**adam_step)
        weights = weights.astype(jnp.float32)
        updated = weights - learn_rate * (
            first_hat / (jnp.sqrt(second_hat) + adam_eps) + weight_decay * weights
        )
        return updated.astype(jnp.bfloat16)

    def piece(values, start):
        group_rows = lax.dynamic_slice_in_dim(values, start, 36, 0)
        padded = jnp.pad(group_rows, ((0, 4), (0, 0)))
        return lax.dynamic_slice(padded, ((xh * 4 + y) * 5, core * 384), (5, 384))

    own_weights = adam(
        own_grad,
        piece(moment_first, 0),
        piece(moment_second, 0),
        piece(head_weights, group_index * 36),
    )
    chip_weights = share(own_weights, COLUMN).reshape(80, 384)
    high = rounded(own_grad)
    middle = rounded(own_grad - high)
    low = own_grad - high - middle
    spare = jnp.zeros((1, 384), jnp.float32)
    grad_parts = jnp.concatenate([high, middle, low, spare], axis=0).astype(jnp.bfloat16)
    plane = share(jnp.concatenate([chip_weights, grad_parts], axis=0), PLANE).reshape(2, 768, 384)
    select_weights = one_hot(weight_order(), 768)
    halves = [
        jnp.dot(select_weights, plane[i], preferred_element_type=jnp.float32) for i in range(2)
    ]
    group_parts = jnp.dot(
        one_hot(grad_order(), 768),
        lax.dynamic_index_in_dim(plane, xl, 0, keepdims=False),
        preferred_element_type=jnp.float32,
    )
    half = jnp.concatenate([*halves, group_parts], axis=0).astype(jnp.bfloat16)
    twin_half = from_twin(half)
    whole = jnp.concatenate(
        [jnp.where(core == 0, half, twin_half), jnp.where(core == 0, twin_half, half)], axis=1
    )
    new_weights = whole[:1152]
    parts = whole[1152:].reshape(3, 40, 768).astype(jnp.float32)
    head_grad = ((parts[0] + parts[1]) + parts[2])[:36]
    new_first = beta_one * moment_first + (1.0 - beta_one) * head_grad
    new_second = beta_two * moment_second + (1.0 - beta_two) * head_grad * head_grad
    return (row_loss, new_first, new_second, new_weights)


def solution(mesh):
    placed = (
        P(("blk", "group"), None),
        P(("blk", "group"), None),
        P(("blk", "group"), None),
        P(),
        P(),
        P("group", None),
        P("group", None),
    )
    return jax.shard_map(
        per_device,
        mesh=mesh,
        in_specs=placed,
        out_specs=(P(("blk", "group")), P("group", None), P("group", None), P()),
        check_vma=False,
    )
```

```python
import functools

import jax
import jax.numpy as jnp
from jax import lax
from jax.experimental import pallas as pl
from jax.experimental.pallas import tpu as pltpu
from jax.sharding import PartitionSpec as P


student_scale = 20.0
student_bias = -1.0
teacher_scale = 25.0
teacher_bias = -1.5
label_mix = 0.5
norm_eps = 1e-06
beta_one = 0.9
beta_two = 0.95
learn_rate = 0.01
weight_decay = 0.0001
adam_eps = 1e-08
adam_step = 100.0

AXES = ("blk", "group")


def device(X, y, core, z):
    return (y * 4 + X % 2 * 2 + core) * 32 + X // 2 * 16 + z


PLANE = [
    [device(X, y, core, z) for X in range(4) for y in range(4)]
    for core in range(2)
    for z in range(16)
]
COLUMN = [
    [device(X, y, core, z) for z in range(16)]
    for X in range(4)
    for y in range(4)
    for core in range(2)
]
TWIN = [(i, i ^ 32) for i in range(512)]


def hop(step, first):
    pairs = []
    for i in range(512):
        blk, group = divmod(i, 32)
        y, xh, core = blk // 4, blk // 2 % 2, blk % 2
        xl, z = divmod(group, 16)
        x = xh * 2 + xl
        if (core == 0) == first:
            x = (x + step) % 4
        else:
            y = (y + step) % 4
        pairs.append((i, device(x % 2 * 2 + x // 2, y, core, z)))
    return pairs


FIRST = {step: hop(step, True) for step in (1, 2, 3)}
SECOND = {step: hop(step, False) for step in (1, 2, 3)}


def moved(shard, pairs):
    return lax.ppermute(shard, AXES, pairs)


def exchange(pieces, groups):
    return lax.all_to_all(pieces, AXES, 0, 0, axis_index_groups=groups, tiled=True)


def share(block, groups):
    return exchange(jnp.broadcast_to(block[None], (len(groups[0]), *block.shape)), groups)


def from_twin(shard):
    return lax.ppermute(shard, AXES, TWIN)


def unit_rows(values):
    values = values.astype(jnp.float32)
    return values * lax.rsqrt(jnp.sum(values * values, axis=-1, keepdims=True) + norm_eps)


def head_kernel(texts_ref, teacher_ref, features_ref, near_ref, images_ref):
    width = texts_ref.shape[1]
    depth = features_ref.shape[1]
    near_ref[:, :width] = unit_rows(texts_ref[...]).astype(jnp.bfloat16)
    near_ref[:, width:] = features_ref[...]
    images_ref[:, :depth] = features_ref[...]
    images_ref[:, depth:] = unit_rows(teacher_ref[...]).astype(jnp.bfloat16)


def head(texts, teacher, features):
    shape = (texts.shape[0], texts.shape[1] + features.shape[1])
    whole = pl.BlockSpec(memory_space=pltpu.VMEM)
    return pl.pallas_call(
        head_kernel,
        out_shape=(jax.ShapeDtypeStruct(shape, jnp.bfloat16),) * 2,
        in_specs=[whole] * 3,
        out_specs=(whole, whole),
        compiler_params=pltpu.CompilerParams(vmem_limit_bytes=8 << 20),
        cost_estimate=pl.CostEstimate(
            flops=8 * texts.size, bytes_accessed=8 * shape[0] * shape[1], transcendentals=0
        ),
    )(texts, teacher, features)


def line_kernel(*refs):
    grads, nears, out_ref = refs[:4], refs[4:8], refs[8]
    total = jnp.zeros(out_ref.shape, jnp.float32)
    for grad_ref, near_ref in zip(grads, nears):
        total += jnp.dot(grad_ref[...], near_ref[:, 1152:], preferred_element_type=jnp.float32)
    out_ref[...] = total


def line_sum(grads, nears):
    whole = pl.BlockSpec(memory_space=pltpu.VMEM)
    return pl.pallas_call(
        line_kernel,
        out_shape=jax.ShapeDtypeStruct((320, 768), jnp.float32),
        in_specs=[whole] * 8,
        out_specs=whole,
        compiler_params=pltpu.CompilerParams(vmem_limit_bytes=12 << 20),
        cost_estimate=pl.CostEstimate(
            flops=8 * 320 * 128 * 768, bytes_accessed=4 << 20, transcendentals=0
        ),
    )(*grads, *nears)


def pair_terms(student_rows, teacher_rows, left_ids, text_rows, right_ids):
    dims = (((1,), (1,)), ((), ()))
    student_logit = (
        student_scale
        * lax.dot_general(student_rows, text_rows, dims, preferred_element_type=jnp.float32)
        + student_bias
    )
    teacher_logit = (
        teacher_scale
        * lax.dot_general(teacher_rows, text_rows, dims, preferred_element_type=jnp.float32)
        + teacher_bias
    )
    labels = (left_ids == right_ids).astype(jnp.float32)
    target = (1.0 - label_mix) * labels + label_mix * jax.nn.sigmoid(teacher_logit)
    tail = jnp.exp(-jnp.abs(student_logit))
    softplus = jnp.maximum(student_logit, 0.0) + jnp.log1p(tail)
    chance = jnp.where(student_logit >= 0.0, 1.0, tail) / (1.0 + tail)
    losses = jnp.sum(softplus - target * student_logit, axis=1, keepdims=True)
    return losses, (chance - target).astype(jnp.bfloat16)


def pair_kernel(parts, carried, *refs):
    student_ref, teacher_ref, left_ref = refs[:3]
    chunks, ids = refs[3 : 3 + parts], refs[3 + parts : 3 + 2 * parts]
    rest = refs[3 + 2 * parts :]
    pulled_ref, losses_ref = rest[-2:]
    if carried:
        pulled_ref[...] = rest[0][...]
        losses_ref[...] = rest[1][...]
    else:
        pulled_ref[...] = jnp.zeros_like(pulled_ref)
        losses_ref[...] = jnp.zeros_like(losses_ref)
    for chunk_ref, ids_ref in zip(chunks, ids):
        texts = chunk_ref[...]
        losses, coeff = pair_terms(
            student_ref[...], teacher_ref[...], left_ref[...], texts, ids_ref[...]
        )
        losses_ref[...] += losses
        pulled_ref[...] += jnp.dot(coeff, texts, preferred_element_type=jnp.float32)


def pair_sums(student_rows, teacher_rows, left_ids, chunks, carried=()):
    rows, width = student_rows.shape
    texts = [chunk for chunk, _ in chunks]
    ids = [ids.reshape(1, -1) for _, ids in chunks]
    count = sum(chunk.shape[0] for chunk in texts)
    operands = (student_rows, teacher_rows, left_ids, *texts, *ids, *carried)
    whole = pl.BlockSpec(memory_space=pltpu.VMEM)
    return pl.pallas_call(
        functools.partial(pair_kernel, len(texts), bool(carried)),
        out_shape=(
            jax.ShapeDtypeStruct((rows, width), jnp.float32),
            jax.ShapeDtypeStruct((rows, 1), jnp.float32),
        ),
        in_specs=[whole] * len(operands),
        out_specs=(whole, whole),
        compiler_params=pltpu.CompilerParams(vmem_limit_bytes=20 << 20),
        cost_estimate=pl.CostEstimate(
            flops=6 * rows * count * width,
            bytes_accessed=2 * count * width,
            transcendentals=4 * rows * count,
        ),
    )(*operands)


def row_order(x, y, core):
    place = lax.iota(jnp.int32, 1280)
    first, second = place // 320, place // 80 % 4
    x = (x + jnp.where(core == 0, first, second)) % 4
    y = (y + jnp.where(core == 0, second, first)) % 4
    row = (x // 2 * 4 + y) * 5 + place % 5
    return jnp.where(row < 36, x % 2 * 576 + place // 5 % 16 * 36 + row, -1)


def weight_order():
    row = lax.iota(jnp.int32, 576)
    q = row % 36
    return q // 5 * 96 + row // 36 * 5 + q % 5


def grad_order():
    part = lax.iota(jnp.int32, 120)
    q = part % 40
    return q // 5 * 96 + 80 + part // 40 * 5 + q % 5


def one_hot(index, width):
    return (index[:, None] == lax.iota(jnp.int32, width)[None, :]).astype(jnp.bfloat16)


def rounded(values):
    return lax.reduce_precision(values, 8, 7)


def per_device(
    student_features,
    teacher_image,
    text_embeds,
    pair_ids,
    head_weights,
    moment_first,
    moment_second,
):
    rows = student_features.shape[0]
    blk_index = lax.axis_index("blk")
    group_index = lax.axis_index("group")
    y, xh, core = blk_index // 4, blk_index // 2 % 2, blk_index % 2
    xl, z = group_index // 16, group_index % 16

    x = xh * 2 + xl
    near, images = head(text_embeds, teacher_image, student_features)
    near_before = moved(near, FIRST[1])
    near_after = moved(near, FIRST[3])
    near_far = moved(near, FIRST[2])
    far_images = from_twin(images)
    width = text_embeds.shape[1]
    top = jnp.concatenate([near[:, :width], near_before[:, :width]], axis=0)
    bottom = jnp.concatenate([near_after[:, :width], near_far[:, :width]], axis=0)
    before_top = moved(top, SECOND[1])
    after_top = moved(top, SECOND[3])
    after_bottom = moved(bottom, SECOND[3])
    before_bottom = moved(bottom, SECOND[1])
    far_top = moved(before_top, SECOND[1])
    far_bottom = moved(after_bottom, SECOND[3])

    depth = student_features.shape[1]
    both_features = jnp.concatenate([student_features, far_images[:, :depth]], axis=0)
    teacher_b = jnp.concatenate([images[:, depth:], far_images[:, depth:]], axis=0)
    projected = lax.dot_general(
        both_features, head_weights, (((1,), (1,)), ((), ())), preferred_element_type=jnp.float32
    )
    inverse = lax.rsqrt(jnp.sum(projected * projected, axis=-1, keepdims=True) + norm_eps)
    student = projected * inverse
    student_b = student.astype(jnp.bfloat16)

    ids_grid = pair_ids.reshape(4, 2, 2, 2, 16, rows)
    ids_plane = lax.dynamic_index_in_dim(ids_grid, z, 4, keepdims=False)
    ids_core = lax.dynamic_index_in_dim(ids_plane, core, 2, keepdims=False)
    ids_yx = ids_core.reshape(4, 4, rows)
    text_ids = jnp.where(core == 0, ids_yx, ids_yx.transpose(1, 0, 2))
    first, second = jnp.where(core == 0, x, y), jnp.where(core == 0, y, x)
    text_ids = jnp.concatenate([text_ids, text_ids], axis=0)
    text_ids = lax.dynamic_slice_in_dim(text_ids, second, 4, 0)
    text_ids = jnp.concatenate([text_ids, text_ids], axis=1)
    text_ids = lax.dynamic_slice_in_dim(text_ids, first, 4, 1)
    top_ids = jnp.concatenate([text_ids[:, 0], text_ids[:, 3]], axis=1)
    bottom_ids = jnp.concatenate([text_ids[:, 1], text_ids[:, 2]], axis=1)

    ids_rows = pair_ids.reshape(512, rows)
    left_ids = jnp.concatenate(
        [
            lax.dynamic_index_in_dim(ids_rows, blk_index * 32 + group_index, 0, keepdims=False),
            lax.dynamic_index_in_dim(ids_rows, (blk_index ^ 1) * 32 + group_index, 0, keepdims=False),
        ]
    )
    pair_rows = (student_b, teacher_b, left_ids.reshape(-1, 1))
    own_chunks = [(top, top_ids[0]), (bottom, bottom_ids[0])]
    sums = pair_sums(*pair_rows, own_chunks)
    near_chunks = [
        (before_top, top_ids[3]),
        (after_top, top_ids[1]),
        (after_bottom, bottom_ids[1]),
        (before_bottom, bottom_ids[3]),
    ]
    sums = pair_sums(*pair_rows, near_chunks, sums)
    far_chunks = [(far_top, top_ids[2]), (far_bottom, bottom_ids[2])]
    pulled, losses = pair_sums(*pair_rows, far_chunks, sums)
    losses = losses.reshape(-1)

    pulled = pulled[:rows] + from_twin(pulled[rows:])
    student, inverse = student[:rows], inverse[:rows]
    grad_student = student_scale / rows * pulled
    grad_projected = (
        inverse * (grad_student - student * jnp.sum(student * grad_student, axis=-1, keepdims=True))
    ).astype(jnp.bfloat16)

    grad_rows = lax.dot_general(
        one_hot(row_order(x, y, core), 1152),
        grad_projected,
        (((1,), (1,)), ((), ())),
        preferred_element_type=jnp.float32,
    ).astype(jnp.bfloat16)
    grad_rows = grad_rows.reshape(4, 320, rows)
    grads = (
        grad_rows[0],
        moved(grad_rows[1], FIRST[1]),
        moved(grad_rows[3], FIRST[3]),
        moved(grad_rows[2], FIRST[2]),
    )
    line_grad = line_sum(grads, (near, near_before, near_after, near_far)).reshape(4, 80, 768)
    core_grad = (line_grad[0] + moved(line_grad[1], SECOND[1])) + (
        moved(line_grad[2], SECOND[2]) + moved(line_grad[3], SECOND[3])
    )
    left, right = core_grad[:, :384], core_grad[:, 384:]
    other_losses = jnp.pad(losses[rows:].reshape(1, rows), ((0, 7), (0, 256)))
    arrived = from_twin(jnp.concatenate([jnp.where(core == 0, right, left), other_losses], axis=0))
    chip_grad = jnp.where(core == 0, left, right) + arrived[:80]
    row_loss = (losses[:rows] + arrived[80, :rows]) / rows

    column_grad = jnp.pad(chip_grad.reshape(16, 15, 128), ((0, 0), (0, 1), (0, 0)))
    own_grad = jnp.sum(exchange(column_grad, COLUMN), axis=0)[:15].reshape(5, 384)

    def adam(head_grad, first, second, weights):
        new_first = beta_one * first + (1.0 - beta_one) * head_grad
        new_second = beta_two * second + (1.0 - beta_two) * head_grad * head_grad
        first_hat = new_first / (1.0 - beta_one**adam_step)
        second_hat = new_second / (1.0 - beta_two**adam_step)
        weights = weights.astype(jnp.float32)
        updated = weights - learn_rate * (
            first_hat / (jnp.sqrt(second_hat) + adam_eps) + weight_decay * weights
        )
        return updated.astype(jnp.bfloat16)

    def piece(values, start):
        group_rows = lax.dynamic_slice_in_dim(values, start, 36, 0)
        padded = jnp.pad(group_rows, ((0, 4), (0, 0)))
        return lax.dynamic_slice(padded, ((xh * 4 + y) * 5, core * 384), (5, 384))

    own_weights = adam(
        own_grad,
        piece(moment_first, 0),
        piece(moment_second, 0),
        piece(head_weights, group_index * 36),
    )
    chip_weights = share(own_weights, COLUMN).reshape(80, 384)
    high = rounded(own_grad)
    middle = rounded(own_grad - high)
    low = own_grad - high - middle
    spare = jnp.zeros((1, 384), jnp.float32)
    grad_parts = jnp.concatenate([high, middle, low, spare], axis=0).astype(jnp.bfloat16)
    plane = share(jnp.concatenate([chip_weights, grad_parts], axis=0), PLANE).reshape(2, 768, 384)
    select_weights = one_hot(weight_order(), 768)
    halves = [
        jnp.dot(select_weights, plane[i], preferred_element_type=jnp.float32) for i in range(2)
    ]
    group_parts = jnp.dot(
        one_hot(grad_order(), 768),
        lax.dynamic_index_in_dim(plane, xl, 0, keepdims=False),
        preferred_element_type=jnp.float32,
    )
    half = jnp.concatenate([*halves, group_parts], axis=0).astype(jnp.bfloat16)
    twin_half = from_twin(half)
    whole = jnp.concatenate(
        [jnp.where(core == 0, half, twin_half), jnp.where(core == 0, twin_half, half)], axis=1
    )
    new_weights = whole[:1152]
    parts = whole[1152:].reshape(3, 40, 768).astype(jnp.float32)
    head_grad = ((parts[0] + parts[1]) + parts[2])[:36]
    new_first = beta_one * moment_first + (1.0 - beta_one) * head_grad
    new_second = beta_two * moment_second + (1.0 - beta_two) * head_grad * head_grad
    return (row_loss, new_first, new_second, new_weights)


def solution(mesh):
    placed = (
        P(("blk", "group"), None),
        P(("blk", "group"), None),
        P(("blk", "group"), None),
        P(),
        P(),
        P("group", None),
        P("group", None),
    )
    return jax.shard_map(
        per_device,
        mesh=mesh,
        in_specs=placed,
        out_specs=(P(("blk", "group")), P("group", None), P("group", None), P()),
        check_vma=False,
    )
```

```python
import functools

import jax
import jax.numpy as jnp
from jax import lax
from jax.experimental import pallas as pl
from jax.experimental.pallas import tpu as pltpu
from jax.sharding import PartitionSpec as P


student_scale = 20.0
student_bias = -1.0
teacher_scale = 25.0
teacher_bias = -1.5
label_mix = 0.5
norm_eps = 1e-06
beta_one = 0.9
beta_two = 0.95
learn_rate = 0.01
weight_decay = 0.0001
adam_eps = 1e-08
adam_step = 100.0

AXES = ("blk", "group")


def device(X, y, core, z):
    return (y * 4 + X % 2 * 2 + core) * 32 + X // 2 * 16 + z


def x_line(y, core, z):
    return [device(X, y, core, z) for X in range(4)]


def y_line(X, core, z):
    return [device(X, y, core, z) for y in range(4)]


def lines(along_x):
    groups = []
    for core in range(2):
        line = x_line if (core == 0) == along_x else y_line
        groups += [line(i, core, z) for z in range(16) for i in range(4)]
    return groups


FIRST = lines(True)
SECOND = lines(False)
PLANE = [
    [device(X, y, core, z) for X in range(4) for y in range(4)]
    for core in range(2)
    for z in range(16)
]
COLUMN = [
    [device(X, y, core, z) for z in range(16)]
    for X in range(4)
    for y in range(4)
    for core in range(2)
]
TWIN = [(i, i ^ 32) for i in range(512)]


def hop(step):
    pairs = []
    for i in range(512):
        blk, group = divmod(i, 32)
        y, xh, core = blk // 4, blk // 2 % 2, blk % 2
        xl, z = divmod(group, 16)
        x = xh * 2 + xl
        if core == 0:
            y = (y + step) % 4
        else:
            x = (x + step) % 4
        pairs.append((i, device(x % 2 * 2 + x // 2, y, core, z)))
    return pairs


FORTH = hop(1)
BACK = hop(-1)


def exchange(pieces, groups):
    return lax.all_to_all(pieces, AXES, 0, 0, axis_index_groups=groups, tiled=True)


def share(block, groups):
    return exchange(jnp.broadcast_to(block[None], (len(groups[0]), *block.shape)), groups)


def from_twin(shard):
    return lax.ppermute(shard, AXES, TWIN)


def unit_rows(values):
    values = values.astype(jnp.float32)
    return values * lax.rsqrt(jnp.sum(values * values, axis=-1, keepdims=True) + norm_eps)


def copies_kernel(texts_ref, features_ref, out_ref, texts, packed, sems):
    width = texts_ref.shape[1]
    take_texts = pltpu.make_async_copy(texts_ref, texts, sems.at[0])
    take_features = pltpu.make_async_copy(features_ref, packed.at[:, width:], sems.at[1])
    take_texts.start()
    take_features.start()
    take_texts.wait()
    packed[:, :width] = unit_rows(texts[...]).astype(jnp.bfloat16)
    take_features.wait()
    puts = [
        pltpu.make_async_copy(packed, out_ref.at[i], sems.at[2 + i])
        for i in range(out_ref.shape[0])
    ]
    for put in puts:
        put.start()
    for put in puts:
        put.wait()


def unit_copies(values, others, count):
    rows, width = values.shape[0], values.shape[1] + others.shape[1]
    return pl.pallas_call(
        copies_kernel,
        out_shape=jax.ShapeDtypeStruct((count, rows, width), jnp.bfloat16),
        in_specs=[pl.BlockSpec(memory_space=pl.ANY)] * 2,
        out_specs=pl.BlockSpec(memory_space=pl.ANY),
        scratch_shapes=[
            pltpu.VMEM(values.shape, jnp.bfloat16),
            pltpu.VMEM((rows, width), jnp.bfloat16),
            pltpu.SemaphoreType.DMA((2 + count,)),
        ],
        compiler_params=pltpu.CompilerParams(vmem_limit_bytes=8 << 20),
        cost_estimate=pl.CostEstimate(
            flops=4 * values.size, bytes_accessed=2 * (count + 1) * rows * width, transcendentals=0
        ),
    )(values, others)


def last_kernel(core_ref, half_ref, twin_ref, first_ref, second_ref, *outs):
    weights_ref, new_first_ref, new_second_ref = outs

    def put(left, right):
        weights_ref[:, :384] = left[:1152, :]
        weights_ref[:, 384:] = right[:1152, :]
        for side, ref in enumerate((left, right)):
            columns = slice(side * 384, side * 384 + 384)
            high, middle, low = (
                ref[1152 + i * 48 : 1200 + i * 48, :].astype(jnp.float32) for i in range(3)
            )
            grad = ((high + middle) + low)[:36]
            new_first_ref[:, columns] = beta_one * first_ref[:, columns] + (1.0 - beta_one) * grad
            new_second_ref[:, columns] = (
                beta_two * second_ref[:, columns] + (1.0 - beta_two) * grad * grad
            )

    @pl.when(core_ref[0] == 0)
    def _():
        put(half_ref, twin_ref)

    @pl.when(core_ref[0] != 0)
    def _():
        put(twin_ref, half_ref)


def last_outputs(core, half, twin_half, moment_first, moment_second):
    whole = pl.BlockSpec(memory_space=pltpu.VMEM)
    moment = jax.ShapeDtypeStruct(moment_first.shape, jnp.float32)
    return pl.pallas_call(
        last_kernel,
        out_shape=(jax.ShapeDtypeStruct((1152, 768), jnp.bfloat16), moment, moment),
        in_specs=[pl.BlockSpec(memory_space=pltpu.SMEM)] + [whole] * 4,
        out_specs=(whole,) * 3,
        compiler_params=pltpu.CompilerParams(vmem_limit_bytes=12 << 20),
        cost_estimate=pl.CostEstimate(flops=0, bytes_accessed=6 << 20, transcendentals=0),
    )(core.reshape(1), half, twin_half, moment_first, moment_second)


def pair_terms(student_rows, teacher_rows, left_ids, text_rows, right_ids):
    dims = (((1,), (1,)), ((), ()))
    student_logit = (
        student_scale
        * lax.dot_general(student_rows, text_rows, dims, preferred_element_type=jnp.float32)
        + student_bias
    )
    teacher_logit = (
        teacher_scale
        * lax.dot_general(teacher_rows, text_rows, dims, preferred_element_type=jnp.float32)
        + teacher_bias
    )
    labels = (left_ids == right_ids).astype(jnp.float32)
    target = (1.0 - label_mix) * labels + label_mix * jax.nn.sigmoid(teacher_logit)
    tail = jnp.exp(-jnp.abs(student_logit))
    softplus = jnp.maximum(student_logit, 0.0) + jnp.log1p(tail)
    chance = jnp.where(student_logit >= 0.0, 1.0, tail) / (1.0 + tail)
    losses = jnp.sum(softplus - target * student_logit, axis=1, keepdims=True)
    return losses, (chance - target).astype(jnp.bfloat16)


def pair_kernel(parts, carried, *refs):
    student_ref, teacher_ref, left_ref = refs[:3]
    chunks, ids = refs[3 : 3 + parts], refs[3 + parts : 3 + 2 * parts]
    rest = refs[3 + 2 * parts :]
    pulled_ref, losses_ref = rest[-2:]
    if carried:
        pulled_ref[...] = rest[0][...]
        losses_ref[...] = rest[1][...]
    else:
        pulled_ref[...] = jnp.zeros_like(pulled_ref)
        losses_ref[...] = jnp.zeros_like(losses_ref)
    for chunk_ref, ids_ref in zip(chunks, ids):
        texts = chunk_ref[...]
        losses, coeff = pair_terms(
            student_ref[...], teacher_ref[...], left_ref[...], texts, ids_ref[...]
        )
        losses_ref[...] += losses
        pulled_ref[...] += jnp.dot(coeff, texts, preferred_element_type=jnp.float32)


def pair_sums(student_rows, teacher_rows, left_ids, chunks, carried=()):
    rows, width = student_rows.shape
    texts = [chunk for chunk, _ in chunks]
    ids = [ids.reshape(1, -1) for _, ids in chunks]
    count = sum(chunk.shape[0] for chunk in texts)
    operands = (student_rows, teacher_rows, left_ids, *texts, *ids, *carried)
    whole = pl.BlockSpec(memory_space=pltpu.VMEM)
    return pl.pallas_call(
        functools.partial(pair_kernel, len(texts), bool(carried)),
        out_shape=(
            jax.ShapeDtypeStruct((rows, width), jnp.float32),
            jax.ShapeDtypeStruct((rows, 1), jnp.float32),
        ),
        in_specs=[whole] * len(operands),
        out_specs=(whole, whole),
        compiler_params=pltpu.CompilerParams(vmem_limit_bytes=20 << 20),
        cost_estimate=pl.CostEstimate(
            flops=6 * rows * count * width,
            bytes_accessed=2 * count * width,
            transcendentals=4 * rows * count,
        ),
    )(*operands)


def row_order(core):
    place = lax.iota(jnp.int32, 1280)
    first, second = place // 320, place // 80 % 4
    X = jnp.where(core == 0, first, second)
    y = jnp.where(core == 0, second, first)
    row = (X % 2 * 4 + y) * 5 + place % 5
    return jnp.where(row < 36, X // 2 * 576 + place // 5 % 16 * 36 + row, -1)


def weight_order():
    row = lax.iota(jnp.int32, 576)
    q = row % 36
    return q // 5 * 96 + row // 36 * 5 + q % 5


def grad_order():
    part = lax.iota(jnp.int32, 144)
    q = part % 48
    return jnp.where(q < 40, q // 5 * 96 + 80 + part // 48 * 5 + q % 5, -1)


def one_hot(index, width):
    return (index[:, None] == lax.iota(jnp.int32, width)[None, :]).astype(jnp.bfloat16)


def rounded(values):
    return lax.reduce_precision(values, 8, 7)


def per_device(
    student_features,
    teacher_image,
    text_embeds,
    pair_ids,
    head_weights,
    moment_first,
    moment_second,
):
    rows = student_features.shape[0]
    blk_index = lax.axis_index("blk")
    group_index = lax.axis_index("group")
    y, xh, core = blk_index // 4, blk_index // 2 % 2, blk_index % 2
    xl, z = group_index // 16, group_index % 16

    copies, teacher_image, twin_features = lax.optimization_barrier(
        (unit_copies(text_embeds, student_features, 4), teacher_image, student_features)
    )
    near = exchange(copies, FIRST)
    top = near[:2, :, :1152].reshape(2 * rows, 1152)
    bottom = near[2:, :, :1152].reshape(2 * rows, 1152)
    features = near[:, :, 1152:]
    before_top = lax.ppermute(top, AXES, FORTH)
    after_bottom = lax.ppermute(bottom, AXES, BACK)
    before_bottom = lax.ppermute(bottom, AXES, FORTH)
    after_top = lax.ppermute(top, AXES, BACK)
    far_top = lax.ppermute(before_top, AXES, FORTH)
    far_bottom = lax.ppermute(after_bottom, AXES, BACK)

    far_features, far_teacher = from_twin(twin_features), from_twin(teacher_image)
    both_features = jnp.concatenate([student_features, far_features], axis=0)
    both_teacher = jnp.concatenate([teacher_image, far_teacher], axis=0)
    projected = lax.dot_general(
        both_features, head_weights, (((1,), (1,)), ((), ())), preferred_element_type=jnp.float32
    )
    inverse = lax.rsqrt(jnp.sum(projected * projected, axis=-1, keepdims=True) + norm_eps)
    student = projected * inverse
    student_b = student.astype(jnp.bfloat16)
    teacher_b = unit_rows(both_teacher).astype(jnp.bfloat16)

    ids_grid = pair_ids.reshape(4, 2, 2, 2, 16, rows)
    ids_plane = lax.dynamic_index_in_dim(ids_grid, z, 4, keepdims=False)
    ids_core = lax.dynamic_index_in_dim(ids_plane, core, 2, keepdims=False)
    ids_yx = ids_core.transpose(0, 2, 1, 3).reshape(4, 4, rows)
    ids_xy = ids_core.transpose(1, 2, 0, 3).reshape(4, 4, rows)
    text_ids = jnp.where(core == 0, ids_yx, ids_xy)
    place = jnp.where(core == 0, y, xh * 2 + xl)

    def ids_at(step):
        return lax.dynamic_index_in_dim(text_ids, (place + step) % 4, 0, keepdims=False)

    ids_rows = pair_ids.reshape(512, rows)
    left_ids = jnp.concatenate(
        [
            lax.dynamic_index_in_dim(ids_rows, blk_index * 32 + group_index, 0, keepdims=False),
            lax.dynamic_index_in_dim(ids_rows, (blk_index ^ 1) * 32 + group_index, 0, keepdims=False),
        ]
    )
    images = (student_b, teacher_b, left_ids.reshape(-1, 1))
    own_chunks = [(top, ids_at(0)[:2]), (bottom, ids_at(0)[2:])]
    sums = pair_sums(*images, own_chunks)
    near_chunks = [
        (before_top, ids_at(3)[:2]),
        (after_bottom, ids_at(1)[2:]),
        (before_bottom, ids_at(3)[2:]),
        (after_top, ids_at(1)[:2]),
    ]
    sums = pair_sums(*images, near_chunks, sums)
    features, sums = lax.optimization_barrier((features, sums))
    pulled, losses = pair_sums(
        *images, [(far_top, ids_at(2)[:2]), (far_bottom, ids_at(2)[2:])], sums
    )
    losses = losses.reshape(-1)

    def piece(values, start):
        group_rows = lax.dynamic_slice_in_dim(values, start, 36, 0)
        padded = jnp.pad(group_rows, ((0, 4), (0, 0)))
        return lax.dynamic_slice(padded, ((xh * 4 + y) * 5, core * 384), (5, 384))

    own_moments = (
        piece(moment_first, 0),
        piece(moment_second, 0),
        piece(head_weights, group_index * 36),
    )
    order = row_order(core)
    own_losses = losses[:rows]
    other_losses = jnp.pad(losses[rows:].reshape(1, rows), ((0, 7), (0, 256)))

    pulled = pulled[:rows] + from_twin(pulled[rows:])
    student, inverse = student[:rows], inverse[:rows]
    grad_student = student_scale / rows * pulled
    grad_projected = (
        inverse * (grad_student - student * jnp.sum(student * grad_student, axis=-1, keepdims=True))
    ).astype(jnp.bfloat16)

    grad_rows = lax.dot_general(
        one_hot(order, 1152),
        grad_projected,
        (((1,), (1,)), ((), ())),
        preferred_element_type=jnp.float32,
    ).astype(jnp.bfloat16)
    grad_rows, own_moments, own_losses, other_losses = lax.optimization_barrier(
        (grad_rows, own_moments, own_losses, other_losses)
    )
    grad_rows = exchange(grad_rows.reshape(4, 320, rows), FIRST)
    line_grad = lax.dot_general(
        grad_rows, features, (((0, 2), (0, 1)), ((), ())), preferred_element_type=jnp.float32
    )
    core_grad = jnp.sum(exchange(line_grad.reshape(4, 80, 768), SECOND), axis=0)
    left, right = core_grad[:, :384], core_grad[:, 384:]
    arrived = from_twin(jnp.concatenate([jnp.where(core == 0, right, left), other_losses], axis=0))
    chip_grad = jnp.where(core == 0, left, right) + arrived[:80]
    row_loss = (own_losses + arrived[80, :rows]) / rows

    column_grad = jnp.pad(chip_grad.reshape(16, 15, 128), ((0, 0), (0, 1), (0, 0)))
    own_grad = jnp.sum(exchange(column_grad, COLUMN), axis=0)[:15].reshape(5, 384)

    def adam(head_grad, first, second, weights):
        new_first = beta_one * first + (1.0 - beta_one) * head_grad
        new_second = beta_two * second + (1.0 - beta_two) * head_grad * head_grad
        first_hat = new_first / (1.0 - beta_one**adam_step)
        second_hat = new_second / (1.0 - beta_two**adam_step)
        weights = weights.astype(jnp.float32)
        updated = weights - learn_rate * (
            first_hat / (jnp.sqrt(second_hat) + adam_eps) + weight_decay * weights
        )
        return updated.astype(jnp.bfloat16)

    own_weights = adam(own_grad, *own_moments)
    chip_weights = share(own_weights, COLUMN).reshape(80, 384)
    high = rounded(own_grad)
    middle = rounded(own_grad - high)
    low = own_grad - high - middle
    spare = jnp.zeros((1, 384), jnp.float32)
    grad_parts = jnp.concatenate([high, middle, low, spare], axis=0).astype(jnp.bfloat16)
    plane = share(jnp.concatenate([chip_weights, grad_parts], axis=0), PLANE).reshape(2, 768, 384)
    plane, same_xl = lax.optimization_barrier((plane, xl))
    after = same_xl - xl
    select_weights = one_hot(weight_order() + after, 768)
    halves = [
        jnp.dot(select_weights, plane[i], preferred_element_type=jnp.float32) for i in range(2)
    ]
    group_parts = jnp.dot(
        one_hot(grad_order() + after, 768),
        lax.dynamic_index_in_dim(plane, xl, 0, keepdims=False),
        preferred_element_type=jnp.float32,
    )
    half = jnp.concatenate([*halves, group_parts], axis=0).astype(jnp.bfloat16)
    new_weights, new_first, new_second = last_outputs(
        core, half, from_twin(half), moment_first, moment_second
    )
    return (row_loss, new_first, new_second, new_weights)


def solution(mesh):
    placed = (
        P(("blk", "group"), None),
        P(("blk", "group"), None),
        P(("blk", "group"), None),
        P(),
        P(),
        P("group", None),
        P("group", None),
    )
    return jax.shard_map(
        per_device,
        mesh=mesh,
        in_specs=placed,
        out_specs=(P(("blk", "group")), P("group", None), P("group", None), P()),
        check_vma=False,
    )
```

```python
import functools

import jax
import jax.numpy as jnp
from jax import lax
from jax.experimental import pallas as pl
from jax.experimental.pallas import tpu as pltpu
from jax.sharding import PartitionSpec as P


student_scale = 20.0
student_bias = -1.0
teacher_scale = 25.0
teacher_bias = -1.5
label_mix = 0.5
norm_eps = 1e-06
beta_one = 0.9
beta_two = 0.95
learn_rate = 0.01
weight_decay = 0.0001
adam_eps = 1e-08
adam_step = 100.0

AXES = ("blk", "group")


def device(X, y, core, z):
    return (y * 4 + X % 2 * 2 + core) * 32 + X // 2 * 16 + z


def x_line(y, core, z):
    return [device(X, y, core, z) for X in range(4)]


def y_line(X, core, z):
    return [device(X, y, core, z) for y in range(4)]


def lines(along_x):
    groups = []
    for core in range(2):
        line = x_line if (core == 0) == along_x else y_line
        groups += [line(i, core, z) for z in range(16) for i in range(4)]
    return groups


FIRST = lines(True)
SECOND = lines(False)
PLANE = [
    [device(X, y, core, z) for X in range(4) for y in range(4)]
    for core in range(2)
    for z in range(16)
]
COLUMN = [
    [device(X, y, core, z) for z in range(16)]
    for X in range(4)
    for y in range(4)
    for core in range(2)
]
TWIN = [(i, i ^ 32) for i in range(512)]


def hop(step):
    pairs = []
    for i in range(512):
        blk, group = divmod(i, 32)
        y, xh, core = blk // 4, blk // 2 % 2, blk % 2
        xl, z = divmod(group, 16)
        x = xh * 2 + xl
        if core == 0:
            y = (y + step) % 4
        else:
            x = (x + step) % 4
        pairs.append((i, device(x % 2 * 2 + x // 2, y, core, z)))
    return pairs


FORTH = hop(1)
BACK = hop(-1)


def exchange(pieces, groups):
    return lax.all_to_all(pieces, AXES, 0, 0, axis_index_groups=groups, tiled=True)


def share(block, groups):
    return exchange(jnp.broadcast_to(block[None], (len(groups[0]), *block.shape)), groups)


def from_twin(shard):
    return lax.ppermute(shard, AXES, TWIN)


def unit_rows(values):
    values = values.astype(jnp.float32)
    return values * lax.rsqrt(jnp.sum(values * values, axis=-1, keepdims=True) + norm_eps)


def copies_kernel(texts_ref, features_ref, out_ref, texts, packed, sems):
    width = texts_ref.shape[1]
    take_texts = pltpu.make_async_copy(texts_ref, texts, sems.at[0])
    take_features = pltpu.make_async_copy(features_ref, packed.at[:, width:], sems.at[1])
    take_texts.start()
    take_features.start()
    take_texts.wait()
    packed[:, :width] = unit_rows(texts[...]).astype(jnp.bfloat16)
    take_features.wait()
    puts = [
        pltpu.make_async_copy(packed, out_ref.at[i], sems.at[2 + i])
        for i in range(out_ref.shape[0])
    ]
    for put in puts:
        put.start()
    for put in puts:
        put.wait()


def unit_copies(values, others, count):
    rows, width = values.shape[0], values.shape[1] + others.shape[1]
    return pl.pallas_call(
        copies_kernel,
        out_shape=jax.ShapeDtypeStruct((count, rows, width), jnp.bfloat16),
        in_specs=[pl.BlockSpec(memory_space=pltpu.HBM)] * 2,
        out_specs=pl.BlockSpec(memory_space=pltpu.HBM),
        scratch_shapes=[
            pltpu.VMEM(values.shape, jnp.bfloat16),
            pltpu.VMEM((rows, width), jnp.bfloat16),
            pltpu.SemaphoreType.DMA((2 + count,)),
        ],
        compiler_params=pltpu.CompilerParams(vmem_limit_bytes=60 << 20),
        cost_estimate=pl.CostEstimate(
            flops=4 * values.size, bytes_accessed=2 * (count + 1) * rows * width, transcendentals=0
        ),
    )(values, others)


def last_kernel(core_ref, half_ref, twin_ref, first_ref, second_ref, *outs):
    weights_ref, new_first_ref, new_second_ref = outs

    def put(left, right):
        weights_ref[:, :384] = left[:1152, :]
        weights_ref[:, 384:] = right[:1152, :]
        for side, ref in enumerate((left, right)):
            columns = slice(side * 384, side * 384 + 384)
            high, middle, low = (
                ref[1152 + i * 48 : 1200 + i * 48, :].astype(jnp.float32) for i in range(3)
            )
            grad = ((high + middle) + low)[:36]
            new_first_ref[:, columns] = beta_one * first_ref[:, columns] + (1.0 - beta_one) * grad
            new_second_ref[:, columns] = (
                beta_two * second_ref[:, columns] + (1.0 - beta_two) * grad * grad
            )

    @pl.when(core_ref[0] == 0)
    def _():
        put(half_ref, twin_ref)

    @pl.when(core_ref[0] != 0)
    def _():
        put(twin_ref, half_ref)


def last_outputs(core, half, twin_half, moment_first, moment_second):
    whole = pl.BlockSpec(memory_space=pltpu.VMEM)
    moment = jax.ShapeDtypeStruct(moment_first.shape, jnp.float32)
    return pl.pallas_call(
        last_kernel,
        out_shape=(jax.ShapeDtypeStruct((1152, 768), jnp.bfloat16), moment, moment),
        in_specs=[pl.BlockSpec(memory_space=pltpu.SMEM)] + [whole] * 4,
        out_specs=(whole,) * 3,
        compiler_params=pltpu.CompilerParams(vmem_limit_bytes=12 << 20),
        cost_estimate=pl.CostEstimate(flops=0, bytes_accessed=6 << 20, transcendentals=0),
    )(core.reshape(1), half, twin_half, moment_first, moment_second)


def pair_terms(student_rows, teacher_rows, left_ids, text_rows, right_ids):
    dims = (((1,), (1,)), ((), ()))
    student_logit = (
        student_scale
        * lax.dot_general(student_rows, text_rows, dims, preferred_element_type=jnp.float32)
        + student_bias
    )
    teacher_logit = (
        teacher_scale
        * lax.dot_general(teacher_rows, text_rows, dims, preferred_element_type=jnp.float32)
        + teacher_bias
    )
    labels = (left_ids == right_ids).astype(jnp.float32)
    target = (1.0 - label_mix) * labels + label_mix * jax.nn.sigmoid(teacher_logit)
    tail = jnp.exp(-jnp.abs(student_logit))
    softplus = jnp.maximum(student_logit, 0.0) + jnp.log1p(tail)
    chance = jnp.where(student_logit >= 0.0, 1.0, tail) / (1.0 + tail)
    losses = jnp.sum(softplus - target * student_logit, axis=1, keepdims=True)
    return losses, (chance - target).astype(jnp.bfloat16)


def pair_kernel(parts, carried, last, *refs):
    student_ref, teacher_ref, left_ref = refs[:3]
    chunks, ids = refs[3 : 3 + parts], refs[3 + parts : 3 + 2 * parts]
    rest = refs[3 + 2 * parts :]
    pulled_ref, losses_ref = rest[-2:]
    if last:
        own_ref, twin_ref, losses_ref, pulled_ref = rest[-4:]
    if carried:
        pulled_ref[...] = rest[0][...]
        losses_ref[...] = rest[1][...]
    else:
        pulled_ref[...] = jnp.zeros_like(pulled_ref)
        losses_ref[...] = jnp.zeros_like(losses_ref)
    for chunk_ref, ids_ref in zip(chunks, ids):
        texts = chunk_ref[...]
        losses, coeff = pair_terms(
            student_ref[...], teacher_ref[...], left_ref[...], texts, ids_ref[...]
        )
        losses_ref[...] += losses
        pulled_ref[...] += jnp.dot(coeff, texts, preferred_element_type=jnp.float32)
    if last:
        half = pulled_ref.shape[0] // 2
        own_ref[...] = pulled_ref[:half]
        twin_ref[...] = pulled_ref[half:]


def pair_sums(student_rows, teacher_rows, left_ids, chunks, carried=(), last=False):
    rows, width = student_rows.shape
    texts = [chunk for chunk, _ in chunks]
    ids = [ids.reshape(1, -1) for _, ids in chunks]
    count = sum(chunk.shape[0] for chunk in texts)
    operands = (student_rows, teacher_rows, left_ids, *texts, *ids, *carried)
    whole = pl.BlockSpec(memory_space=pltpu.VMEM)
    parts = 1 + last
    sums = (jax.ShapeDtypeStruct((rows // parts, width), jnp.float32),) * parts
    return pl.pallas_call(
        functools.partial(pair_kernel, len(texts), bool(carried), last),
        out_shape=(*sums, jax.ShapeDtypeStruct((rows, 1), jnp.float32)),
        in_specs=[whole] * len(operands),
        out_specs=(whole,) * (len(sums) + 1),
        scratch_shapes=[pltpu.VMEM((rows, width), jnp.float32)] * last,
        compiler_params=pltpu.CompilerParams(vmem_limit_bytes=20 << 20),
        cost_estimate=pl.CostEstimate(
            flops=6 * rows * count * width,
            bytes_accessed=2 * count * width,
            transcendentals=4 * rows * count,
        ),
    )(*operands)


def row_order(core):
    place = lax.iota(jnp.int32, 1280)
    first, second = place // 320, place // 80 % 4
    X = jnp.where(core == 0, first, second)
    y = jnp.where(core == 0, second, first)
    row = (X % 2 * 4 + y) * 5 + place % 5
    return jnp.where(row < 36, X // 2 * 576 + place // 5 % 16 * 36 + row, -1)


def weight_order():
    row = lax.iota(jnp.int32, 576)
    q = row % 36
    return q // 5 * 96 + row // 36 * 5 + q % 5


def grad_order():
    part = lax.iota(jnp.int32, 144)
    q = part % 48
    return jnp.where(q < 40, q // 5 * 96 + 80 + part // 48 * 5 + q % 5, -1)


def one_hot(index, width):
    return (index[:, None] == lax.iota(jnp.int32, width)[None, :]).astype(jnp.bfloat16)


def rounded(values):
    return lax.reduce_precision(values, 8, 7)


def per_device(
    student_features,
    teacher_image,
    text_embeds,
    pair_ids,
    head_weights,
    moment_first,
    moment_second,
):
    rows = student_features.shape[0]
    blk_index = lax.axis_index("blk")
    group_index = lax.axis_index("group")
    y, xh, core = blk_index // 4, blk_index // 2 % 2, blk_index % 2
    xl, z = group_index // 16, group_index % 16

    copies, teacher_image, twin_features = lax.optimization_barrier(
        (unit_copies(text_embeds, student_features, 4), teacher_image, student_features)
    )
    near = exchange(copies, FIRST)
    top = near[:2, :, :1152].reshape(2 * rows, 1152)
    bottom = near[2:, :, :1152].reshape(2 * rows, 1152)
    features = near[:, :, 1152:]
    before_top = lax.ppermute(top, AXES, FORTH)
    after_bottom = lax.ppermute(bottom, AXES, BACK)
    before_bottom = lax.ppermute(bottom, AXES, FORTH)
    after_top = lax.ppermute(top, AXES, BACK)
    far_top = lax.ppermute(before_top, AXES, FORTH)
    far_bottom = lax.ppermute(after_bottom, AXES, BACK)

    far_features, far_teacher = from_twin(twin_features), from_twin(teacher_image)
    both_features = jnp.concatenate([student_features, far_features], axis=0)
    both_teacher = jnp.concatenate([teacher_image, far_teacher], axis=0)
    projected = lax.dot_general(
        both_features, head_weights, (((1,), (1,)), ((), ())), preferred_element_type=jnp.float32
    )
    inverse = lax.rsqrt(jnp.sum(projected * projected, axis=-1, keepdims=True) + norm_eps)
    student = projected * inverse
    student_b = student.astype(jnp.bfloat16)
    teacher_b = unit_rows(both_teacher).astype(jnp.bfloat16)

    ids_grid = pair_ids.reshape(4, 2, 2, 2, 16, rows)
    ids_plane = lax.dynamic_index_in_dim(ids_grid, z, 4, keepdims=False)
    ids_core = lax.dynamic_index_in_dim(ids_plane, core, 2, keepdims=False)
    ids_yx = ids_core.transpose(0, 2, 1, 3).reshape(4, 4, rows)
    ids_xy = ids_core.transpose(1, 2, 0, 3).reshape(4, 4, rows)
    text_ids = jnp.where(core == 0, ids_yx, ids_xy)
    place = jnp.where(core == 0, y, xh * 2 + xl)

    def ids_at(step):
        return lax.dynamic_index_in_dim(text_ids, (place + step) % 4, 0, keepdims=False)

    ids_rows = pair_ids.reshape(512, rows)
    left_ids = jnp.concatenate(
        [
            lax.dynamic_index_in_dim(ids_rows, blk_index * 32 + group_index, 0, keepdims=False),
            lax.dynamic_index_in_dim(ids_rows, (blk_index ^ 1) * 32 + group_index, 0, keepdims=False),
        ]
    )
    images = (student_b, teacher_b, left_ids.reshape(-1, 1))
    own_chunks = [(top, ids_at(0)[:2]), (bottom, ids_at(0)[2:])]
    sums = pair_sums(*images, own_chunks)
    near_chunks = [
        (before_top, ids_at(3)[:2]),
        (after_bottom, ids_at(1)[2:]),
        (before_bottom, ids_at(3)[2:]),
        (after_top, ids_at(1)[:2]),
    ]
    sums = pair_sums(*images, near_chunks, sums)
    features, sums = lax.optimization_barrier((features, sums))
    far_chunks = [(far_top, ids_at(2)[:2]), (far_bottom, ids_at(2)[2:])]
    pulled, twin_pulled, losses = pair_sums(*images, far_chunks, sums, last=True)
    losses = losses.reshape(-1)

    pulled = pulled + from_twin(twin_pulled)
    student, inverse = student[:rows], inverse[:rows]
    grad_student = student_scale / rows * pulled
    grad_projected = (
        inverse * (grad_student - student * jnp.sum(student * grad_student, axis=-1, keepdims=True))
    ).astype(jnp.bfloat16)

    grad_rows = lax.dot_general(
        one_hot(row_order(core), 1152),
        grad_projected,
        (((1,), (1,)), ((), ())),
        preferred_element_type=jnp.float32,
    ).astype(jnp.bfloat16)
    grad_rows = exchange(grad_rows.reshape(4, 320, rows), FIRST)
    line_grad = lax.dot_general(
        grad_rows, features, (((0, 2), (0, 1)), ((), ())), preferred_element_type=jnp.float32
    )
    core_grad = jnp.sum(exchange(line_grad.reshape(4, 80, 768), SECOND), axis=0)
    left, right = core_grad[:, :384], core_grad[:, 384:]
    other_losses = jnp.pad(losses[rows:].reshape(1, rows), ((0, 7), (0, 256)))
    arrived = from_twin(jnp.concatenate([jnp.where(core == 0, right, left), other_losses], axis=0))
    chip_grad = jnp.where(core == 0, left, right) + arrived[:80]
    row_loss = (losses[:rows] + arrived[80, :rows]) / rows

    column_grad = jnp.pad(chip_grad.reshape(16, 15, 128), ((0, 0), (0, 1), (0, 0)))
    own_grad = jnp.sum(exchange(column_grad, COLUMN), axis=0)[:15].reshape(5, 384)

    def adam(head_grad, first, second, weights):
        new_first = beta_one * first + (1.0 - beta_one) * head_grad
        new_second = beta_two * second + (1.0 - beta_two) * head_grad * head_grad
        first_hat = new_first / (1.0 - beta_one**adam_step)
        second_hat = new_second / (1.0 - beta_two**adam_step)
        weights = weights.astype(jnp.float32)
        updated = weights - learn_rate * (
            first_hat / (jnp.sqrt(second_hat) + adam_eps) + weight_decay * weights
        )
        return updated.astype(jnp.bfloat16)

    def piece(values, start):
        group_rows = lax.dynamic_slice_in_dim(values, start, 36, 0)
        padded = jnp.pad(group_rows, ((0, 4), (0, 0)))
        return lax.dynamic_slice(padded, ((xh * 4 + y) * 5, core * 384), (5, 384))

    own_weights = adam(
        own_grad,
        piece(moment_first, 0),
        piece(moment_second, 0),
        piece(head_weights, group_index * 36),
    )
    chip_weights = share(own_weights, COLUMN).reshape(80, 384)
    high = rounded(own_grad)
    middle = rounded(own_grad - high)
    low = own_grad - high - middle
    spare = jnp.zeros((1, 384), jnp.float32)
    grad_parts = jnp.concatenate([high, middle, low, spare], axis=0).astype(jnp.bfloat16)
    plane = share(jnp.concatenate([chip_weights, grad_parts], axis=0), PLANE).reshape(2, 768, 384)
    select_weights = one_hot(weight_order(), 768)
    halves = [
        jnp.dot(select_weights, plane[i], preferred_element_type=jnp.float32) for i in range(2)
    ]
    group_parts = jnp.dot(
        one_hot(grad_order(), 768),
        lax.dynamic_index_in_dim(plane, xl, 0, keepdims=False),
        preferred_element_type=jnp.float32,
    )
    half = jnp.concatenate([*halves, group_parts], axis=0).astype(jnp.bfloat16)
    new_weights, new_first, new_second = last_outputs(
        core, half, from_twin(half), moment_first, moment_second
    )
    return (row_loss, new_first, new_second, new_weights)


def solution(mesh):
    placed = (
        P(("blk", "group"), None),
        P(("blk", "group"), None),
        P(("blk", "group"), None),
        P(),
        P(),
        P("group", None),
        P("group", None),
    )
    return jax.shard_map(
        per_device,
        mesh=mesh,
        in_specs=placed,
        out_specs=(P(("blk", "group")), P("group", None), P("group", None), P()),
        check_vma=False,
    )
```

```python
import functools

import jax
import jax.numpy as jnp
from jax import lax
from jax.experimental import pallas as pl
from jax.experimental.pallas import tpu as pltpu
from jax.sharding import PartitionSpec as P


student_scale = 20.0
student_bias = -1.0
teacher_scale = 25.0
teacher_bias = -1.5
label_mix = 0.5
norm_eps = 1e-06
beta_one = 0.9
beta_two = 0.95
learn_rate = 0.01
weight_decay = 0.0001
adam_eps = 1e-08
adam_step = 100.0

AXES = ("blk", "group")


def device(X, y, core, z):
    return (y * 4 + X % 2 * 2 + core) * 32 + X // 2 * 16 + z


def x_line(y, core, z):
    return [device(X, y, core, z) for X in range(4)]


def y_line(X, core, z):
    return [device(X, y, core, z) for y in range(4)]


def lines(along_x):
    groups = []
    for core in range(2):
        line = x_line if (core == 0) == along_x else y_line
        groups += [line(i, core, z) for z in range(16) for i in range(4)]
    return groups


FIRST = lines(True)
SECOND = lines(False)
PLANE = [
    [device(X, y, core, z) for X in range(4) for y in range(4)]
    for core in range(2)
    for z in range(16)
]
COLUMN = [
    [device(X, y, core, z) for z in range(16)]
    for X in range(4)
    for y in range(4)
    for core in range(2)
]
TWIN = [(i, i ^ 32) for i in range(512)]


def hop(step):
    pairs = []
    for i in range(512):
        blk, group = divmod(i, 32)
        y, xh, core = blk // 4, blk // 2 % 2, blk % 2
        xl, z = divmod(group, 16)
        x = xh * 2 + xl
        if core == 0:
            y = (y + step) % 4
        else:
            x = (x + step) % 4
        pairs.append((i, device(x % 2 * 2 + x // 2, y, core, z)))
    return pairs


FORTH = hop(1)
BACK = hop(-1)


def exchange(pieces, groups):
    return lax.all_to_all(pieces, AXES, 0, 0, axis_index_groups=groups, tiled=True)


def share(block, groups):
    return exchange(jnp.broadcast_to(block[None], (len(groups[0]), *block.shape)), groups)


def from_twin(shard):
    return lax.ppermute(shard, AXES, TWIN)


def unit_rows(values):
    values = values.astype(jnp.float32)
    return values * lax.rsqrt(jnp.sum(values * values, axis=-1, keepdims=True) + norm_eps)


def head_kernel(texts_ref, features_ref, teacher_ref, out_ref, unit_ref, texts, teacher, packed, unit, sems):
    width = texts_ref.shape[1]
    take_texts = pltpu.make_async_copy(texts_ref, texts, sems.at[0])
    take_features = pltpu.make_async_copy(features_ref, packed.at[:, width:], sems.at[1])
    take_teacher = pltpu.make_async_copy(teacher_ref, teacher, sems.at[2])
    take_texts.start()
    take_features.start()
    take_teacher.start()
    take_texts.wait()
    packed[:, :width] = unit_rows(texts[...]).astype(jnp.bfloat16)
    take_features.wait()
    puts = [
        pltpu.make_async_copy(packed, out_ref.at[i], sems.at[3 + i])
        for i in range(out_ref.shape[0])
    ]
    for put in puts:
        put.start()
    take_teacher.wait()
    unit[...] = unit_rows(teacher[...]).astype(jnp.bfloat16)
    put_unit = pltpu.make_async_copy(unit, unit_ref, sems.at[3 + len(puts)])
    put_unit.start()
    for put in puts:
        put.wait()
    put_unit.wait()


def head(texts, features, teacher, count):
    rows, width = texts.shape[0], texts.shape[1] + features.shape[1]
    return pl.pallas_call(
        head_kernel,
        out_shape=(
            jax.ShapeDtypeStruct((count, rows, width), jnp.bfloat16),
            jax.ShapeDtypeStruct(teacher.shape, jnp.bfloat16),
        ),
        in_specs=[pl.BlockSpec(memory_space=pltpu.HBM)] * 3,
        out_specs=(pl.BlockSpec(memory_space=pltpu.HBM),) * 2,
        scratch_shapes=[
            pltpu.VMEM(texts.shape, jnp.bfloat16),
            pltpu.VMEM(teacher.shape, jnp.bfloat16),
            pltpu.VMEM((rows, width), jnp.bfloat16),
            pltpu.VMEM(teacher.shape, jnp.bfloat16),
            pltpu.SemaphoreType.DMA((4 + count,)),
        ],
        compiler_params=pltpu.CompilerParams(vmem_limit_bytes=60 << 20),
        cost_estimate=pl.CostEstimate(
            flops=8 * texts.size, bytes_accessed=2 * (count + 2) * rows * width, transcendentals=0
        ),
    )(texts, features, teacher)


def last_kernel(core_ref, half_ref, twin_ref, first_ref, second_ref, *outs):
    weights_ref, new_first_ref, new_second_ref = outs

    def put(left, right):
        weights_ref[:, :384] = left[:1152, :]
        weights_ref[:, 384:] = right[:1152, :]
        for side, ref in enumerate((left, right)):
            columns = slice(side * 384, side * 384 + 384)
            high, middle, low = (
                ref[1152 + i * 48 : 1200 + i * 48, :].astype(jnp.float32) for i in range(3)
            )
            grad = ((high + middle) + low)[:36]
            new_first_ref[:, columns] = beta_one * first_ref[:, columns] + (1.0 - beta_one) * grad
            new_second_ref[:, columns] = (
                beta_two * second_ref[:, columns] + (1.0 - beta_two) * grad * grad
            )

    @pl.when(core_ref[0] == 0)
    def _():
        put(half_ref, twin_ref)

    @pl.when(core_ref[0] != 0)
    def _():
        put(twin_ref, half_ref)


def last_outputs(core, half, twin_half, moment_first, moment_second):
    whole = pl.BlockSpec(memory_space=pltpu.VMEM)
    moment = jax.ShapeDtypeStruct(moment_first.shape, jnp.float32)
    return pl.pallas_call(
        last_kernel,
        out_shape=(jax.ShapeDtypeStruct((1152, 768), jnp.bfloat16), moment, moment),
        in_specs=[pl.BlockSpec(memory_space=pltpu.SMEM)] + [whole] * 4,
        out_specs=(whole,) * 3,
        compiler_params=pltpu.CompilerParams(vmem_limit_bytes=12 << 20),
        cost_estimate=pl.CostEstimate(flops=0, bytes_accessed=6 << 20, transcendentals=0),
    )(core.reshape(1), half, twin_half, moment_first, moment_second)


def pair_terms(student_rows, teacher_rows, left_ids, text_rows, right_ids):
    dims = (((1,), (1,)), ((), ()))
    student_logit = (
        student_scale
        * lax.dot_general(student_rows, text_rows, dims, preferred_element_type=jnp.float32)
        + student_bias
    )
    teacher_logit = (
        teacher_scale
        * lax.dot_general(teacher_rows, text_rows, dims, preferred_element_type=jnp.float32)
        + teacher_bias
    )
    labels = (left_ids == right_ids).astype(jnp.float32)
    target = (1.0 - label_mix) * labels + label_mix * jax.nn.sigmoid(teacher_logit)
    tail = jnp.exp(-jnp.abs(student_logit))
    softplus = jnp.maximum(student_logit, 0.0) + jnp.log1p(tail)
    chance = jnp.where(student_logit >= 0.0, 1.0, tail) / (1.0 + tail)
    losses = jnp.sum(softplus - target * student_logit, axis=1, keepdims=True)
    return losses, (chance - target).astype(jnp.bfloat16)


def pair_kernel(places, carried, last, *refs):
    student_ref, own_teacher_ref, twin_teacher_ref, left_ref, ids_ref = refs[:5]
    chunks, rest = refs[5 : 5 + len(places)], refs[5 + len(places) :]
    pulled_ref, losses_ref = rest[-2:]
    if last:
        own_ref, twin_ref, losses_ref, pulled_ref = rest[-4:]
    if carried:
        pulled_ref[...] = rest[0][...]
        losses_ref[...] = rest[1][...]
    else:
        pulled_ref[...] = jnp.zeros_like(pulled_ref)
        losses_ref[...] = jnp.zeros_like(losses_ref)
    teacher = jnp.concatenate([own_teacher_ref[...], twin_teacher_ref[...]], axis=0)
    left_ids = jnp.concatenate(
        [jnp.transpose(jnp.broadcast_to(left_ref[i : i + 1, :], (128, 128))) for i in range(2)], axis=0
    )[:, :1]
    for place, chunk_ref in zip(places, chunks):
        texts = chunk_ref[...]
        losses, coeff = pair_terms(
            student_ref[...], teacher, left_ids, texts, ids_ref[place : place + 1, :]
        )
        losses_ref[...] += losses
        pulled_ref[...] += jnp.dot(coeff, texts, preferred_element_type=jnp.float32)
    if last:
        half = pulled_ref.shape[0] // 2
        own_ref[...] = pulled_ref[:half]
        twin_ref[...] = pulled_ref[half:]


def pair_sums(student_rows, own_teacher, twin_teacher, left_ids, text_ids, chunks, carried=(), last=False):
    rows, width = student_rows.shape
    texts, places = zip(*chunks)
    count = sum(chunk.shape[0] for chunk in texts)
    operands = (student_rows, own_teacher, twin_teacher, left_ids, text_ids, *texts, *carried)
    whole = pl.BlockSpec(memory_space=pltpu.VMEM)
    parts = 1 + last
    sums = (jax.ShapeDtypeStruct((rows // parts, width), jnp.float32),) * parts
    return pl.pallas_call(
        functools.partial(pair_kernel, places, bool(carried), last),
        out_shape=(*sums, jax.ShapeDtypeStruct((rows, 1), jnp.float32)),
        in_specs=[whole] * len(operands),
        out_specs=(whole,) * (len(sums) + 1),
        scratch_shapes=[pltpu.VMEM((rows, width), jnp.float32)] * last,
        compiler_params=pltpu.CompilerParams(vmem_limit_bytes=20 << 20),
        cost_estimate=pl.CostEstimate(
            flops=6 * rows * count * width,
            bytes_accessed=2 * count * width,
            transcendentals=4 * rows * count,
        ),
    )(*operands)


def row_order(core):
    place = lax.iota(jnp.int32, 1280)
    first, second = place // 320, place // 80 % 4
    X = jnp.where(core == 0, first, second)
    y = jnp.where(core == 0, second, first)
    row = (X % 2 * 4 + y) * 5 + place % 5
    return jnp.where(row < 36, X // 2 * 576 + place // 5 % 16 * 36 + row, -1)


def weight_order():
    row = lax.iota(jnp.int32, 576)
    q = row % 36
    return q // 5 * 96 + row // 36 * 5 + q % 5


def grad_order():
    part = lax.iota(jnp.int32, 144)
    q = part % 48
    return jnp.where(q < 40, q // 5 * 96 + 80 + part // 48 * 5 + q % 5, -1)


def one_hot(index, width):
    return (index[:, None] == lax.iota(jnp.int32, width)[None, :]).astype(jnp.bfloat16)


def rounded(values):
    return lax.reduce_precision(values, 8, 7)


def per_device(
    student_features,
    teacher_image,
    text_embeds,
    pair_ids,
    head_weights,
    moment_first,
    moment_second,
):
    rows = student_features.shape[0]
    blk_index = lax.axis_index("blk")
    group_index = lax.axis_index("group")
    y, xh, core = blk_index // 4, blk_index // 2 % 2, blk_index % 2
    xl, z = group_index // 16, group_index % 16

    copies, unit_teacher = head(text_embeds, student_features, teacher_image, 4)
    copies, twin_features = lax.optimization_barrier((copies, student_features))
    near = exchange(copies, FIRST)

    far_features, far_teacher = from_twin(twin_features), from_twin(unit_teacher)
    both_features = jnp.concatenate([student_features, far_features], axis=0)
    projected = lax.dot_general(
        both_features,
        head_weights,
        (((1,), (1,)), ((), ())),
        preferred_element_type=jnp.float32,
    )
    inverse = lax.rsqrt(jnp.sum(projected * projected, axis=-1, keepdims=True) + norm_eps)
    student = projected * inverse
    student_b = student.astype(jnp.bfloat16)

    ids_grid = pair_ids.reshape(4, 2, 2, 2, 16, rows)
    ids_plane = lax.dynamic_index_in_dim(ids_grid, z, 4, keepdims=False)
    ids_core = lax.dynamic_index_in_dim(ids_plane, core, 2, keepdims=False)
    ids_yx = ids_core.transpose(0, 2, 1, 3).reshape(4, 4, rows)
    ids_xy = ids_core.transpose(1, 2, 0, 3).reshape(4, 4, rows)
    text_ids = jnp.where(core == 0, ids_yx, ids_xy)
    text_ids = jnp.concatenate([text_ids, text_ids[:3]], axis=0)
    text_ids = lax.dynamic_slice_in_dim(text_ids, jnp.where(core == 0, y, xh * 2 + xl), 4, 0)
    text_ids = text_ids.reshape(8, 2 * rows)
    ids_rows = pair_ids.reshape(512, rows)
    left_ids = jnp.stack(
        [
            lax.dynamic_index_in_dim(ids_rows, blk_index * 32 + group_index, 0, keepdims=False),
            lax.dynamic_index_in_dim(ids_rows, (blk_index ^ 1) * 32 + group_index, 0, keepdims=False),
        ]
    )
    near, *images = lax.optimization_barrier(
        (near, student_b, unit_teacher, far_teacher, left_ids, text_ids)
    )

    top = near[:2, :, :1152].reshape(2 * rows, 1152)
    bottom = near[2:, :, :1152].reshape(2 * rows, 1152)
    before_top = lax.ppermute(top, AXES, FORTH)
    after_bottom = lax.ppermute(bottom, AXES, BACK)
    before_bottom = lax.ppermute(bottom, AXES, FORTH)
    after_top = lax.ppermute(top, AXES, BACK)
    far_top = lax.ppermute(before_top, AXES, FORTH)
    far_bottom = lax.ppermute(after_bottom, AXES, BACK)
    sums = pair_sums(*images, [(top, 0), (bottom, 1)])
    near_chunks = [(before_top, 6), (after_bottom, 3), (before_bottom, 7), (after_top, 2)]
    sums = pair_sums(*images, near_chunks, sums)
    far_chunks = [(far_top, 4), (far_bottom, 5)]
    pulled, twin_pulled, losses = pair_sums(*images, far_chunks, sums, last=True)
    losses = losses.reshape(-1)

    pulled = pulled + from_twin(twin_pulled)
    features = lax.optimization_barrier(near[:, :, 1152:])
    student, inverse = student[:rows], inverse[:rows]
    grad_student = student_scale / rows * pulled
    grad_projected = (
        inverse * (grad_student - student * jnp.sum(student * grad_student, axis=-1, keepdims=True))
    ).astype(jnp.bfloat16)

    grad_rows = lax.dot_general(
        one_hot(row_order(core), 1152),
        grad_projected,
        (((1,), (1,)), ((), ())),
        preferred_element_type=jnp.float32,
    ).astype(jnp.bfloat16)
    grad_rows = exchange(grad_rows.reshape(4, 320, rows), FIRST)
    line_grad = lax.dot_general(
        grad_rows, features, (((0, 2), (0, 1)), ((), ())), preferred_element_type=jnp.float32
    )
    core_grad = jnp.sum(exchange(line_grad.reshape(4, 80, 768), SECOND), axis=0)
    left, right = core_grad[:, :384], core_grad[:, 384:]
    other_losses = jnp.pad(losses[rows:].reshape(1, rows), ((0, 7), (0, 256)))
    arrived = from_twin(jnp.concatenate([jnp.where(core == 0, right, left), other_losses], axis=0))
    chip_grad = jnp.where(core == 0, left, right) + arrived[:80]
    row_loss = (losses[:rows] + arrived[80, :rows]) / rows

    column_grad = jnp.pad(chip_grad.reshape(16, 15, 128), ((0, 0), (0, 1), (0, 0)))
    own_grad = jnp.sum(exchange(column_grad, COLUMN), axis=0)[:15].reshape(5, 384)

    def adam(head_grad, first, second, weights):
        new_first = beta_one * first + (1.0 - beta_one) * head_grad
        new_second = beta_two * second + (1.0 - beta_two) * head_grad * head_grad
        first_hat = new_first / (1.0 - beta_one**adam_step)
        second_hat = new_second / (1.0 - beta_two**adam_step)
        weights = weights.astype(jnp.float32)
        updated = weights - learn_rate * (
            first_hat / (jnp.sqrt(second_hat) + adam_eps) + weight_decay * weights
        )
        return updated.astype(jnp.bfloat16)

    def piece(values, start):
        group_rows = lax.dynamic_slice_in_dim(values, start, 36, 0)
        padded = jnp.pad(group_rows, ((0, 4), (0, 0)))
        return lax.dynamic_slice(padded, ((xh * 4 + y) * 5, core * 384), (5, 384))

    own_weights = adam(
        own_grad,
        piece(moment_first, 0),
        piece(moment_second, 0),
        piece(head_weights, group_index * 36),
    )
    chip_weights = share(own_weights, COLUMN).reshape(80, 384)
    high = rounded(own_grad)
    middle = rounded(own_grad - high)
    low = own_grad - high - middle
    spare = jnp.zeros((1, 384), jnp.float32)
    grad_parts = jnp.concatenate([high, middle, low, spare], axis=0).astype(jnp.bfloat16)
    plane = share(jnp.concatenate([chip_weights, grad_parts], axis=0), PLANE).reshape(2, 768, 384)
    select_weights = one_hot(weight_order(), 768)
    halves = [
        jnp.dot(select_weights, plane[i], preferred_element_type=jnp.float32) for i in range(2)
    ]
    group_parts = jnp.dot(
        one_hot(grad_order(), 768),
        lax.dynamic_index_in_dim(plane, xl, 0, keepdims=False),
        preferred_element_type=jnp.float32,
    )
    half = jnp.concatenate([*halves, group_parts], axis=0).astype(jnp.bfloat16)
    new_weights, new_first, new_second = last_outputs(
        core, half, from_twin(half), moment_first, moment_second
    )
    return (row_loss, new_first, new_second, new_weights)


def solution(mesh):
    placed = (
        P(("blk", "group"), None),
        P(("blk", "group"), None),
        P(("blk", "group"), None),
        P(),
        P(),
        P("group", None),
        P("group", None),
    )
    return jax.shard_map(
        per_device,
        mesh=mesh,
        in_specs=placed,
        out_specs=(P(("blk", "group")), P("group", None), P("group", None), P()),
        check_vma=False,
    )
```

```python
import functools

import jax
import jax.numpy as jnp
from jax import lax
from jax.experimental import pallas as pl
from jax.experimental.pallas import tpu as pltpu
from jax.sharding import PartitionSpec as P


student_scale = 20.0
student_bias = -1.0
teacher_scale = 25.0
teacher_bias = -1.5
label_mix = 0.5
norm_eps = 1e-06
beta_one = 0.9
beta_two = 0.95
learn_rate = 0.01
weight_decay = 0.0001
adam_eps = 1e-08
adam_step = 100.0

AXES = ("blk", "group")


def device(X, y, core, z):
    return (y * 4 + X % 2 * 2 + core) * 32 + X // 2 * 16 + z


def x_line(y, core, z):
    return [device(X, y, core, z) for X in range(4)]


def y_line(X, core, z):
    return [device(X, y, core, z) for y in range(4)]


def lines(along_x):
    groups = []
    for core in range(2):
        line = x_line if (core == 0) == along_x else y_line
        groups += [line(i, core, z) for z in range(16) for i in range(4)]
    return groups


FIRST = lines(True)
SECOND = lines(False)
PLANE = [
    [device(X, y, core, z) for X in range(4) for y in range(4)]
    for core in range(2)
    for z in range(16)
]
COLUMN = [
    [device(X, y, core, z) for z in range(16)]
    for X in range(4)
    for y in range(4)
    for core in range(2)
]
TWIN = [(i, i ^ 32) for i in range(512)]


def hop(step):
    pairs = []
    for i in range(512):
        blk, group = divmod(i, 32)
        y, xh, core = blk // 4, blk // 2 % 2, blk % 2
        xl, z = divmod(group, 16)
        x = xh * 2 + xl
        if core == 0:
            y = (y + step) % 4
        else:
            x = (x + step) % 4
        pairs.append((i, device(x % 2 * 2 + x // 2, y, core, z)))
    return pairs


FORTH = hop(1)
BACK = hop(-1)


def exchange(pieces, groups):
    return lax.all_to_all(pieces, AXES, 0, 0, axis_index_groups=groups, tiled=True)


def share(block, groups):
    return exchange(jnp.broadcast_to(block[None], (len(groups[0]), *block.shape)), groups)


def from_twin(shard):
    return lax.ppermute(shard, AXES, TWIN)


def unit_rows(values):
    values = values.astype(jnp.float32)
    return values * lax.rsqrt(jnp.sum(values * values, axis=-1, keepdims=True) + norm_eps)


def head_kernel(texts_ref, features_ref, teacher_ref, out_ref, unit_ref, texts, teacher, packed, unit, sems):
    width = texts_ref.shape[1]
    take_texts = pltpu.make_async_copy(texts_ref, texts, sems.at[0])
    take_features = pltpu.make_async_copy(features_ref, packed.at[:, width:], sems.at[1])
    take_teacher = pltpu.make_async_copy(teacher_ref, teacher, sems.at[2])
    take_texts.start()
    take_features.start()
    take_teacher.start()
    take_texts.wait()
    packed[:, :width] = unit_rows(texts[...]).astype(jnp.bfloat16)
    take_features.wait()
    puts = [
        pltpu.make_async_copy(packed, out_ref.at[i], sems.at[3 + i])
        for i in range(out_ref.shape[0])
    ]
    for put in puts:
        put.start()
    take_teacher.wait()
    unit[...] = unit_rows(teacher[...]).astype(jnp.bfloat16)
    put_unit = pltpu.make_async_copy(unit, unit_ref, sems.at[3 + len(puts)])
    put_unit.start()
    for put in puts:
        put.wait()
    put_unit.wait()


def head(texts, features, teacher, count):
    rows, width = texts.shape[0], texts.shape[1] + features.shape[1]
    return pl.pallas_call(
        head_kernel,
        out_shape=(
            jax.ShapeDtypeStruct((count, rows, width), jnp.bfloat16),
            jax.ShapeDtypeStruct(teacher.shape, jnp.bfloat16),
        ),
        in_specs=[pl.BlockSpec(memory_space=pltpu.HBM)] * 3,
        out_specs=(pl.BlockSpec(memory_space=pltpu.HBM),) * 2,
        scratch_shapes=[
            pltpu.VMEM(texts.shape, jnp.bfloat16),
            pltpu.VMEM(teacher.shape, jnp.bfloat16),
            pltpu.VMEM((rows, width), jnp.bfloat16),
            pltpu.VMEM(teacher.shape, jnp.bfloat16),
            pltpu.SemaphoreType.DMA((4 + count,)),
        ],
        compiler_params=pltpu.CompilerParams(vmem_limit_bytes=60 << 20),
        cost_estimate=pl.CostEstimate(
            flops=8 * texts.size, bytes_accessed=2 * (count + 2) * rows * width, transcendentals=0
        ),
    )(texts, features, teacher)


def last_kernel(core_ref, half_ref, twin_ref, first_ref, second_ref, *outs):
    weights_ref, new_first_ref, new_second_ref = outs

    def put(left, right):
        weights_ref[:, :384] = left[:1152, :]
        weights_ref[:, 384:] = right[:1152, :]
        for side, ref in enumerate((left, right)):
            columns = slice(side * 384, side * 384 + 384)
            high, middle, low = (
                ref[1152 + i * 48 : 1200 + i * 48, :].astype(jnp.float32) for i in range(3)
            )
            grad = ((high + middle) + low)[:36]
            new_first_ref[:, columns] = beta_one * first_ref[:, columns] + (1.0 - beta_one) * grad
            new_second_ref[:, columns] = (
                beta_two * second_ref[:, columns] + (1.0 - beta_two) * grad * grad
            )

    @pl.when(core_ref[0] == 0)
    def _():
        put(half_ref, twin_ref)

    @pl.when(core_ref[0] != 0)
    def _():
        put(twin_ref, half_ref)


def last_outputs(core, half, twin_half, moment_first, moment_second):
    whole = pl.BlockSpec(memory_space=pltpu.VMEM)
    moment = jax.ShapeDtypeStruct(moment_first.shape, jnp.float32)
    return pl.pallas_call(
        last_kernel,
        out_shape=(jax.ShapeDtypeStruct((1152, 768), jnp.bfloat16), moment, moment),
        in_specs=[pl.BlockSpec(memory_space=pltpu.SMEM)] + [whole] * 4,
        out_specs=(whole,) * 3,
        compiler_params=pltpu.CompilerParams(vmem_limit_bytes=12 << 20),
        cost_estimate=pl.CostEstimate(flops=0, bytes_accessed=6 << 20, transcendentals=0),
    )(core.reshape(1), half, twin_half, moment_first, moment_second)


def pair_terms(student_rows, teacher_rows, left_ids, text_rows, right_ids):
    dims = (((1,), (1,)), ((), ()))
    student_logit = (
        student_scale
        * lax.dot_general(student_rows, text_rows, dims, preferred_element_type=jnp.float32)
        + student_bias
    )
    teacher_logit = (
        teacher_scale
        * lax.dot_general(teacher_rows, text_rows, dims, preferred_element_type=jnp.float32)
        + teacher_bias
    )
    labels = (left_ids == right_ids).astype(jnp.float32)
    target = (1.0 - label_mix) * labels + label_mix * jax.nn.sigmoid(teacher_logit)
    tail = jnp.exp(-jnp.abs(student_logit))
    softplus = jnp.maximum(student_logit, 0.0) + jnp.log1p(tail)
    chance = jnp.where(student_logit >= 0.0, 1.0, tail) / (1.0 + tail)
    losses = jnp.sum(softplus - target * student_logit, axis=1, keepdims=True)
    return losses, (chance - target).astype(jnp.bfloat16)


def pair_kernel(places, carried, last, *refs):
    student_ref, own_teacher_ref, twin_teacher_ref, left_ref, ids_ref = refs[:5]
    chunks, rest = refs[5 : 5 + len(places)], refs[5 + len(places) :]
    pulled_ref, losses_ref = rest[-2:]
    if last:
        own_ref, twin_ref, losses_ref, pulled_ref = rest[-4:]
    if carried:
        pulled_ref[...] = rest[0][...]
        total = rest[1][...]
    else:
        pulled_ref[...] = jnp.zeros_like(pulled_ref)
        total = jnp.zeros(losses_ref.shape, jnp.float32)
    teacher = jnp.concatenate([own_teacher_ref[...], twin_teacher_ref[...]], axis=0)
    left_ids = jnp.concatenate(
        [jnp.transpose(jnp.broadcast_to(left_ref[i : i + 1, :], (128, 128))) for i in range(2)], axis=0
    )[:, :1]
    for place, chunk_ref in zip(places, chunks):
        texts = chunk_ref[...]
        losses, coeff = pair_terms(
            student_ref[...], teacher, left_ids, texts, ids_ref[place : place + 1, :]
        )
        total += losses
        pulled_ref[...] += jnp.dot(coeff, texts, preferred_element_type=jnp.float32)
    if not last:
        losses_ref[...] = total
        return
    own_ref[...] = pulled_ref[:128]
    twin_ref[...] = pulled_ref[128:]
    for i in range(2):
        column = jnp.broadcast_to(total[i * 128 : i * 128 + 128], (128, 128))
        losses_ref[i : i + 1, :] = jnp.transpose(column)[:1]


def pair_sums(student_rows, own_teacher, twin_teacher, left_ids, text_ids, chunks, carried=(), last=False):
    rows, width = student_rows.shape
    texts, places = zip(*chunks)
    count = sum(chunk.shape[0] for chunk in texts)
    operands = (student_rows, own_teacher, twin_teacher, left_ids, text_ids, *texts, *carried)
    whole = pl.BlockSpec(memory_space=pltpu.VMEM)
    parts = 1 + last
    sums = (jax.ShapeDtypeStruct((rows // parts, width), jnp.float32),) * parts
    return pl.pallas_call(
        functools.partial(pair_kernel, places, bool(carried), last),
        out_shape=(*sums, jax.ShapeDtypeStruct((2, 128) if last else (rows, 1), jnp.float32)),
        in_specs=[whole] * len(operands),
        out_specs=(whole,) * (len(sums) + 1),
        scratch_shapes=[pltpu.VMEM((rows, width), jnp.float32)] * last,
        compiler_params=pltpu.CompilerParams(vmem_limit_bytes=20 << 20),
        cost_estimate=pl.CostEstimate(
            flops=6 * rows * count * width,
            bytes_accessed=2 * count * width,
            transcendentals=4 * rows * count,
        ),
    )(*operands)


def row_order(core):
    place = lax.iota(jnp.int32, 1280)
    first, second = place // 320, place // 80 % 4
    X = jnp.where(core == 0, first, second)
    y = jnp.where(core == 0, second, first)
    row = (X % 2 * 4 + y) * 5 + place % 5
    return jnp.where(row < 36, X // 2 * 576 + place // 5 % 16 * 36 + row, -1)


def weight_order():
    row = lax.iota(jnp.int32, 576)
    q = row % 36
    return q // 5 * 96 + row // 36 * 5 + q % 5


def grad_order():
    part = lax.iota(jnp.int32, 144)
    q = part % 48
    return jnp.where(q < 40, q // 5 * 96 + 80 + part // 48 * 5 + q % 5, -1)


def one_hot(index, width):
    return (index[:, None] == lax.iota(jnp.int32, width)[None, :]).astype(jnp.bfloat16)


def rounded(values):
    return lax.reduce_precision(values, 8, 7)


def per_device(
    student_features,
    teacher_image,
    text_embeds,
    pair_ids,
    head_weights,
    moment_first,
    moment_second,
):
    rows = student_features.shape[0]
    blk_index = lax.axis_index("blk")
    group_index = lax.axis_index("group")
    y, xh, core = blk_index // 4, blk_index // 2 % 2, blk_index % 2
    xl, z = group_index // 16, group_index % 16

    copies, unit_teacher = head(text_embeds, student_features, teacher_image, 4)
    copies, twin_features = lax.optimization_barrier((copies, student_features))
    near = exchange(copies, FIRST)

    far_features, far_teacher = from_twin(twin_features), from_twin(unit_teacher)
    both_features = jnp.concatenate([student_features, far_features], axis=0)
    projected = lax.dot_general(
        both_features,
        head_weights,
        (((1,), (1,)), ((), ())),
        preferred_element_type=jnp.float32,
    )
    inverse = lax.rsqrt(jnp.sum(projected * projected, axis=-1, keepdims=True) + norm_eps)
    student = projected * inverse
    student_b = student.astype(jnp.bfloat16)

    ids_grid = pair_ids.reshape(4, 2, 2, 2, 16, rows)
    ids_plane = lax.dynamic_index_in_dim(ids_grid, z, 4, keepdims=False)
    ids_core = lax.dynamic_index_in_dim(ids_plane, core, 2, keepdims=False)
    ids_yx = ids_core.transpose(0, 2, 1, 3).reshape(4, 4, rows)
    ids_xy = ids_core.transpose(1, 2, 0, 3).reshape(4, 4, rows)
    text_ids = jnp.where(core == 0, ids_yx, ids_xy)
    text_ids = jnp.concatenate([text_ids, text_ids[:3]], axis=0)
    text_ids = lax.dynamic_slice_in_dim(text_ids, jnp.where(core == 0, y, xh * 2 + xl), 4, 0)
    text_ids = text_ids.reshape(8, 2 * rows)
    ids_rows = pair_ids.reshape(512, rows)
    left_ids = jnp.stack(
        [
            lax.dynamic_index_in_dim(ids_rows, blk_index * 32 + group_index, 0, keepdims=False),
            lax.dynamic_index_in_dim(ids_rows, (blk_index ^ 1) * 32 + group_index, 0, keepdims=False),
        ]
    )
    near, *images = lax.optimization_barrier(
        (near, student_b, unit_teacher, far_teacher, left_ids, text_ids)
    )

    top = near[:2, :, :1152].reshape(2 * rows, 1152)
    bottom = near[2:, :, :1152].reshape(2 * rows, 1152)
    before_top = lax.ppermute(top, AXES, FORTH)
    after_bottom = lax.ppermute(bottom, AXES, BACK)
    before_bottom = lax.ppermute(bottom, AXES, FORTH)
    after_top = lax.ppermute(top, AXES, BACK)
    far_top = lax.ppermute(before_top, AXES, FORTH)
    far_bottom = lax.ppermute(after_bottom, AXES, BACK)
    sums = pair_sums(*images, [(top, 0), (bottom, 1)])
    near_chunks = [(before_top, 6), (after_bottom, 3), (before_bottom, 7), (after_top, 2)]
    sums = pair_sums(*images, near_chunks, sums)
    features = near[:, :, 1152:]
    features, sums = lax.optimization_barrier((features, sums))
    far_chunks = [(far_top, 4), (far_bottom, 5)]
    pulled, twin_pulled, losses = pair_sums(*images, far_chunks, sums, last=True)

    pulled = pulled + from_twin(twin_pulled)
    student, inverse = student[:rows], inverse[:rows]
    grad_student = student_scale / rows * pulled
    grad_projected = (
        inverse * (grad_student - student * jnp.sum(student * grad_student, axis=-1, keepdims=True))
    ).astype(jnp.bfloat16)

    grad_rows = lax.dot_general(
        one_hot(row_order(core), 1152),
        grad_projected,
        (((1,), (1,)), ((), ())),
        preferred_element_type=jnp.float32,
    ).astype(jnp.bfloat16)
    grad_rows = exchange(grad_rows.reshape(4, 320, rows), FIRST)
    line_grad = lax.dot_general(
        grad_rows, features, (((0, 2), (0, 1)), ((), ())), preferred_element_type=jnp.float32
    )
    core_grad = jnp.sum(exchange(line_grad.reshape(4, 80, 768), SECOND), axis=0)
    left, right = core_grad[:, :384], core_grad[:, 384:]
    other_losses = jnp.pad(losses[1:], ((0, 7), (0, 256)))
    arrived = from_twin(jnp.concatenate([jnp.where(core == 0, right, left), other_losses], axis=0))
    chip_grad = jnp.where(core == 0, left, right) + arrived[:80]
    row_loss = (losses[0] + arrived[80, :rows]) / rows

    column_grad = jnp.pad(chip_grad.reshape(16, 15, 128), ((0, 0), (0, 1), (0, 0)))
    own_grad = jnp.sum(exchange(column_grad, COLUMN), axis=0)[:15].reshape(5, 384)

    def adam(head_grad, first, second, weights):
        new_first = beta_one * first + (1.0 - beta_one) * head_grad
        new_second = beta_two * second + (1.0 - beta_two) * head_grad * head_grad
        first_hat = new_first / (1.0 - beta_one**adam_step)
        second_hat = new_second / (1.0 - beta_two**adam_step)
        weights = weights.astype(jnp.float32)
        updated = weights - learn_rate * (
            first_hat / (jnp.sqrt(second_hat) + adam_eps) + weight_decay * weights
        )
        return updated.astype(jnp.bfloat16)

    def piece(values, start):
        group_rows = lax.dynamic_slice_in_dim(values, start, 36, 0)
        padded = jnp.pad(group_rows, ((0, 4), (0, 0)))
        return lax.dynamic_slice(padded, ((xh * 4 + y) * 5, core * 384), (5, 384))

    own_weights = adam(
        own_grad,
        piece(moment_first, 0),
        piece(moment_second, 0),
        piece(head_weights, group_index * 36),
    )
    chip_weights = share(own_weights, COLUMN).reshape(80, 384)
    high = rounded(own_grad)
    middle = rounded(own_grad - high)
    low = own_grad - high - middle
    spare = jnp.zeros((1, 384), jnp.float32)
    grad_parts = jnp.concatenate([high, middle, low, spare], axis=0).astype(jnp.bfloat16)
    plane = share(jnp.concatenate([chip_weights, grad_parts], axis=0), PLANE).reshape(2, 768, 384)
    select_weights = one_hot(weight_order(), 768)
    halves = [
        jnp.dot(select_weights, plane[i], preferred_element_type=jnp.float32) for i in range(2)
    ]
    group_parts = jnp.dot(
        one_hot(grad_order(), 768),
        lax.dynamic_index_in_dim(plane, xl, 0, keepdims=False),
        preferred_element_type=jnp.float32,
    )
    half = jnp.concatenate([*halves, group_parts], axis=0).astype(jnp.bfloat16)
    new_weights, new_first, new_second = last_outputs(
        core, half, from_twin(half), moment_first, moment_second
    )
    return (row_loss, new_first, new_second, new_weights)


def solution(mesh):
    placed = (
        P(("blk", "group"), None),
        P(("blk", "group"), None),
        P(("blk", "group"), None),
        P(),
        P(),
        P("group", None),
        P("group", None),
    )
    return jax.shard_map(
        per_device,
        mesh=mesh,
        in_specs=placed,
        out_specs=(P(("blk", "group")), P("group", None), P("group", None), P()),
        check_vma=False,
    )
```

```python
import functools

import jax
import jax.numpy as jnp
import numpy as np
from jax import lax
from jax.experimental import pallas as pl
from jax.experimental.pallas import tpu as pltpu
from jax.sharding import PartitionSpec as P


student_scale = 20.0
student_bias = -1.0
teacher_scale = 25.0
teacher_bias = -1.5
label_mix = 0.5
norm_eps = 1e-06
beta_one = 0.9
beta_two = 0.95
learn_rate = 0.01
weight_decay = 0.0001
adam_eps = 1e-08
adam_step = 100.0

AXES = ("blk", "group")


def device(X, y, core, z):
    return (y * 4 + X % 2 * 2 + core) * 32 + X // 2 * 16 + z


def x_line(y, core, z):
    return [device(X, y, core, z) for X in range(4)]


def y_line(X, core, z):
    return [device(X, y, core, z) for y in range(4)]


def lines(along_x):
    groups = []
    for core in range(2):
        line = x_line if (core == 0) == along_x else y_line
        groups += [line(i, core, z) for z in range(16) for i in range(4)]
    return groups


FIRST = lines(True)
SECOND = lines(False)
PLANE = [
    [device(X, y, core, z) for X in range(4) for y in range(4)]
    for core in range(2)
    for z in range(16)
]
COLUMN = [
    [device(X, y, core, z) for z in range(16)]
    for X in range(4)
    for y in range(4)
    for core in range(2)
]
TWIN = [(i, i ^ 32) for i in range(512)]


def hop(step):
    pairs = []
    for i in range(512):
        blk, group = divmod(i, 32)
        y, xh, core = blk // 4, blk // 2 % 2, blk % 2
        xl, z = divmod(group, 16)
        x = xh * 2 + xl
        if core == 0:
            y = (y + step) % 4
        else:
            x = (x + step) % 4
        pairs.append((i, device(x % 2 * 2 + x // 2, y, core, z)))
    return pairs


FORTH = hop(1)
BACK = hop(-1)


def exchange(pieces, groups):
    return lax.all_to_all(pieces, AXES, 0, 0, axis_index_groups=groups, tiled=True)


def share(block, groups):
    return exchange(jnp.broadcast_to(block[None], (len(groups[0]), *block.shape)), groups)


def from_twin(shard):
    return lax.ppermute(shard, AXES, TWIN)


def unit_rows(values):
    values = values.astype(jnp.float32)
    return values * lax.rsqrt(jnp.sum(values * values, axis=-1, keepdims=True) + norm_eps)


def head_kernel(texts_ref, features_ref, teacher_ref, out_ref, unit_ref, texts, teacher, packed, unit, sems):
    width = texts_ref.shape[1]
    take_texts = pltpu.make_async_copy(texts_ref, texts, sems.at[0])
    take_features = pltpu.make_async_copy(features_ref, packed.at[:, width:], sems.at[1])
    take_teacher = pltpu.make_async_copy(teacher_ref, teacher, sems.at[2])
    take_texts.start()
    take_features.start()
    take_teacher.start()
    take_texts.wait()
    packed[:, :width] = unit_rows(texts[...]).astype(jnp.bfloat16)
    take_features.wait()
    puts = [
        pltpu.make_async_copy(packed, out_ref.at[i], sems.at[3 + i])
        for i in range(out_ref.shape[0])
    ]
    for put in puts:
        put.start()
    take_teacher.wait()
    unit[...] = unit_rows(teacher[...]).astype(jnp.bfloat16)
    put_unit = pltpu.make_async_copy(unit, unit_ref, sems.at[3 + len(puts)])
    put_unit.start()
    for put in puts:
        put.wait()
    put_unit.wait()


def head(texts, features, teacher, count):
    rows, width = texts.shape[0], texts.shape[1] + features.shape[1]
    return pl.pallas_call(
        head_kernel,
        out_shape=(
            jax.ShapeDtypeStruct((count, rows, width), jnp.bfloat16),
            jax.ShapeDtypeStruct(teacher.shape, jnp.bfloat16),
        ),
        in_specs=[pl.BlockSpec(memory_space=pltpu.HBM)] * 3,
        out_specs=(pl.BlockSpec(memory_space=pltpu.HBM),) * 2,
        scratch_shapes=[
            pltpu.VMEM(texts.shape, jnp.bfloat16),
            pltpu.VMEM(teacher.shape, jnp.bfloat16),
            pltpu.VMEM((rows, width), jnp.bfloat16),
            pltpu.VMEM(teacher.shape, jnp.bfloat16),
            pltpu.SemaphoreType.DMA((4 + count,)),
        ],
        compiler_params=pltpu.CompilerParams(vmem_limit_bytes=60 << 20),
        cost_estimate=pl.CostEstimate(
            flops=8 * texts.size, bytes_accessed=2 * (count + 2) * rows * width, transcendentals=0
        ),
    )(texts, features, teacher)


def select_kernel(xl_ref, rows_ref, plane_ref, out_ref):
    def picked(count, which, part):
        rows = lax.broadcasted_iota(jnp.int32, (count, rows_ref.shape[1]), 0)
        chosen = (rows == rows_ref[which : which + 1, :]).astype(jnp.bfloat16)
        return [
            jnp.dot(chosen, values, preferred_element_type=jnp.float32).astype(jnp.bfloat16)
            for values in part
        ]

    low, high = picked(576, 0, (plane_ref[0], plane_ref[1]))
    out_ref[:576, :] = low
    out_ref[576:1152, :] = high
    (out_ref[1152:, :],) = picked(144, 1, (plane_ref[xl_ref[0]],))


def selected(xl, plane):
    whole = pl.BlockSpec(memory_space=pltpu.VMEM)
    return pl.pallas_call(
        select_kernel,
        out_shape=jax.ShapeDtypeStruct((1296, 384), jnp.bfloat16),
        in_specs=[pl.BlockSpec(memory_space=pltpu.SMEM), whole, whole],
        out_specs=whole,
        compiler_params=pltpu.CompilerParams(vmem_limit_bytes=12 << 20),
        cost_estimate=pl.CostEstimate(
            flops=2 * 1296 * 768 * 384, bytes_accessed=2 << 20, transcendentals=0
        ),
    )(xl.reshape(1), jnp.asarray(place_rows()), plane)


def last_kernel(core_ref, half_ref, twin_ref, first_ref, second_ref, *outs):
    weights_ref, new_first_ref, new_second_ref = outs

    def put(left, right):
        weights_ref[:, :384] = left[:1152, :]
        weights_ref[:, 384:] = right[:1152, :]
        for side, ref in enumerate((left, right)):
            columns = slice(side * 384, side * 384 + 384)
            high, middle, low = (
                ref[1152 + i * 48 : 1200 + i * 48, :].astype(jnp.float32) for i in range(3)
            )
            grad = ((high + middle) + low)[:36]
            new_first_ref[:, columns] = beta_one * first_ref[:, columns] + (1.0 - beta_one) * grad
            new_second_ref[:, columns] = (
                beta_two * second_ref[:, columns] + (1.0 - beta_two) * grad * grad
            )

    @pl.when(core_ref[0] == 0)
    def _():
        put(half_ref, twin_ref)

    @pl.when(core_ref[0] != 0)
    def _():
        put(twin_ref, half_ref)


def last_outputs(core, half, twin_half, moment_first, moment_second):
    whole = pl.BlockSpec(memory_space=pltpu.VMEM)
    moment = jax.ShapeDtypeStruct(moment_first.shape, jnp.float32)
    return pl.pallas_call(
        last_kernel,
        out_shape=(jax.ShapeDtypeStruct((1152, 768), jnp.bfloat16), moment, moment),
        in_specs=[pl.BlockSpec(memory_space=pltpu.SMEM)] + [whole] * 4,
        out_specs=(whole,) * 3,
        compiler_params=pltpu.CompilerParams(vmem_limit_bytes=12 << 20),
        cost_estimate=pl.CostEstimate(flops=0, bytes_accessed=6 << 20, transcendentals=0),
    )(core.reshape(1), half, twin_half, moment_first, moment_second)


def pair_terms(student_rows, teacher_rows, left_ids, text_rows, right_ids):
    dims = (((1,), (1,)), ((), ()))
    student_logit = (
        student_scale
        * lax.dot_general(student_rows, text_rows, dims, preferred_element_type=jnp.float32)
        + student_bias
    )
    teacher_logit = (
        teacher_scale
        * lax.dot_general(teacher_rows, text_rows, dims, preferred_element_type=jnp.float32)
        + teacher_bias
    )
    labels = (left_ids == right_ids).astype(jnp.float32)
    target = (1.0 - label_mix) * labels + label_mix * jax.nn.sigmoid(teacher_logit)
    tail = jnp.exp(-jnp.abs(student_logit))
    softplus = jnp.maximum(student_logit, 0.0) + jnp.log1p(tail)
    chance = jnp.where(student_logit >= 0.0, 1.0, tail) / (1.0 + tail)
    losses = jnp.sum(softplus - target * student_logit, axis=1, keepdims=True)
    return losses, (chance - target).astype(jnp.bfloat16)


def pair_kernel(places, carried, last, *refs):
    student_ref, own_teacher_ref, twin_teacher_ref, left_ref, ids_ref = refs[:5]
    chunks, rest = refs[5 : 5 + len(places)], refs[5 + len(places) :]
    pulled_ref, losses_ref = rest[-2:]
    if last:
        own_ref, twin_ref, losses_ref, pulled_ref = rest[-4:]
    if carried:
        pulled_ref[...] = rest[0][...]
        total = rest[1][...]
    else:
        pulled_ref[...] = jnp.zeros_like(pulled_ref)
        total = jnp.zeros(losses_ref.shape, jnp.float32)
    teacher = jnp.concatenate([own_teacher_ref[...], twin_teacher_ref[...]], axis=0)
    left_ids = jnp.concatenate(
        [jnp.transpose(jnp.broadcast_to(left_ref[i : i + 1, :], (128, 128))) for i in range(2)], axis=0
    )[:, :1]
    for place, chunk_ref in zip(places, chunks):
        texts = chunk_ref[...]
        losses, coeff = pair_terms(
            student_ref[...], teacher, left_ids, texts, ids_ref[place : place + 1, :]
        )
        total += losses
        pulled_ref[...] += jnp.dot(coeff, texts, preferred_element_type=jnp.float32)
    if not last:
        losses_ref[...] = total
        return
    own_ref[...] = pulled_ref[:128]
    twin_ref[...] = pulled_ref[128:]
    for i in range(2):
        column = jnp.broadcast_to(total[i * 128 : i * 128 + 128], (128, 128))
        losses_ref[i : i + 1, :] = jnp.transpose(column)[:1]


def pair_sums(student_rows, own_teacher, twin_teacher, left_ids, text_ids, chunks, carried=(), last=False):
    rows, width = student_rows.shape
    texts, places = zip(*chunks)
    count = sum(chunk.shape[0] for chunk in texts)
    operands = (student_rows, own_teacher, twin_teacher, left_ids, text_ids, *texts, *carried)
    whole = pl.BlockSpec(memory_space=pltpu.VMEM)
    parts = 1 + last
    sums = (jax.ShapeDtypeStruct((rows // parts, width), jnp.float32),) * parts
    return pl.pallas_call(
        functools.partial(pair_kernel, places, bool(carried), last),
        out_shape=(*sums, jax.ShapeDtypeStruct((2, 128) if last else (rows, 1), jnp.float32)),
        in_specs=[whole] * len(operands),
        out_specs=(whole,) * (len(sums) + 1),
        scratch_shapes=[pltpu.VMEM((rows, width), jnp.float32)] * last,
        compiler_params=pltpu.CompilerParams(vmem_limit_bytes=20 << 20),
        cost_estimate=pl.CostEstimate(
            flops=6 * rows * count * width,
            bytes_accessed=2 * count * width,
            transcendentals=4 * rows * count,
        ),
    )(*operands)


def row_order(core):
    place = lax.iota(jnp.int32, 1280)
    first, second = place // 320, place // 80 % 4
    X = jnp.where(core == 0, first, second)
    y = jnp.where(core == 0, second, first)
    row = (X % 2 * 4 + y) * 5 + place % 5
    return jnp.where(row < 36, X // 2 * 576 + place // 5 % 16 * 36 + row, -1)


def place_rows():
    chip, row = np.arange(768) // 96, np.arange(768) % 96
    q = chip * 5 + row % 5
    weights = np.where((row < 80) & (q < 36), row // 5 * 36 + q, -1)
    grads = np.where((row >= 80) & (row < 95), (row - 80) // 5 * 48 + q, -1)
    return np.stack([weights, grads]).astype(np.int32)


def one_hot(index, width):
    return (index[:, None] == lax.iota(jnp.int32, width)[None, :]).astype(jnp.bfloat16)


def rounded(values):
    return lax.reduce_precision(values, 8, 7)


def per_device(
    student_features,
    teacher_image,
    text_embeds,
    pair_ids,
    head_weights,
    moment_first,
    moment_second,
):
    rows = student_features.shape[0]
    blk_index = lax.axis_index("blk")
    group_index = lax.axis_index("group")
    y, xh, core = blk_index // 4, blk_index // 2 % 2, blk_index % 2
    xl, z = group_index // 16, group_index % 16

    copies, unit_teacher = head(text_embeds, student_features, teacher_image, 4)
    copies, twin_features = lax.optimization_barrier((copies, student_features))
    near = exchange(copies, FIRST)

    far_features, far_teacher = from_twin(twin_features), from_twin(unit_teacher)
    both_features = jnp.concatenate([student_features, far_features], axis=0)
    projected = lax.dot_general(
        both_features,
        head_weights,
        (((1,), (1,)), ((), ())),
        preferred_element_type=jnp.float32,
    )
    inverse = lax.rsqrt(jnp.sum(projected * projected, axis=-1, keepdims=True) + norm_eps)
    student = projected * inverse
    student_b = student.astype(jnp.bfloat16)

    ids_grid = pair_ids.reshape(4, 2, 2, 2, 16, rows)
    ids_plane = lax.dynamic_index_in_dim(ids_grid, z, 4, keepdims=False)
    ids_core = lax.dynamic_index_in_dim(ids_plane, core, 2, keepdims=False)
    ids_yx = ids_core.transpose(0, 2, 1, 3).reshape(4, 4, rows)
    ids_xy = ids_core.transpose(1, 2, 0, 3).reshape(4, 4, rows)
    text_ids = jnp.where(core == 0, ids_yx, ids_xy)
    text_ids = jnp.concatenate([text_ids, text_ids[:3]], axis=0)
    text_ids = lax.dynamic_slice_in_dim(text_ids, jnp.where(core == 0, y, xh * 2 + xl), 4, 0)
    text_ids = text_ids.reshape(8, 2 * rows)
    ids_rows = pair_ids.reshape(512, rows)
    left_ids = jnp.stack(
        [
            lax.dynamic_index_in_dim(ids_rows, blk_index * 32 + group_index, 0, keepdims=False),
            lax.dynamic_index_in_dim(ids_rows, (blk_index ^ 1) * 32 + group_index, 0, keepdims=False),
        ]
    )
    near, *images = lax.optimization_barrier(
        (near, student_b, unit_teacher, far_teacher, left_ids, text_ids)
    )

    top = near[:2, :, :1152].reshape(2 * rows, 1152)
    bottom = near[2:, :, :1152].reshape(2 * rows, 1152)
    before_top = lax.ppermute(top, AXES, FORTH)
    after_bottom = lax.ppermute(bottom, AXES, BACK)
    before_bottom = lax.ppermute(bottom, AXES, FORTH)
    after_top = lax.ppermute(top, AXES, BACK)
    far_top = lax.ppermute(before_top, AXES, FORTH)
    far_bottom = lax.ppermute(after_bottom, AXES, BACK)
    sums = pair_sums(*images, [(top, 0), (bottom, 1)])
    near_chunks = [(before_top, 6), (after_bottom, 3), (before_bottom, 7), (after_top, 2)]
    sums = pair_sums(*images, near_chunks, sums)
    features = near[:, :, 1152:]
    features, sums = lax.optimization_barrier((features, sums))
    far_chunks = [(far_top, 4), (far_bottom, 5)]
    pulled, twin_pulled, losses = pair_sums(*images, far_chunks, sums, last=True)

    pulled = pulled + from_twin(twin_pulled)
    student, inverse = student[:rows], inverse[:rows]
    grad_student = student_scale / rows * pulled
    grad_projected = (
        inverse * (grad_student - student * jnp.sum(student * grad_student, axis=-1, keepdims=True))
    ).astype(jnp.bfloat16)

    grad_rows = lax.dot_general(
        one_hot(row_order(core), 1152),
        grad_projected,
        (((1,), (1,)), ((), ())),
        preferred_element_type=jnp.float32,
    ).astype(jnp.bfloat16)
    grad_rows = exchange(grad_rows.reshape(4, 320, rows), FIRST)
    line_grad = lax.dot_general(
        grad_rows, features, (((0, 2), (0, 1)), ((), ())), preferred_element_type=jnp.float32
    )
    core_grad = jnp.sum(exchange(line_grad.reshape(4, 80, 768), SECOND), axis=0)
    left, right = core_grad[:, :384], core_grad[:, 384:]
    other_losses = jnp.pad(losses[1:], ((0, 7), (0, 256)))
    arrived = from_twin(jnp.concatenate([jnp.where(core == 0, right, left), other_losses], axis=0))
    chip_grad = jnp.where(core == 0, left, right) + arrived[:80]
    row_loss = (losses[0] + arrived[80, :rows]) / rows

    column_grad = jnp.pad(chip_grad.reshape(16, 15, 128), ((0, 0), (0, 1), (0, 0)))
    own_grad = jnp.sum(exchange(column_grad, COLUMN), axis=0)[:15].reshape(5, 384)

    def adam(head_grad, first, second, weights):
        new_first = beta_one * first + (1.0 - beta_one) * head_grad
        new_second = beta_two * second + (1.0 - beta_two) * head_grad * head_grad
        first_hat = new_first / (1.0 - beta_one**adam_step)
        second_hat = new_second / (1.0 - beta_two**adam_step)
        weights = weights.astype(jnp.float32)
        updated = weights - learn_rate * (
            first_hat / (jnp.sqrt(second_hat) + adam_eps) + weight_decay * weights
        )
        return updated.astype(jnp.bfloat16)

    def piece(values, start):
        group_rows = lax.dynamic_slice_in_dim(values, start, 36, 0)
        padded = jnp.pad(group_rows, ((0, 4), (0, 0)))
        return lax.dynamic_slice(padded, ((xh * 4 + y) * 5, core * 384), (5, 384))

    own_weights = adam(
        own_grad,
        piece(moment_first, 0),
        piece(moment_second, 0),
        piece(head_weights, group_index * 36),
    )
    chip_weights = share(own_weights, COLUMN).reshape(80, 384)
    high = rounded(own_grad)
    middle = rounded(own_grad - high)
    low = own_grad - high - middle
    spare = jnp.zeros((1, 384), jnp.float32)
    grad_parts = jnp.concatenate([high, middle, low, spare], axis=0).astype(jnp.bfloat16)
    plane = share(jnp.concatenate([chip_weights, grad_parts], axis=0), PLANE).reshape(2, 768, 384)
    half = selected(xl, plane)
    new_weights, new_first, new_second = last_outputs(
        core, half, from_twin(half), moment_first, moment_second
    )
    return (row_loss, new_first, new_second, new_weights)


def solution(mesh):
    placed = (
        P(("blk", "group"), None),
        P(("blk", "group"), None),
        P(("blk", "group"), None),
        P(),
        P(),
        P("group", None),
        P("group", None),
    )
    return jax.shard_map(
        per_device,
        mesh=mesh,
        in_specs=placed,
        out_specs=(P(("blk", "group")), P("group", None), P("group", None), P()),
        check_vma=False,
    )
```

```python
import functools

import jax
import jax.numpy as jnp
import numpy as np
from jax import lax
from jax.experimental import pallas as pl
from jax.experimental.pallas import tpu as pltpu
from jax.sharding import PartitionSpec as P


student_scale = 20.0
student_bias = -1.0
teacher_scale = 25.0
teacher_bias = -1.5
label_mix = 0.5
norm_eps = 1e-06
beta_one = 0.9
beta_two = 0.95
learn_rate = 0.01
weight_decay = 0.0001
adam_eps = 1e-08
adam_step = 100.0

AXES = ("blk", "group")


def device(X, y, core, z):
    return (y * 4 + X % 2 * 2 + core) * 32 + X // 2 * 16 + z


def x_line(y, core, z):
    return [device(X, y, core, z) for X in range(4)]


def y_line(X, core, z):
    return [device(X, y, core, z) for y in range(4)]


def lines(along_x):
    groups = []
    for core in range(2):
        line = x_line if (core == 0) == along_x else y_line
        groups += [line(i, core, z) for z in range(16) for i in range(4)]
    return groups


FIRST = lines(True)
SECOND = lines(False)
PLANE = [
    [device(X, y, core, z) for X in range(4) for y in range(4)]
    for core in range(2)
    for z in range(16)
]
COLUMN = [
    [device(X, y, core, z) for z in range(16)]
    for X in range(4)
    for y in range(4)
    for core in range(2)
]
TWIN = [(i, i ^ 32) for i in range(512)]


def hop(step):
    pairs = []
    for i in range(512):
        blk, group = divmod(i, 32)
        y, xh, core = blk // 4, blk // 2 % 2, blk % 2
        xl, z = divmod(group, 16)
        x = xh * 2 + xl
        if core == 0:
            y = (y + step) % 4
        else:
            x = (x + step) % 4
        pairs.append((i, device(x % 2 * 2 + x // 2, y, core, z)))
    return pairs


FORTH = hop(1)
BACK = hop(-1)


def exchange(pieces, groups):
    return lax.all_to_all(pieces, AXES, 0, 0, axis_index_groups=groups, tiled=True)


def share(block, groups):
    return exchange(jnp.broadcast_to(block[None], (len(groups[0]), *block.shape)), groups)


def from_twin(shard):
    return lax.ppermute(shard, AXES, TWIN)


def unit_rows(values):
    values = values.astype(jnp.float32)
    return values * lax.rsqrt(jnp.sum(values * values, axis=-1, keepdims=True) + norm_eps)


def head_kernel(texts_ref, features_ref, teacher_ref, out_ref, unit_ref, texts, teacher, packed, unit, sems):
    width = texts_ref.shape[1]
    take_texts = pltpu.make_async_copy(texts_ref, texts, sems.at[0])
    take_features = pltpu.make_async_copy(features_ref, packed.at[:, width:], sems.at[1])
    take_teacher = pltpu.make_async_copy(teacher_ref, teacher, sems.at[2])
    take_texts.start()
    take_features.start()
    take_teacher.start()
    take_texts.wait()
    packed[:, :width] = unit_rows(texts[...]).astype(jnp.bfloat16)
    take_features.wait()
    puts = [
        pltpu.make_async_copy(packed, out_ref.at[i], sems.at[3 + i])
        for i in range(out_ref.shape[0])
    ]
    for put in puts:
        put.start()
    take_teacher.wait()
    unit[...] = unit_rows(teacher[...]).astype(jnp.bfloat16)
    put_unit = pltpu.make_async_copy(unit, unit_ref, sems.at[3 + len(puts)])
    put_unit.start()
    for put in puts:
        put.wait()
    put_unit.wait()


def head(texts, features, teacher, count):
    rows, width = texts.shape[0], texts.shape[1] + features.shape[1]
    return pl.pallas_call(
        head_kernel,
        out_shape=(
            jax.ShapeDtypeStruct((count, rows, width), jnp.bfloat16),
            jax.ShapeDtypeStruct(teacher.shape, jnp.bfloat16),
        ),
        in_specs=[pl.BlockSpec(memory_space=pltpu.HBM)] * 3,
        out_specs=(pl.BlockSpec(memory_space=pltpu.HBM),) * 2,
        scratch_shapes=[
            pltpu.VMEM(texts.shape, jnp.bfloat16),
            pltpu.VMEM(teacher.shape, jnp.bfloat16),
            pltpu.VMEM((rows, width), jnp.bfloat16),
            pltpu.VMEM(teacher.shape, jnp.bfloat16),
            pltpu.SemaphoreType.DMA((4 + count,)),
        ],
        compiler_params=pltpu.CompilerParams(vmem_limit_bytes=60 << 20),
        cost_estimate=pl.CostEstimate(
            flops=8 * texts.size, bytes_accessed=2 * (count + 2) * rows * width, transcendentals=0
        ),
    )(texts, features, teacher)


def column_kernel(core_ref, parts_ref, others_ref, keep_ref, send_ref):
    def put(keep, send):
        keep_ref[...] = jnp.sum(parts_ref[:, :, keep], axis=0)
        send_ref[:80, :] = jnp.sum(parts_ref[:, :, send], axis=0)

    left, right = slice(0, 384), slice(384, 768)

    @pl.when(core_ref[0] == 0)
    def _():
        put(left, right)

    @pl.when(core_ref[0] != 0)
    def _():
        put(right, left)

    send_ref[80:, :] = others_ref[...]


def column_sums(core, parts, others):
    whole = pl.BlockSpec(memory_space=pltpu.VMEM)
    return pl.pallas_call(
        column_kernel,
        out_shape=(
            jax.ShapeDtypeStruct((80, 384), jnp.float32),
            jax.ShapeDtypeStruct((88, 384), jnp.float32),
        ),
        in_specs=[pl.BlockSpec(memory_space=pltpu.SMEM), whole, whole],
        out_specs=(whole, whole),
        compiler_params=pltpu.CompilerParams(vmem_limit_bytes=12 << 20),
        cost_estimate=pl.CostEstimate(flops=4 * 80 * 768, bytes_accessed=2 << 20, transcendentals=0),
    )(core.reshape(1), parts, others)


def select_kernel(xl_ref, rows_ref, plane_ref, out_ref):
    def picked(count, which, part):
        rows = lax.broadcasted_iota(jnp.int32, (count, rows_ref.shape[1]), 0)
        chosen = (rows == rows_ref[which : which + 1, :]).astype(jnp.bfloat16)
        return [
            jnp.dot(chosen, values, preferred_element_type=jnp.float32).astype(jnp.bfloat16)
            for values in part
        ]

    low, high = picked(576, 0, (plane_ref[0], plane_ref[1]))
    out_ref[:576, :] = low
    out_ref[576:1152, :] = high
    (out_ref[1152:, :],) = picked(144, 1, (plane_ref[xl_ref[0]],))


def selected(xl, plane):
    whole = pl.BlockSpec(memory_space=pltpu.VMEM)
    return pl.pallas_call(
        select_kernel,
        out_shape=jax.ShapeDtypeStruct((1296, 384), jnp.bfloat16),
        in_specs=[pl.BlockSpec(memory_space=pltpu.SMEM), whole, whole],
        out_specs=whole,
        compiler_params=pltpu.CompilerParams(vmem_limit_bytes=12 << 20),
        cost_estimate=pl.CostEstimate(
            flops=2 * 1296 * 768 * 384, bytes_accessed=2 << 20, transcendentals=0
        ),
    )(xl.reshape(1), jnp.asarray(place_rows()), plane)


def last_kernel(core_ref, half_ref, twin_ref, first_ref, second_ref, *outs):
    weights_ref, new_first_ref, new_second_ref, sems = outs

    def put(left, right):
        copies = [
            pltpu.make_async_copy(
                ref.at[:1152, :], weights_ref.at[:, side * 384 : side * 384 + 384], sems.at[side]
            )
            for side, ref in enumerate((left, right))
        ]
        for copy in copies:
            copy.start()
        for side, ref in enumerate((left, right)):
            columns = slice(side * 384, side * 384 + 384)
            high, middle, low = (
                ref[1152 + i * 48 : 1200 + i * 48, :].astype(jnp.float32) for i in range(3)
            )
            grad = ((high + middle) + low)[:36]
            new_first_ref[:, columns] = beta_one * first_ref[:, columns] + (1.0 - beta_one) * grad
            new_second_ref[:, columns] = (
                beta_two * second_ref[:, columns] + (1.0 - beta_two) * grad * grad
            )
        for copy in copies:
            copy.wait()

    @pl.when(core_ref[0] == 0)
    def _():
        put(half_ref, twin_ref)

    @pl.when(core_ref[0] != 0)
    def _():
        put(twin_ref, half_ref)


def last_outputs(core, half, twin_half, moment_first, moment_second):
    whole = pl.BlockSpec(memory_space=pltpu.VMEM)
    moment = jax.ShapeDtypeStruct(moment_first.shape, jnp.float32)
    return pl.pallas_call(
        last_kernel,
        out_shape=(jax.ShapeDtypeStruct((1152, 768), jnp.bfloat16), moment, moment),
        in_specs=[pl.BlockSpec(memory_space=pltpu.SMEM)] + [whole] * 4,
        out_specs=(pl.BlockSpec(memory_space=pltpu.HBM), whole, whole),
        scratch_shapes=[pltpu.SemaphoreType.DMA((2,))],
        compiler_params=pltpu.CompilerParams(vmem_limit_bytes=12 << 20),
        cost_estimate=pl.CostEstimate(flops=0, bytes_accessed=6 << 20, transcendentals=0),
    )(core.reshape(1), half, twin_half, moment_first, moment_second)


def pair_terms(student_rows, teacher_rows, left_ids, text_rows, right_ids):
    dims = (((1,), (1,)), ((), ()))
    student_logit = (
        student_scale
        * lax.dot_general(student_rows, text_rows, dims, preferred_element_type=jnp.float32)
        + student_bias
    )
    teacher_logit = (
        teacher_scale
        * lax.dot_general(teacher_rows, text_rows, dims, preferred_element_type=jnp.float32)
        + teacher_bias
    )
    labels = (left_ids == right_ids).astype(jnp.float32)
    target = (1.0 - label_mix) * labels + label_mix * jax.nn.sigmoid(teacher_logit)
    tail = jnp.exp(-jnp.abs(student_logit))
    softplus = jnp.maximum(student_logit, 0.0) + jnp.log1p(tail)
    chance = jnp.where(student_logit >= 0.0, 1.0, tail) / (1.0 + tail)
    losses = jnp.sum(softplus - target * student_logit, axis=1, keepdims=True)
    return losses, (chance - target).astype(jnp.bfloat16)


def pair_kernel(places, carried, last, *refs):
    student_ref, own_teacher_ref, twin_teacher_ref, left_ref, ids_ref = refs[:5]
    chunks, rest = refs[5 : 5 + len(places)], refs[5 + len(places) :]
    pulled_ref, losses_ref = rest[-2:]
    if last:
        own_ref, twin_ref, losses_ref, others_ref, pulled_ref = rest[-5:]
    if carried:
        pulled_ref[...] = rest[0][...]
        total = rest[1][...]
    else:
        pulled_ref[...] = jnp.zeros_like(pulled_ref)
        total = jnp.zeros(losses_ref.shape, jnp.float32)
    teacher = jnp.concatenate([own_teacher_ref[...], twin_teacher_ref[...]], axis=0)
    left_ids = jnp.concatenate(
        [jnp.transpose(jnp.broadcast_to(left_ref[i : i + 1, :], (128, 128))) for i in range(2)], axis=0
    )[:, :1]
    for place, chunk_ref in zip(places, chunks):
        texts = chunk_ref[...]
        losses, coeff = pair_terms(
            student_ref[...], teacher, left_ids, texts, ids_ref[place : place + 1, :]
        )
        total += losses
        pulled_ref[...] += jnp.dot(coeff, texts, preferred_element_type=jnp.float32)
    if not last:
        losses_ref[...] = total
        return
    own_ref[...] = pulled_ref[:128]
    twin_ref[...] = pulled_ref[128:]
    lanes = [
        jnp.transpose(jnp.broadcast_to(total[i * 128 : i * 128 + 128], (128, 128)))[:1]
        for i in range(2)
    ]
    losses_ref[...] = lanes[0]
    others_ref[...] = jnp.zeros_like(others_ref)
    others_ref[:1, :128] = lanes[1]


def pair_sums(student_rows, own_teacher, twin_teacher, left_ids, text_ids, chunks, carried=(), last=False):
    rows, width = student_rows.shape
    texts, places = zip(*chunks)
    count = sum(chunk.shape[0] for chunk in texts)
    operands = (student_rows, own_teacher, twin_teacher, left_ids, text_ids, *texts, *carried)
    whole = pl.BlockSpec(memory_space=pltpu.VMEM)
    parts = 1 + last
    shapes = [(rows // parts, width)] * parts + ([(1, 128), (8, 384)] if last else [(rows, 1)])
    return pl.pallas_call(
        functools.partial(pair_kernel, places, bool(carried), last),
        out_shape=[jax.ShapeDtypeStruct(shape, jnp.float32) for shape in shapes],
        in_specs=[whole] * len(operands),
        out_specs=[whole] * len(shapes),
        scratch_shapes=[pltpu.VMEM((rows, width), jnp.float32)] * last,
        compiler_params=pltpu.CompilerParams(vmem_limit_bytes=20 << 20),
        cost_estimate=pl.CostEstimate(
            flops=6 * rows * count * width,
            bytes_accessed=2 * count * width,
            transcendentals=4 * rows * count,
        ),
    )(*operands)


def row_order(core):
    place = lax.iota(jnp.int32, 1280)
    first, second = place // 320, place // 80 % 4
    X = jnp.where(core == 0, first, second)
    y = jnp.where(core == 0, second, first)
    row = (X % 2 * 4 + y) * 5 + place % 5
    return jnp.where(row < 36, X // 2 * 576 + place // 5 % 16 * 36 + row, -1)


def place_rows():
    chip, row = np.arange(768) // 96, np.arange(768) % 96
    q = chip * 5 + row % 5
    weights = np.where((row < 80) & (q < 36), row // 5 * 36 + q, -1)
    grads = np.where((row >= 80) & (row < 95), (row - 80) // 5 * 48 + q, -1)
    return np.stack([weights, grads]).astype(np.int32)


def one_hot(index, width):
    return (index[:, None] == lax.iota(jnp.int32, width)[None, :]).astype(jnp.bfloat16)


def rounded(values):
    return lax.reduce_precision(values, 8, 7)


def per_device(
    student_features,
    teacher_image,
    text_embeds,
    pair_ids,
    head_weights,
    moment_first,
    moment_second,
):
    rows = student_features.shape[0]
    blk_index = lax.axis_index("blk")
    group_index = lax.axis_index("group")
    y, xh, core = blk_index // 4, blk_index // 2 % 2, blk_index % 2
    xl, z = group_index // 16, group_index % 16

    copies, unit_teacher = head(text_embeds, student_features, teacher_image, 4)
    copies, twin_features = lax.optimization_barrier((copies, student_features))
    near = exchange(copies, FIRST)

    far_features, far_teacher = from_twin(twin_features), from_twin(unit_teacher)
    both_features = jnp.concatenate([student_features, far_features], axis=0)
    projected = lax.dot_general(
        both_features,
        head_weights,
        (((1,), (1,)), ((), ())),
        preferred_element_type=jnp.float32,
    )
    inverse = lax.rsqrt(jnp.sum(projected * projected, axis=-1, keepdims=True) + norm_eps)
    student = projected * inverse
    student_b = student.astype(jnp.bfloat16)

    ids_grid = pair_ids.reshape(4, 2, 2, 2, 16, rows)
    ids_plane = lax.dynamic_index_in_dim(ids_grid, z, 4, keepdims=False)
    ids_core = lax.dynamic_index_in_dim(ids_plane, core, 2, keepdims=False)
    ids_yx = ids_core.transpose(0, 2, 1, 3).reshape(4, 4, rows)
    ids_xy = ids_core.transpose(1, 2, 0, 3).reshape(4, 4, rows)
    text_ids = jnp.where(core == 0, ids_yx, ids_xy)
    text_ids = jnp.concatenate([text_ids, text_ids[:3]], axis=0)
    text_ids = lax.dynamic_slice_in_dim(text_ids, jnp.where(core == 0, y, xh * 2 + xl), 4, 0)
    text_ids = text_ids.reshape(8, 2 * rows)
    ids_rows = pair_ids.reshape(512, rows)
    left_ids = jnp.stack(
        [
            lax.dynamic_index_in_dim(ids_rows, blk_index * 32 + group_index, 0, keepdims=False),
            lax.dynamic_index_in_dim(ids_rows, (blk_index ^ 1) * 32 + group_index, 0, keepdims=False),
        ]
    )

    def piece(values, start):
        group_rows = lax.dynamic_slice_in_dim(values, start, 36, 0)
        padded = jnp.pad(group_rows, ((0, 4), (0, 0)))
        return lax.dynamic_slice(padded, ((xh * 4 + y) * 5, core * 384), (5, 384))

    weight_rows = piece(head_weights, group_index * 36)
    near, weight_rows, *images = lax.optimization_barrier(
        (near, weight_rows, student_b, unit_teacher, far_teacher, left_ids, text_ids)
    )

    top = near[:2, :, :1152].reshape(2 * rows, 1152)
    bottom = near[2:, :, :1152].reshape(2 * rows, 1152)
    before_top = lax.ppermute(top, AXES, FORTH)
    after_bottom = lax.ppermute(bottom, AXES, BACK)
    before_bottom = lax.ppermute(bottom, AXES, FORTH)
    after_top = lax.ppermute(top, AXES, BACK)
    far_top = lax.ppermute(before_top, AXES, FORTH)
    far_bottom = lax.ppermute(after_bottom, AXES, BACK)
    sums = pair_sums(*images, [(top, 0), (bottom, 1)])
    near_chunks = [(before_top, 6), (after_bottom, 3), (before_bottom, 7), (after_top, 2)]
    sums = pair_sums(*images, near_chunks, sums)
    features = near[:, :, 1152:]
    features, sums = lax.optimization_barrier((features, sums))
    far_chunks = [(far_top, 4), (far_bottom, 5)]
    pulled, twin_pulled, losses, other_losses = pair_sums(*images, far_chunks, sums, last=True)

    pulled = pulled + from_twin(twin_pulled)
    student, inverse = student[:rows], inverse[:rows]
    grad_student = student_scale / rows * pulled
    grad_projected = (
        inverse * (grad_student - student * jnp.sum(student * grad_student, axis=-1, keepdims=True))
    ).astype(jnp.bfloat16)

    grad_rows = lax.dot_general(
        one_hot(row_order(core), 1152),
        grad_projected,
        (((1,), (1,)), ((), ())),
        preferred_element_type=jnp.float32,
    ).astype(jnp.bfloat16)
    grad_rows = exchange(grad_rows.reshape(4, 320, rows), FIRST)
    line_grad = lax.dot_general(
        grad_rows, features, (((0, 2), (0, 1)), ((), ())), preferred_element_type=jnp.float32
    )
    line_parts = exchange(line_grad.reshape(4, 80, 768), SECOND)
    kept, sent = column_sums(core, line_parts, other_losses)
    arrived = from_twin(sent)
    chip_grad = kept + arrived[:80]
    row_loss = (losses[0] + arrived[80, :rows]) / rows

    column_grad = jnp.pad(chip_grad.reshape(16, 15, 128), ((0, 0), (0, 1), (0, 0)))
    own_grad = jnp.sum(exchange(column_grad, COLUMN), axis=0)[:15].reshape(5, 384)

    def adam(head_grad, first, second, weights):
        new_first = beta_one * first + (1.0 - beta_one) * head_grad
        new_second = beta_two * second + (1.0 - beta_two) * head_grad * head_grad
        first_hat = new_first / (1.0 - beta_one**adam_step)
        second_hat = new_second / (1.0 - beta_two**adam_step)
        weights = weights.astype(jnp.float32)
        updated = weights - learn_rate * (
            first_hat / (jnp.sqrt(second_hat) + adam_eps) + weight_decay * weights
        )
        return updated.astype(jnp.bfloat16)

    own_weights = adam(
        own_grad,
        piece(moment_first, 0),
        piece(moment_second, 0),
        weight_rows,
    )
    packed = jnp.pad(own_weights.reshape(15, 128), ((0, 1), (0, 0)))
    chip_weights = share(packed, COLUMN)[:, :15].reshape(80, 384)
    high = rounded(own_grad)
    middle = rounded(own_grad - high)
    low = own_grad - high - middle
    spare = jnp.zeros((1, 384), jnp.float32)
    grad_parts = jnp.concatenate([high, middle, low, spare], axis=0).astype(jnp.bfloat16)
    plane = share(jnp.concatenate([chip_weights, grad_parts], axis=0), PLANE).reshape(2, 768, 384)
    half = selected(xl, plane)
    new_weights, new_first, new_second = last_outputs(
        core, half, from_twin(half), moment_first, moment_second
    )
    return (row_loss, new_first, new_second, new_weights)


def solution(mesh):
    placed = (
        P(("blk", "group"), None),
        P(("blk", "group"), None),
        P(("blk", "group"), None),
        P(),
        P(),
        P("group", None),
        P("group", None),
    )
    return jax.shard_map(
        per_device,
        mesh=mesh,
        in_specs=placed,
        out_specs=(P(("blk", "group")), P("group", None), P("group", None), P()),
        check_vma=False,
    )
```

```python
import functools

import jax
import jax.numpy as jnp
import numpy as np
from jax import lax
from jax.experimental import pallas as pl
from jax.experimental.pallas import tpu as pltpu
from jax.sharding import PartitionSpec as P


student_scale = 20.0
student_bias = -1.0
teacher_scale = 25.0
teacher_bias = -1.5
label_mix = 0.5
norm_eps = 1e-06
beta_one = 0.9
beta_two = 0.95
learn_rate = 0.01
weight_decay = 0.0001
adam_eps = 1e-08
adam_step = 100.0

AXES = ("blk", "group")


def device(X, y, core, z):
    return (y * 4 + X % 2 * 2 + core) * 32 + X // 2 * 16 + z


def x_line(y, core, z):
    return [device(X, y, core, z) for X in range(4)]


def y_line(X, core, z):
    return [device(X, y, core, z) for y in range(4)]


def lines(along_x):
    groups = []
    for core in range(2):
        line = x_line if (core == 0) == along_x else y_line
        groups += [line(i, core, z) for z in range(16) for i in range(4)]
    return groups


FIRST = lines(True)
SECOND = lines(False)
PLANE = [
    [device(X, y, core, z) for X in range(4) for y in range(4)]
    for core in range(2)
    for z in range(16)
]
COLUMN = [
    [device(X, y, core, z) for z in range(16)]
    for X in range(4)
    for y in range(4)
    for core in range(2)
]
TWIN = [(i, i ^ 32) for i in range(512)]


def hop(step):
    pairs = []
    for i in range(512):
        blk, group = divmod(i, 32)
        y, xh, core = blk // 4, blk // 2 % 2, blk % 2
        xl, z = divmod(group, 16)
        x = xh * 2 + xl
        if core == 0:
            y = (y + step) % 4
        else:
            x = (x + step) % 4
        pairs.append((i, device(x % 2 * 2 + x // 2, y, core, z)))
    return pairs


FORTH = hop(1)
BACK = hop(-1)


def exchange(pieces, groups):
    return lax.all_to_all(pieces, AXES, 0, 0, axis_index_groups=groups, tiled=True)


def share(block, groups):
    return exchange(jnp.broadcast_to(block[None], (len(groups[0]), *block.shape)), groups)


def from_twin(shard):
    return lax.ppermute(shard, AXES, TWIN)


def unit_rows(values):
    values = values.astype(jnp.float32)
    return values * lax.rsqrt(jnp.sum(values * values, axis=-1, keepdims=True) + norm_eps)


def head_kernel(texts_ref, features_ref, teacher_ref, out_ref, unit_ref, texts, teacher, packed, unit, sems):
    width = texts_ref.shape[1]
    take_texts = pltpu.make_async_copy(texts_ref, texts, sems.at[0])
    take_features = pltpu.make_async_copy(features_ref, packed.at[:, width:], sems.at[1])
    take_teacher = pltpu.make_async_copy(teacher_ref, teacher, sems.at[2])
    take_texts.start()
    take_features.start()
    take_teacher.start()
    take_texts.wait()
    packed[:, :width] = unit_rows(texts[...]).astype(jnp.bfloat16)
    take_features.wait()
    puts = [
        pltpu.make_async_copy(packed, out_ref.at[i], sems.at[3 + i])
        for i in range(out_ref.shape[0])
    ]
    for put in puts:
        put.start()
    take_teacher.wait()
    unit[...] = unit_rows(teacher[...]).astype(jnp.bfloat16)
    put_unit = pltpu.make_async_copy(unit, unit_ref, sems.at[3 + len(puts)])
    put_unit.start()
    for put in puts:
        put.wait()
    put_unit.wait()


def head(texts, features, teacher, count):
    rows, width = texts.shape[0], texts.shape[1] + features.shape[1]
    return pl.pallas_call(
        head_kernel,
        out_shape=(
            jax.ShapeDtypeStruct((count, rows, width), jnp.bfloat16),
            jax.ShapeDtypeStruct(teacher.shape, jnp.bfloat16),
        ),
        in_specs=[pl.BlockSpec(memory_space=pltpu.HBM)] * 3,
        out_specs=(pl.BlockSpec(memory_space=pltpu.HBM),) * 2,
        scratch_shapes=[
            pltpu.VMEM(texts.shape, jnp.bfloat16),
            pltpu.VMEM(teacher.shape, jnp.bfloat16),
            pltpu.VMEM((rows, width), jnp.bfloat16),
            pltpu.VMEM(teacher.shape, jnp.bfloat16),
            pltpu.SemaphoreType.DMA((4 + count,)),
        ],
        compiler_params=pltpu.CompilerParams(vmem_limit_bytes=60 << 20),
        cost_estimate=pl.CostEstimate(
            flops=8 * texts.size, bytes_accessed=2 * (count + 2) * rows * width, transcendentals=0
        ),
    )(texts, features, teacher)


def column_kernel(core_ref, parts_ref, others_ref, keep_ref, send_ref):
    def put(keep, send):
        keep_ref[...] = jnp.sum(parts_ref[:, :, keep], axis=0)
        send_ref[:80, :] = jnp.sum(parts_ref[:, :, send], axis=0)

    left, right = slice(0, 384), slice(384, 768)

    @pl.when(core_ref[0] == 0)
    def _():
        put(left, right)

    @pl.when(core_ref[0] != 0)
    def _():
        put(right, left)

    send_ref[80:, :] = others_ref[...]


def column_sums(core, parts, others):
    whole = pl.BlockSpec(memory_space=pltpu.VMEM)
    return pl.pallas_call(
        column_kernel,
        out_shape=(
            jax.ShapeDtypeStruct((80, 384), jnp.float32),
            jax.ShapeDtypeStruct((88, 384), jnp.float32),
        ),
        in_specs=[pl.BlockSpec(memory_space=pltpu.SMEM), whole, whole],
        out_specs=(whole, whole),
        compiler_params=pltpu.CompilerParams(vmem_limit_bytes=12 << 20),
        cost_estimate=pl.CostEstimate(flops=4 * 80 * 768, bytes_accessed=2 << 20, transcendentals=0),
    )(core.reshape(1), parts, others)


def select_kernel(xl_ref, rows_ref, plane_ref, out_ref):
    def picked(count, which, part):
        rows = lax.broadcasted_iota(jnp.int32, (count, rows_ref.shape[1]), 0)
        chosen = (rows == rows_ref[which : which + 1, :]).astype(jnp.bfloat16)
        return [
            jnp.dot(chosen, values, preferred_element_type=jnp.float32).astype(jnp.bfloat16)
            for values in part
        ]

    low, high = picked(576, 0, (plane_ref[0], plane_ref[1]))
    out_ref[:576, :] = low
    out_ref[576:1152, :] = high
    (out_ref[1152:, :],) = picked(144, 1, (plane_ref[xl_ref[0]],))


def selected(xl, plane):
    whole = pl.BlockSpec(memory_space=pltpu.VMEM)
    return pl.pallas_call(
        select_kernel,
        out_shape=jax.ShapeDtypeStruct((1296, 384), jnp.bfloat16),
        in_specs=[pl.BlockSpec(memory_space=pltpu.SMEM), whole, whole],
        out_specs=whole,
        compiler_params=pltpu.CompilerParams(vmem_limit_bytes=12 << 20),
        cost_estimate=pl.CostEstimate(
            flops=2 * 1296 * 768 * 384, bytes_accessed=2 << 20, transcendentals=0
        ),
    )(xl.reshape(1), jnp.asarray(place_rows()), plane)


def last_kernel(core_ref, half_ref, twin_ref, first_ref, second_ref, *outs):
    weights_ref, new_first_ref, new_second_ref = outs

    def put(left, right):
        weights_ref[:, :384] = left[:1152, :]
        weights_ref[:, 384:] = right[:1152, :]
        for side, ref in enumerate((left, right)):
            columns = slice(side * 384, side * 384 + 384)
            high, middle, low = (
                ref[1152 + i * 48 : 1200 + i * 48, :].astype(jnp.float32) for i in range(3)
            )
            grad = ((high + middle) + low)[:36]
            new_first_ref[:, columns] = beta_one * first_ref[:, columns] + (1.0 - beta_one) * grad
            new_second_ref[:, columns] = (
                beta_two * second_ref[:, columns] + (1.0 - beta_two) * grad * grad
            )

    @pl.when(core_ref[0] == 0)
    def _():
        put(half_ref, twin_ref)

    @pl.when(core_ref[0] != 0)
    def _():
        put(twin_ref, half_ref)


def last_outputs(core, half, twin_half, moment_first, moment_second):
    whole = pl.BlockSpec(memory_space=pltpu.VMEM)
    moment = jax.ShapeDtypeStruct(moment_first.shape, jnp.float32)
    return pl.pallas_call(
        last_kernel,
        out_shape=(jax.ShapeDtypeStruct((1152, 768), jnp.bfloat16), moment, moment),
        in_specs=[pl.BlockSpec(memory_space=pltpu.SMEM)] + [whole] * 4,
        out_specs=(whole,) * 3,
        compiler_params=pltpu.CompilerParams(vmem_limit_bytes=12 << 20),
        cost_estimate=pl.CostEstimate(flops=0, bytes_accessed=6 << 20, transcendentals=0),
    )(core.reshape(1), half, twin_half, moment_first, moment_second)


def pair_terms(student_rows, teacher_rows, left_ids, text_rows, right_ids):
    dims = (((1,), (1,)), ((), ()))
    student_logit = (
        student_scale
        * lax.dot_general(student_rows, text_rows, dims, preferred_element_type=jnp.float32)
        + student_bias
    )
    teacher_logit = (
        teacher_scale
        * lax.dot_general(teacher_rows, text_rows, dims, preferred_element_type=jnp.float32)
        + teacher_bias
    )
    labels = (left_ids == right_ids).astype(jnp.float32)
    target = (1.0 - label_mix) * labels + label_mix * jax.nn.sigmoid(teacher_logit)
    tail = jnp.exp(-jnp.abs(student_logit))
    softplus = jnp.maximum(student_logit, 0.0) + jnp.log1p(tail)
    chance = jnp.where(student_logit >= 0.0, 1.0, tail) / (1.0 + tail)
    losses = jnp.sum(softplus - target * student_logit, axis=1, keepdims=True)
    return losses, (chance - target).astype(jnp.bfloat16)


def pair_kernel(places, carried, last, *refs):
    student_ref, own_teacher_ref, twin_teacher_ref, left_ref, ids_ref = refs[:5]
    chunks, rest = refs[5 : 5 + len(places)], refs[5 + len(places) :]
    pulled_ref, losses_ref = rest[-2:]
    if last:
        own_ref, twin_ref, losses_ref, others_ref, pulled_ref = rest[-5:]
    if carried:
        pulled_ref[...] = rest[0][...]
        total = rest[1][...]
    else:
        pulled_ref[...] = jnp.zeros_like(pulled_ref)
        total = jnp.zeros(losses_ref.shape, jnp.float32)
    teacher = jnp.concatenate([own_teacher_ref[...], twin_teacher_ref[...]], axis=0)
    left_ids = jnp.concatenate(
        [jnp.transpose(jnp.broadcast_to(left_ref[i : i + 1, :], (128, 128))) for i in range(2)], axis=0
    )[:, :1]
    for place, chunk_ref in zip(places, chunks):
        texts = chunk_ref[...]
        losses, coeff = pair_terms(
            student_ref[...], teacher, left_ids, texts, ids_ref[place : place + 1, :]
        )
        total += losses
        pulled_ref[...] += jnp.dot(coeff, texts, preferred_element_type=jnp.float32)
    if not last:
        losses_ref[...] = total
        return
    own_ref[...] = pulled_ref[:128]
    twin_ref[...] = pulled_ref[128:]
    lanes = [
        jnp.transpose(jnp.broadcast_to(total[i * 128 : i * 128 + 128], (128, 128)))[:1]
        for i in range(2)
    ]
    losses_ref[...] = lanes[0]
    others_ref[...] = jnp.zeros_like(others_ref)
    others_ref[:1, :128] = lanes[1]


def pair_sums(student_rows, own_teacher, twin_teacher, left_ids, text_ids, chunks, carried=(), last=False):
    rows, width = student_rows.shape
    texts, places = zip(*chunks)
    count = sum(chunk.shape[0] for chunk in texts)
    operands = (student_rows, own_teacher, twin_teacher, left_ids, text_ids, *texts, *carried)
    whole = pl.BlockSpec(memory_space=pltpu.VMEM)
    parts = 1 + last
    shapes = [(rows // parts, width)] * parts + ([(1, 128), (8, 384)] if last else [(rows, 1)])
    return pl.pallas_call(
        functools.partial(pair_kernel, places, bool(carried), last),
        out_shape=[jax.ShapeDtypeStruct(shape, jnp.float32) for shape in shapes],
        in_specs=[whole] * len(operands),
        out_specs=[whole] * len(shapes),
        scratch_shapes=[pltpu.VMEM((rows, width), jnp.float32)] * last,
        compiler_params=pltpu.CompilerParams(vmem_limit_bytes=20 << 20),
        cost_estimate=pl.CostEstimate(
            flops=6 * rows * count * width,
            bytes_accessed=2 * count * width,
            transcendentals=4 * rows * count,
        ),
    )(*operands)


def row_order(core):
    place = lax.iota(jnp.int32, 1280)
    first, second = place // 320, place // 80 % 4
    X = jnp.where(core == 0, first, second)
    y = jnp.where(core == 0, second, first)
    row = (X % 2 * 4 + y) * 5 + place % 5
    return jnp.where(row < 36, X // 2 * 576 + place // 5 % 16 * 36 + row, -1)


def place_rows():
    chip, row = np.arange(768) // 96, np.arange(768) % 96
    q = chip * 5 + row % 5
    weights = np.where((row < 80) & (q < 36), row // 5 * 36 + q, -1)
    grads = np.where((row >= 80) & (row < 95), (row - 80) // 5 * 48 + q, -1)
    return np.stack([weights, grads]).astype(np.int32)


def one_hot(index, width):
    return (index[:, None] == lax.iota(jnp.int32, width)[None, :]).astype(jnp.bfloat16)


def rounded(values):
    return lax.reduce_precision(values, 8, 7)


def per_device(
    student_features,
    teacher_image,
    text_embeds,
    pair_ids,
    head_weights,
    moment_first,
    moment_second,
):
    rows = student_features.shape[0]
    blk_index = lax.axis_index("blk")
    group_index = lax.axis_index("group")
    y, xh, core = blk_index // 4, blk_index // 2 % 2, blk_index % 2
    xl, z = group_index // 16, group_index % 16

    copies, unit_teacher = head(text_embeds, student_features, teacher_image, 4)
    copies, twin_features = lax.optimization_barrier((copies, student_features))
    near = exchange(copies, FIRST)

    far_features, far_teacher = from_twin(twin_features), from_twin(unit_teacher)
    both_features = jnp.concatenate([student_features, far_features], axis=0)
    projected = lax.dot_general(
        both_features,
        head_weights,
        (((1,), (1,)), ((), ())),
        preferred_element_type=jnp.float32,
    )
    inverse = lax.rsqrt(jnp.sum(projected * projected, axis=-1, keepdims=True) + norm_eps)
    student = projected * inverse
    student_b = student.astype(jnp.bfloat16)

    ids_grid = pair_ids.reshape(4, 2, 2, 2, 16, rows)
    ids_plane = lax.dynamic_index_in_dim(ids_grid, z, 4, keepdims=False)
    ids_core = lax.dynamic_index_in_dim(ids_plane, core, 2, keepdims=False)
    ids_yx = ids_core.transpose(0, 2, 1, 3).reshape(4, 4, rows)
    ids_xy = ids_core.transpose(1, 2, 0, 3).reshape(4, 4, rows)
    text_ids = jnp.where(core == 0, ids_yx, ids_xy)
    text_ids = jnp.concatenate([text_ids, text_ids[:3]], axis=0)
    text_ids = lax.dynamic_slice_in_dim(text_ids, jnp.where(core == 0, y, xh * 2 + xl), 4, 0)
    text_ids = text_ids.reshape(8, 2 * rows)
    ids_rows = pair_ids.reshape(512, rows)
    left_ids = jnp.stack(
        [
            lax.dynamic_index_in_dim(ids_rows, blk_index * 32 + group_index, 0, keepdims=False),
            lax.dynamic_index_in_dim(ids_rows, (blk_index ^ 1) * 32 + group_index, 0, keepdims=False),
        ]
    )

    def piece(values, start):
        group_rows = lax.dynamic_slice_in_dim(values, start, 36, 0)
        padded = jnp.pad(group_rows, ((0, 4), (0, 0)))
        return lax.dynamic_slice(padded, ((xh * 4 + y) * 5, core * 384), (5, 384))

    weight_rows = piece(head_weights, group_index * 36)
    near, weight_rows, *images = lax.optimization_barrier(
        (near, weight_rows, student_b, unit_teacher, far_teacher, left_ids, text_ids)
    )

    top = near[:2, :, :1152].reshape(2 * rows, 1152)
    bottom = near[2:, :, :1152].reshape(2 * rows, 1152)
    before_top = lax.ppermute(top, AXES, FORTH)
    after_bottom = lax.ppermute(bottom, AXES, BACK)
    after_top = lax.ppermute(top, AXES, BACK)
    before_bottom = lax.ppermute(bottom, AXES, FORTH)
    far_top = lax.ppermute(before_top, AXES, FORTH)
    far_bottom = lax.ppermute(after_bottom, AXES, BACK)
    sums = pair_sums(*images, [(top, 0), (bottom, 1)])
    near_chunks = [(before_top, 6), (after_bottom, 3), (before_bottom, 7), (after_top, 2)]
    sums = pair_sums(*images, near_chunks, sums)
    features = near[:, :, 1152:]
    features, sums = lax.optimization_barrier((features, sums))
    far_chunks = [(far_top, 4), (far_bottom, 5)]
    pulled, twin_pulled, losses, other_losses = pair_sums(*images, far_chunks, sums, last=True)

    pulled = pulled + from_twin(twin_pulled)
    student, inverse = student[:rows], inverse[:rows]
    grad_student = student_scale / rows * pulled
    grad_projected = (
        inverse * (grad_student - student * jnp.sum(student * grad_student, axis=-1, keepdims=True))
    ).astype(jnp.bfloat16)

    grad_rows = lax.dot_general(
        one_hot(row_order(core), 1152),
        grad_projected,
        (((1,), (1,)), ((), ())),
        preferred_element_type=jnp.float32,
    ).astype(jnp.bfloat16)
    grad_rows = exchange(grad_rows.reshape(4, 320, rows), FIRST)
    line_grad = lax.dot_general(
        grad_rows, features, (((0, 2), (0, 1)), ((), ())), preferred_element_type=jnp.float32
    )
    line_parts = exchange(line_grad.reshape(4, 80, 768), SECOND)
    kept, sent = column_sums(core, line_parts, other_losses)
    arrived = from_twin(sent)
    chip_grad = kept + arrived[:80]
    row_loss = (losses[0] + arrived[80, :rows]) / rows

    column_grad = jnp.pad(chip_grad.reshape(16, 15, 128), ((0, 0), (0, 1), (0, 0)))
    own_grad = jnp.sum(exchange(column_grad, COLUMN), axis=0)[:15].reshape(5, 384)

    def adam(head_grad, first, second, weights):
        new_first = beta_one * first + (1.0 - beta_one) * head_grad
        new_second = beta_two * second + (1.0 - beta_two) * head_grad * head_grad
        first_hat = new_first / (1.0 - beta_one**adam_step)
        second_hat = new_second / (1.0 - beta_two**adam_step)
        weights = weights.astype(jnp.float32)
        updated = weights - learn_rate * (
            first_hat / (jnp.sqrt(second_hat) + adam_eps) + weight_decay * weights
        )
        return updated.astype(jnp.bfloat16)

    own_weights = adam(
        own_grad,
        piece(moment_first, 0),
        piece(moment_second, 0),
        weight_rows,
    )
    packed = jnp.pad(own_weights.reshape(15, 128), ((0, 1), (0, 0)))
    chip_weights = share(packed, COLUMN)[:, :15].reshape(80, 384)
    high = rounded(own_grad)
    middle = rounded(own_grad - high)
    low = own_grad - high - middle
    spare = jnp.zeros((1, 384), jnp.float32)
    grad_parts = jnp.concatenate([high, middle, low, spare], axis=0).astype(jnp.bfloat16)
    plane = share(jnp.concatenate([chip_weights, grad_parts], axis=0), PLANE).reshape(2, 768, 384)
    half = selected(xl, plane)
    new_weights, new_first, new_second = last_outputs(
        core, half, from_twin(half), moment_first, moment_second
    )
    return (row_loss, new_first, new_second, new_weights)


def solution(mesh):
    placed = (
        P(("blk", "group"), None),
        P(("blk", "group"), None),
        P(("blk", "group"), None),
        P(),
        P(),
        P("group", None),
        P("group", None),
    )
    return jax.shard_map(
        per_device,
        mesh=mesh,
        in_specs=placed,
        out_specs=(P(("blk", "group")), P("group", None), P("group", None), P()),
        check_vma=False,
    )
```
